32 devices in a mesh: groups: 2 (over y), blk: 8 (over z, x), head: 2 (over core).
Axes of the slice: x: 2, y: 2, z: 4, core: 2. Of those that a mesh axis runs over, the one named last changes fastest.
Arguments:
- tokens: float32 [3072, 1024], P(('groups', 'blk'), 'head'), parts along dimension 0, may hold values from -20 to 20
- norm_gain: float32 [1024], replicated, may hold values from 0.1 to 1.9
- qkv_weight: bfloat16 [3, 1024, 1024], P(None, None, 'head'), may hold values from -20 to 20
- out_weight: bfloat16 [1024, 1024], P('head'), may hold values from -0.1875 to 0.1875
- lateral_weight: bfloat16 [2, 1024, 256], replicated, may hold values from -0.1875 to 0.1875
- conv_weight: bfloat16 [2, 3, 3, 256, 256], replicated, may hold values from -0.125 to 0.125
- level_gains: float32 [2, 2, 256], replicated, may hold values from 0.1 to 1.9
Outputs:
- fine_map: bfloat16 [32, 96, 256], P(('groups', 'blk'), 'head'), parts along dimension 0
- coarse_map: bfloat16 [16, 48, 256], P(('groups', 'blk'), 'head'), parts along dimension 0
The draws below stay inside these ranges and needn't reach their ends.
There are 2 independent parts, one for each index of `groups`. The reference program is written for one: setup_inputs(seed, part) draws one part's arguments, and reference() takes and returns one part's arrays. A program takes and returns all parts, laid end to end along the dimension named above; an argument that names none is the same for every part. Nothing has to cross between parts.
All inputs are finite; a program needn't handle non-finite values.
Results may differ from the reference program's by a relative error of at most 0.014.
The reference program's roundings to bfloat16 on the way count: a program that leaves them out, or rounds other values in their place, can miss the bound.
Values may be sent and summed in bfloat16 or wider, within the bound.
No kernel may reach another device: no remote copies, remote signals or barrier semaphores. Data moves between devices by JAX's collectives and lax.ppermute only.
A program may use at most 128 MiB of HBM per device.

```python
import math
import jax
import jax.numpy as jnp
from jax import lax

D = 1024
HEADS = 16
HEAD_DIM = 64
CHANNELS = 256
GW = 96
GH = 16
TOKENS = 1536


def draw_tokens(key, part):
    normal_base = jnp.clip(jax.random.normal(jax.random.fold_in(key, 11), (TOKENS, D), jnp.float32), -6.0, 6.0)
    return 0.4 * normal_base


def draw_qkv_weight(key, part):
    normal_base = jnp.clip(jax.random.normal(jax.random.fold_in(key, 21), (3, D, D), jnp.float32), -6.0, 6.0)
    std_match = 1.58 / math.sqrt(D)
    std_value = 2.0 / math.sqrt(D)
    scales = jnp.array([std_match, std_match, std_value], jnp.float32)[:, None, None]
    weights = normal_base * scales
    return weights.astype(jnp.bfloat16)


def block_scale(stream_key, shape, pieces, smallest, high):
    loudness, own = 1.0, jax.random.fold_in(stream_key, 6)
    for position, shards_of in pieces:
        heights = jnp.exp(jax.random.uniform(jax.random.fold_in(own, position), (shards_of,), jnp.float32, smallest / len(pieces), high / len(pieces)))
        loudness = loudness * jnp.repeat(heights, shape[position] // shards_of).reshape([-1 if axis == position else 1 for axis in range(len(shape))])
    return loudness


def noise(rng, dims, deviation, limit, pieces=(), kind=jnp.bfloat16):
    gain = block_scale(rng, dims, pieces, -0.22, 0.18) if pieces else 1.0
    drawn = jax.random.normal(rng, dims, jnp.float32) * deviation * gain
    return jnp.minimum(jnp.maximum(drawn, -limit), limit).astype(kind)


def setup_inputs(seed: int = 0, part: int = 0) -> dict:
    splits = jax.random.split(jax.random.key(seed), 8)
    part_splits = jax.random.split(jax.random.fold_in(splits[7], part), 8)
    return {
        "tokens": draw_tokens(jax.random.fold_in(jax.random.fold_in(splits[7], part), 71), part),
        "norm_gain": jnp.clip(1.0 + 0.18 * jax.random.normal(splits[1], (D,), jnp.float32), 0.1, 1.9),
        "qkv_weight": draw_qkv_weight(jax.random.fold_in(splits[7], 71), part),
        "out_weight": noise(splits[3], (D, D), D ** -0.5, 0.1875, ((0, 2),)),
        "lateral_weight": noise(splits[4], (2, D, CHANNELS), D ** -0.5, 0.1875),
        "conv_weight": noise(splits[5], (2, 3, 3, CHANNELS, CHANNELS), (9 * CHANNELS) ** -0.5, 0.125),
        "level_gains": jnp.clip(1.0 + 0.18 * jax.random.normal(splits[6], (2, 2, CHANNELS), jnp.float32), 0.1, 1.9),
    }


def layer_norm(values_in, gain_row):
    mean_row = lax.optimization_barrier(jnp.mean(values_in, axis=-1, keepdims=True))
    centred = values_in - mean_row
    spread = lax.optimization_barrier(jnp.mean(centred * centred, axis=-1, keepdims=True))
    return centred * lax.rsqrt(spread + 1e-06) * gain_row

def attention(queries, key_rows, value_rows):
    token_count = queries.shape[0]
    query_rows = math.gcd(token_count, 2048)
    block_count = token_count // query_rows
    score_scale = HEAD_DIM ** (-0.5)

    def single_head(head_index):
        query_head = lax.dynamic_slice_in_dim(queries, head_index * HEAD_DIM, HEAD_DIM, 1)
        key_head = lax.dynamic_slice_in_dim(key_rows, head_index * HEAD_DIM, HEAD_DIM, 1)
        value_head = lax.dynamic_slice_in_dim(value_rows, head_index * HEAD_DIM, HEAD_DIM, 1)

        def single_block(block_index):
            query_block = lax.dynamic_slice_in_dim(query_head, block_index * query_rows, query_rows, 0)
            scores = jnp.dot(query_block, key_head.T, preferred_element_type=jnp.float32) * score_scale
            weights = jnp.exp(scores - lax.optimization_barrier(jnp.max(scores, axis=-1, keepdims=True)))
            totals = lax.optimization_barrier(jnp.sum(weights, axis=-1, keepdims=True))
            mixed = jnp.dot(weights.astype(jnp.bfloat16), value_head, preferred_element_type=jnp.float32)
            return (mixed / totals).astype(jnp.bfloat16)
        blocks = lax.map(single_block, jnp.arange(block_count, dtype=jnp.int32))
        return blocks.reshape(token_count, HEAD_DIM)
    per_head = lax.map(single_head, jnp.arange(HEADS, dtype=jnp.int32))
    return jnp.transpose(per_head, (1, 0, 2)).reshape(token_count, HEADS * HEAD_DIM)

def pyramid_level(grid_in, lateral, kernel, gains):
    mixed = jnp.einsum('rcd,de->rce', grid_in.astype(jnp.float32), lateral.astype(jnp.float32))
    lateral_out = layer_norm(mixed, gains[0]).astype(jnp.bfloat16)
    row_count = grid_in.shape[0]
    col_count = grid_in.shape[1]
    padded = jnp.pad(lateral_out, ((1, 1), (1, 1), (0, 0)))
    total_out = jnp.zeros((row_count, col_count, kernel.shape[-1]), jnp.float32)
    for tap_row in range(3):
        for tap_col in range(3):
            window = padded[tap_row:tap_row + row_count, tap_col:tap_col + col_count]
            total_out = total_out + jnp.einsum('rcd,de->rce', window.astype(jnp.float32), kernel[tap_row, tap_col].astype(jnp.float32))
    return layer_norm(total_out, gains[1]).astype(jnp.bfloat16)

def reference(tokens, norm_gain, qkv_weight, out_weight, lateral_weight, conv_weight, level_gains):
    normed = layer_norm(tokens, norm_gain).astype(jnp.bfloat16)
    queries = jnp.dot(normed, qkv_weight[0], preferred_element_type=jnp.float32).astype(jnp.bfloat16)
    key_rows = jnp.dot(normed, qkv_weight[1], preferred_element_type=jnp.float32).astype(jnp.bfloat16)
    value_rows = jnp.dot(normed, qkv_weight[2], preferred_element_type=jnp.float32).astype(jnp.bfloat16)
    attended = attention(queries, key_rows, value_rows)
    block_out = (tokens + jnp.dot(attended, out_weight, preferred_element_type=jnp.float32)).astype(jnp.bfloat16)
    grid = block_out.reshape(GH, GW, D)
    pooled = lax.optimization_barrier(jnp.max(grid.reshape(GH // 2, 2, GW // 2, 2, D), axis=(1, 3)))
    fine_map = pyramid_level(grid, lateral_weight[0], conv_weight[0], level_gains[0])
    coarse_map = pyramid_level(pooled, lateral_weight[1], conv_weight[1], level_gains[1])
    return (fine_map, coarse_map)
```

```python
import functools
import math

import jax
import jax.numpy as jnp
from jax import lax
from jax.experimental import pallas as pl
from jax.experimental.pallas import tpu as pltpu
from jax.sharding import PartitionSpec as P

HEAD_DIM = 64
LANES = 128
GRID_COLS = 96
EPS = 1e-06
BF16 = jnp.bfloat16
F32 = jnp.float32
VMEM_LIMIT = 48 * 1024 * 1024


def vmem_specs(count):
    return [pl.BlockSpec(memory_space=pltpu.VMEM)] * count


def kernel_params():
    return pltpu.CompilerParams(vmem_limit_bytes=VMEM_LIMIT)


def nbytes(*arrays):
    return sum(math.prod(a.shape) * jnp.dtype(a.dtype).itemsize for a in arrays)


def call(kernel, outs, args, scratch=(), flops=0, exps=0):
    outs = tuple(jax.ShapeDtypeStruct(shape, dtype) for shape, dtype in outs)
    return pl.pallas_call(
        kernel,
        out_shape=outs,
        in_specs=vmem_specs(len(args)),
        out_specs=tuple(vmem_specs(len(outs))),
        scratch_shapes=list(scratch),
        compiler_params=kernel_params(),
        cost_estimate=pl.CostEstimate(
            flops=flops, transcendentals=exps, bytes_accessed=nbytes(*args, *outs)
        ),
    )(*args)


def layer_norm(values_in, gain_row):
    mean_row = jnp.mean(values_in, axis=-1, keepdims=True)
    centred = values_in - mean_row
    spread = jnp.mean(centred * centred, axis=-1, keepdims=True)
    return centred * lax.rsqrt(spread + EPS) * gain_row


def dot(a, b):
    return jnp.dot(a, b, preferred_element_type=F32)


def low_lanes(shape):
    return lax.broadcasted_iota(jnp.int32, shape, len(shape) - 1) % LANES < HEAD_DIM


def half_turn(tile):
    return pltpu.roll(tile, HEAD_DIM, axis=1)


def project(mine_ref, other_ref, gain_ref, weight_ref):
    core = lax.axis_index("head")
    half = mine_ref.shape[1]
    width = 2 * half
    mine, other = mine_ref[...], other_ref[...]
    mean = (
        jnp.sum(mine, axis=-1, keepdims=True) + jnp.sum(other, axis=-1, keepdims=True)
    ) / width
    mine, other = mine - mean, other - mean
    spread = (
        jnp.sum(mine * mine, axis=-1, keepdims=True)
        + jnp.sum(other * other, axis=-1, keepdims=True)
    ) / width
    scale = lax.rsqrt(spread + EPS)
    mine = (mine * scale * gain_ref[pl.ds(core, 1), :]).astype(BF16)
    other = (other * scale * gain_ref[pl.ds(1 - core, 1), :]).astype(BF16)
    mine_at = pl.ds(pl.multiple_of(core * half, half), half)
    other_at = pl.ds(pl.multiple_of((1 - core) * half, half), half)
    return [
        dot(mine, weight_ref[part, mine_at, :]) + dot(other, weight_ref[part, other_at, :])
        for part in range(3)
    ]


def qkv_kernel(mine_ref, other_ref, gain_ref, weight_ref, send_ref):
    queries, keys, values = project(mine_ref, other_ref, gain_ref, weight_ref)
    rows = queries.shape[0]
    low = low_lanes((rows, LANES))
    low_q = low_lanes((rows // 2, LANES))
    for pair in range(queries.shape[1] // LANES):
        cols = slice(pair * LANES, (pair + 1) * LANES)
        key, value = keys[:, cols], values[:, cols]
        top, bottom = queries[: rows // 2, cols], queries[rows // 2 :, cols]
        send_ref[2 * pair, :rows] = jnp.where(low, key, half_turn(value)).astype(BF16)
        send_ref[2 * pair + 1, :rows] = jnp.where(low, half_turn(key), value).astype(BF16)
        send_ref[2 * pair, rows:] = jnp.where(low_q, top, half_turn(bottom)).astype(BF16)
        send_ref[2 * pair + 1, rows:] = jnp.where(low_q, half_turn(top), bottom).astype(BF16)


def plain_qkv_kernel(mine_ref, other_ref, gain_ref, weight_ref, q_ref, k_ref, v_ref):
    for ref, value in zip(
        (q_ref, k_ref, v_ref), project(mine_ref, other_ref, gain_ref, weight_ref)
    ):
        ref[...] = value.astype(BF16)


def attend_kernel(got_ref, out_ref, pair_ref):
    blocks, packed_rows = got_ref.shape[0], out_ref.shape[1]
    rows = 2 * packed_rows
    for block in range(blocks):
        pair_ref[block * rows : (block + 1) * rows] = got_ref[block, :rows]
    factor = HEAD_DIM ** (-0.5) * math.log2(math.e)
    low = low_lanes((packed_rows, LANES))
    for block in range(blocks):
        packed = got_ref[block, rows:].astype(F32)
        queries = jnp.concatenate(
            [jnp.where(low, packed, 0.0), jnp.where(low, half_turn(packed), 0.0)], axis=0
        ).astype(BF16)
        scores = lax.dot_general(
            queries, pair_ref[...], (((1,), (1,)), ((), ())), preferred_element_type=F32
        )
        top = jnp.max(scores, axis=-1, keepdims=True)
        weights = jnp.exp2((scores - top) * factor)
        total = jnp.sum(weights, axis=-1, keepdims=True)
        mixed = dot(weights.astype(BF16), pair_ref[...]) / total
        out_ref[block] = jnp.where(
            low, half_turn(mixed[:packed_rows]), mixed[packed_rows:]
        ).astype(BF16)


def out_terms(attended, weight_ref, mine_ref, other_ref, send_ref, keep_ref, full_ref):
    core = lax.axis_index("head")
    window = send_ref.shape[1]
    half = mine_ref.shape[1]
    shift = GRID_COLS - window
    full_ref[...] = dot(attended, weight_ref[...])
    for row in range(send_ref.shape[0]):
        there = pl.ds(pl.multiple_of(row * GRID_COLS + (1 - core) * shift, 8), window)
        send_ref[row] = full_ref[there, :].astype(BF16)
        here = pl.ds(pl.multiple_of(row * GRID_COLS + core * shift, 8), window)
        for part, ref in ((core, mine_ref), (1 - core, other_ref)):
            cols = pl.ds(pl.multiple_of(part * half, half), half)
            keep_ref[row, :, cols] = full_ref[here, cols] + ref[here, :]


def out_kernel(back_ref, weight_ref, mine_ref, other_ref, send_ref, keep_ref, full_ref, att_ref):
    packed_rows = back_ref.shape[1]
    low = low_lanes((packed_rows, LANES))
    for pair in range(back_ref.shape[0] // 2):
        cols = slice(pair * LANES, (pair + 1) * LANES)
        left = back_ref[2 * pair].astype(F32)
        right = back_ref[2 * pair + 1].astype(F32)
        att_ref[:packed_rows, cols] = jnp.where(low, left, half_turn(right)).astype(BF16)
        att_ref[packed_rows:, cols] = jnp.where(low, half_turn(left), right).astype(BF16)
    out_terms(att_ref[...], weight_ref, mine_ref, other_ref, send_ref, keep_ref, full_ref)


def plain_out_kernel(att_ref, weight_ref, mine_ref, other_ref, send_ref, keep_ref, full_ref):
    out_terms(att_ref[...], weight_ref, mine_ref, other_ref, send_ref, keep_ref, full_ref)


def lateral_kernel(keep_ref, got_ref, lateral_ref, gain_ref, up_ref, down_ref, pool_ref):
    window, features = keep_ref.shape[1], keep_ref.shape[2]
    cells = (keep_ref[...] + got_ref[...].astype(F32)).astype(BF16)
    fine = layer_norm(
        dot(cells.reshape(2 * window, features), lateral_ref[0]), gain_ref[0, 0][None, :]
    ).astype(BF16)
    up_ref[:window] = fine[:window]
    down_ref[:window] = fine[window:]
    tall = jnp.maximum(cells[0].astype(F32), cells[1].astype(F32))
    pooled = []
    for part in range(features // LANES):
        pool_ref[part] = tall[:, part * LANES : (part + 1) * LANES]
        even = pool_ref[part, pl.ds(0, window // 2, stride=2), :]
        odd = pool_ref[part, pl.ds(1, window // 2, stride=2), :]
        pooled.append(jnp.maximum(even, odd).astype(BF16))
    pooled = jnp.concatenate(pooled, axis=1)
    coarse = layer_norm(dot(pooled, lateral_ref[1]), gain_ref[1, 0][None, :]).astype(BF16)
    up_ref[window:] = coarse
    down_ref[window:] = coarse


def conv_level(stacked_ref, weight_ref, level, rows, window, sum_ref):
    block = rows * window
    place = lax.broadcasted_iota(jnp.int32, (block, weight_ref.shape[-1]), 0) % window
    taps = []
    for tap_col in range(3):
        total = None
        for tap_row in range(3):
            term = dot(
                stacked_ref[tap_row * window : tap_row * window + block],
                weight_ref[level, tap_row, tap_col],
            )
            total = term if total is None else total + term
        taps.append(total)
    left = jnp.where(place == 0, 0.0, pltpu.roll(taps[0], 1, axis=0))
    right = jnp.where(place == window - 1, 0.0, pltpu.roll(taps[2], block - 1, axis=0))
    sum_ref[...] = left + taps[1] + right


def conv_kernel(
    up_ref,
    down_ref,
    above_ref,
    below_ref,
    weight_ref,
    gain_ref,
    fine_ref,
    coarse_ref,
    fine_in,
    coarse_in,
    fine_sum,
    coarse_sum,
):
    core = lax.axis_index("head")
    window = fine_sum.shape[0] // 2
    half = window // 2
    has_above = lax.axis_index("blk") > 0
    has_below = lax.axis_index("blk") < lax.axis_size("blk") - 1
    fine_in[window : 2 * window] = up_ref[:window]
    fine_in[2 * window : 3 * window] = down_ref[:window]
    coarse_in[half : 2 * half] = up_ref[window:]
    above = jnp.where(has_above, above_ref[...].astype(F32), 0.0).astype(BF16)
    below = jnp.where(has_below, below_ref[...].astype(F32), 0.0).astype(BF16)
    fine_in[:window] = above[:window]
    fine_in[3 * window :] = below[:window]
    coarse_in[:half] = above[window:]
    coarse_in[2 * half :] = below[window:]
    conv_level(fine_in, weight_ref, 0, 2, window, fine_sum)
    conv_level(coarse_in, weight_ref, 1, 1, half, coarse_sum)
    cols = fine_ref.shape[1]
    shift = GRID_COLS - window
    inset = cols - shift
    for row in range(2):
        here = pl.ds(pl.multiple_of(row * window + core * inset, 8), cols)
        fine_ref[row] = layer_norm(fine_sum[here, :], gain_ref[0, 1][None, :]).astype(BF16)
    here = pl.ds(pl.multiple_of(core * (inset // 2), 8), cols // 2)
    coarse_ref[0] = layer_norm(coarse_sum[here, :], gain_ref[1, 1][None, :]).astype(BF16)


def attend_shared(queries, keys, values):
    factor = HEAD_DIM ** (-0.5)
    step = math.gcd(keys.shape[0], 1536)
    rows = queries.shape[0]

    def block(state, pair):
        running, totals, weighted = state
        key, value = pair
        scores = (
            lax.dot_general(queries, key, (((1,), (1,)), ((), ())), preferred_element_type=F32)
            * factor
        )
        newmax = jnp.maximum(running, jnp.max(scores, axis=-1, keepdims=True))
        weights = jnp.exp(scores - newmax)
        shrink = jnp.exp(running - newmax)
        totals = totals * shrink + jnp.sum(weights, axis=-1, keepdims=True)
        weighted = weighted * shrink + dot(weights.astype(BF16), value)
        return (newmax, totals, weighted), None

    state = (
        jnp.full((rows, 1), -jnp.inf, F32),
        jnp.zeros((rows, 1), F32),
        jnp.zeros((rows, HEAD_DIM), F32),
    )
    state, _ = lax.scan(
        block, state, (keys.reshape(-1, step, HEAD_DIM), values.reshape(-1, step, HEAD_DIM))
    )
    return (state[2] / state[1]).astype(BF16)


def exchange(value):
    return lax.all_to_all(value, "blk", split_axis=0, concat_axis=0, tiled=True)


def attention_shared(mine, other, gain_halves, qkv_weight, slices):
    rows = mine.shape[0]
    width = qkv_weight.shape[2]
    heads = width // HEAD_DIM
    blocks = heads * slices
    share = rows // slices
    queries, keys, values = call(
        plain_qkv_kernel, [((rows, width), BF16)] * 3, (mine, other, gain_halves, qkv_weight)
    )
    query_send = jnp.transpose(
        queries.reshape(slices, share, heads, HEAD_DIM), (2, 0, 1, 3)
    ).reshape(blocks, share * HEAD_DIM)
    pair = jnp.concatenate(
        (keys.reshape(rows, heads, HEAD_DIM), values.reshape(rows, heads, HEAD_DIM)), axis=2
    )
    pair = jnp.transpose(pair, (1, 0, 2))
    pair_send = jnp.broadcast_to(pair[:, None], (heads, slices, rows, 2 * HEAD_DIM)).reshape(
        blocks, rows, 2 * HEAD_DIM
    )
    query_got = exchange(query_send).reshape(blocks * share, HEAD_DIM)
    pair_got = exchange(pair_send).reshape(blocks * rows, 2 * HEAD_DIM)
    one_head = attend_shared(query_got, pair_got[:, :HEAD_DIM], pair_got[:, HEAD_DIM:])
    back = exchange(one_head.reshape(blocks, share * HEAD_DIM))
    return jnp.transpose(back.reshape(heads, slices, share, HEAD_DIM), (1, 2, 0, 3)).reshape(
        rows, width
    )


def body(tokens, norm_gain, qkv_weight, out_weight, lateral_weight, conv_weight, level_gains):
    rows, half = tokens.shape
    features = out_weight.shape[1]
    width = qkv_weight.shape[2]
    heads = width // HEAD_DIM
    blocks = lax.axis_size("blk")
    cores = lax.axis_size("head")
    grid_rows = rows // GRID_COLS
    cols = GRID_COLS // cores
    channels = lateral_weight.shape[2]
    window = 2 * GRID_COLS // 3
    swap = [(i, cores - 1 - i) for i in range(cores)]

    other = lax.ppermute(tokens, "head", swap)
    gain_halves = norm_gain.reshape(cores, half)
    tail = (out_weight, tokens, other)
    tail_outs = [
        ((grid_rows, window, features), BF16),
        ((grid_rows, window, features), F32),
    ]
    full = pltpu.VMEM((rows, features), F32)
    out_flops = 2 * rows * width * features
    if heads == blocks:
        (send,) = call(
            qkv_kernel,
            [((blocks, rows + rows // 2, LANES), BF16)],
            (tokens, other, gain_halves, qkv_weight),
            flops=6 * rows * features * width,
        )
        got = exchange(send)
        total = blocks * rows
        (one_head,) = call(
            attend_kernel,
            [((blocks, rows // 2, LANES), BF16)],
            (got,),
            [pltpu.VMEM((total, LANES), BF16)],
            flops=4 * total * total * LANES,
            exps=total * total,
        )
        back = exchange(one_head)
        peer_term, keep = call(
            out_kernel,
            tail_outs,
            (back,) + tail,
            [full, pltpu.VMEM((rows, width), BF16)],
            flops=out_flops,
        )
    else:
        attended = attention_shared(tokens, other, gain_halves, qkv_weight, blocks // heads)
        peer_term, keep = call(plain_out_kernel, tail_outs, (attended,) + tail, [full], out_flops)
    peer_term = lax.ppermute(peer_term, "head", swap)

    message = (window + window // 2, channels)
    up, down = call(
        lateral_kernel,
        [(message, BF16), (message, BF16)],
        (keep, peer_term, lateral_weight, level_gains),
        [pltpu.VMEM((features // LANES, window, LANES), F32)],
        flops=5 * window * features * channels,
    )
    above = lax.ppermute(down, "blk", [(i, (i + 1) % blocks) for i in range(blocks)])
    below = lax.ppermute(up, "blk", [((i + 1) % blocks, i) for i in range(blocks)])
    return call(
        conv_kernel,
        [((grid_rows, cols, channels), BF16), ((grid_rows // 2, cols // 2, channels), BF16)],
        (up, down, above, below, conv_weight, level_gains),
        [
            pltpu.VMEM((4 * window, channels), BF16),
            pltpu.VMEM((3 * window // 2, channels), BF16),
            pltpu.VMEM((2 * window, channels), F32),
            pltpu.VMEM((window // 2, channels), F32),
        ],
        flops=45 * window * channels * channels,
    )


def solution(mesh):
    in_specs = (
        P(("groups", "blk"), "head"),
        P(),
        P(None, None, "head"),
        P("head", None),
        P(),
        P(),
        P(),
    )
    out_specs = (P(("groups", "blk"), "head", None), P(("groups", "blk"), "head", None))
    return jax.shard_map(body, mesh=mesh, in_specs=in_specs, out_specs=out_specs, check_vma=False)
```

```python
import functools
import math

import jax
import jax.numpy as jnp
from jax import lax
from jax.experimental import pallas as pl
from jax.experimental.pallas import tpu as pltpu
from jax.sharding import PartitionSpec as P

HEAD_DIM = 64
LANES = 128
GRID_COLS = 96
EPS = 1e-06
BF16 = jnp.bfloat16
F32 = jnp.float32
VMEM_LIMIT = 48 * 1024 * 1024


def specs(count, space=pltpu.VMEM):
    return [pl.BlockSpec(memory_space=space)] * count


def kernel_params():
    return pltpu.CompilerParams(vmem_limit_bytes=VMEM_LIMIT)


def nbytes(*arrays):
    return sum(math.prod(a.shape) * jnp.dtype(a.dtype).itemsize for a in arrays)


def call(kernel, outs, args, scratch=(), flops=0, exps=0, space=pltpu.VMEM):
    outs = tuple(jax.ShapeDtypeStruct(shape, dtype) for shape, dtype in outs)
    return pl.pallas_call(
        kernel,
        out_shape=outs,
        in_specs=specs(len(args), space),
        out_specs=tuple(specs(len(outs))),
        scratch_shapes=list(scratch),
        compiler_params=kernel_params(),
        cost_estimate=pl.CostEstimate(
            flops=flops, transcendentals=exps, bytes_accessed=nbytes(*args, *outs)
        ),
    )(*args)


def layer_norm(values_in, gain_row):
    mean_row = jnp.mean(values_in, axis=-1, keepdims=True)
    centred = values_in - mean_row
    spread = jnp.mean(centred * centred, axis=-1, keepdims=True)
    return centred * lax.rsqrt(spread + EPS) * gain_row


def dot(a, b):
    return jnp.dot(a, b, preferred_element_type=F32)


def low_lanes(shape):
    return lax.broadcasted_iota(jnp.int32, shape, len(shape) - 1) % LANES < HEAD_DIM


def half_turn(tile):
    return pltpu.roll(tile, HEAD_DIM, axis=1)


def fetch_kernel(weight_ref, out_ref, sems):
    copies = [
        pltpu.make_async_copy(weight_ref.at[part], out_ref.at[part], sems.at[part])
        for part in range(weight_ref.shape[0])
    ]
    for copy in copies:
        copy.start()
    for copy in copies:
        copy.wait()


def project(mine_ref, other_ref, gain_ref, weight_ref):
    core = lax.axis_index("head")
    half = mine_ref.shape[1]
    width = 2 * half
    mine, other = mine_ref[...], other_ref[...]
    mean = (
        jnp.sum(mine, axis=-1, keepdims=True) + jnp.sum(other, axis=-1, keepdims=True)
    ) / width
    mine, other = mine - mean, other - mean
    spread = (
        jnp.sum(mine * mine, axis=-1, keepdims=True)
        + jnp.sum(other * other, axis=-1, keepdims=True)
    ) / width
    scale = lax.rsqrt(spread + EPS)
    low_gain, high_gain = gain_ref[:half][None, :], gain_ref[half:][None, :]
    first = core == 0
    mine = (mine * scale * jnp.where(first, low_gain, high_gain)).astype(BF16)
    other = (other * scale * jnp.where(first, high_gain, low_gain)).astype(BF16)
    mine_at = pl.ds(pl.multiple_of(core * half, half), half)
    other_at = pl.ds(pl.multiple_of((1 - core) * half, half), half)
    return [
        dot(mine, weight_ref[part, mine_at, :]) + dot(other, weight_ref[part, other_at, :])
        for part in range(3)
    ]


def qkv_kernel(mine_ref, other_ref, gain_ref, weight_ref, send_ref):
    queries, keys, values = project(mine_ref, other_ref, gain_ref, weight_ref)
    rows = queries.shape[0]
    low = low_lanes((rows, LANES))
    low_q = low_lanes((rows // 2, LANES))
    for pair in range(queries.shape[1] // LANES):
        cols = slice(pair * LANES, (pair + 1) * LANES)
        key, value = keys[:, cols], values[:, cols]
        top, bottom = queries[: rows // 2, cols], queries[rows // 2 :, cols]
        send_ref[2 * pair, :rows] = jnp.where(low, key, half_turn(value)).astype(BF16)
        send_ref[2 * pair + 1, :rows] = jnp.where(low, half_turn(key), value).astype(BF16)
        send_ref[2 * pair, rows:] = jnp.where(low_q, top, half_turn(bottom)).astype(BF16)
        send_ref[2 * pair + 1, rows:] = jnp.where(low_q, half_turn(top), bottom).astype(BF16)


def plain_qkv_kernel(mine_ref, other_ref, gain_ref, weight_ref, q_ref, k_ref, v_ref):
    for ref, value in zip(
        (q_ref, k_ref, v_ref), project(mine_ref, other_ref, gain_ref, weight_ref)
    ):
        ref[...] = value.astype(BF16)


def attend_kernel(got_ref, out_ref, pair_ref, query_ref, value_ref, mixed_ref):
    blocks, packed_rows = got_ref.shape[0], out_ref.shape[1]
    rows = 2 * packed_rows
    share = blocks * packed_rows
    low = low_lanes((packed_rows, LANES))
    for block in range(blocks):
        pair_ref[block * rows : (block + 1) * rows] = got_ref[block, :rows]
        packed = got_ref[block, rows:].astype(F32)
        here = block * packed_rows
        query_ref[here : here + packed_rows] = jnp.where(low, packed, 0.0).astype(BF16)
        query_ref[share + here : share + here + packed_rows] = jnp.where(
            low, half_turn(packed), 0.0
        ).astype(BF16)
    value_ref[...] = pair_ref[...].astype(F32).T[HEAD_DIM:].astype(BF16)
    factor = HEAD_DIM ** (-0.5) * math.log2(math.e)
    tile = math.gcd(share, 256)
    for part in range(2):
        for start in range(0, share, tile):
            queries = query_ref[part * share + start : part * share + start + tile]
            scores = lax.dot_general(
                pair_ref[...], queries, (((1,), (1,)), ((), ())), preferred_element_type=F32
            )
            top = jnp.max(scores, axis=0, keepdims=True)
            weights = jnp.exp2((scores - top) * factor)
            total = jnp.sum(weights, axis=0, keepdims=True)
            mixed = dot(value_ref[...], weights.astype(BF16)) / total
            mixed_ref[part * HEAD_DIM : (part + 1) * HEAD_DIM, start : start + tile] = mixed
    out_ref[...] = mixed_ref[...].T.astype(BF16).reshape(out_ref.shape)


def out_terms(attended, weight_ref, mine_ref, other_ref, send_ref, keep_ref, full_ref):
    core = lax.axis_index("head")
    window = send_ref.shape[1]
    half = mine_ref.shape[1]
    shift = GRID_COLS - window
    full_ref[...] = dot(attended, weight_ref[...])
    for row in range(send_ref.shape[0]):
        there = pl.ds(pl.multiple_of(row * GRID_COLS + (1 - core) * shift, 8), window)
        send_ref[row] = full_ref[there, :].astype(BF16)
        here = pl.ds(pl.multiple_of(row * GRID_COLS + core * shift, 8), window)
        for part, ref in ((core, mine_ref), (1 - core, other_ref)):
            cols = pl.ds(pl.multiple_of(part * half, half), half)
            keep_ref[row, :, cols] = full_ref[here, cols] + ref[here, :]


def out_kernel(back_ref, weight_ref, mine_ref, other_ref, send_ref, keep_ref, full_ref, att_ref):
    packed_rows = back_ref.shape[1]
    low = low_lanes((packed_rows, LANES))
    for pair in range(back_ref.shape[0] // 2):
        cols = slice(pair * LANES, (pair + 1) * LANES)
        left = back_ref[2 * pair].astype(F32)
        right = back_ref[2 * pair + 1].astype(F32)
        att_ref[:packed_rows, cols] = jnp.where(low, left, half_turn(right)).astype(BF16)
        att_ref[packed_rows:, cols] = jnp.where(low, half_turn(left), right).astype(BF16)
    out_terms(att_ref[...], weight_ref, mine_ref, other_ref, send_ref, keep_ref, full_ref)


def plain_out_kernel(att_ref, weight_ref, mine_ref, other_ref, send_ref, keep_ref, full_ref):
    out_terms(att_ref[...], weight_ref, mine_ref, other_ref, send_ref, keep_ref, full_ref)


def lateral_kernel(
    keep_ref, got_ref, lateral_ref, gain_ref, near_ref, far_ref, pool_ref, fine_ref
):
    odd = lax.axis_index("blk") % 2
    window, features = keep_ref.shape[1], keep_ref.shape[2]
    cells = (keep_ref[...] + got_ref[...].astype(F32)).astype(BF16)
    fine_ref[...] = layer_norm(
        dot(cells.reshape(2 * window, features), lateral_ref[0]), gain_ref[0, 0][None, :]
    ).astype(BF16)
    near_ref[:window] = fine_ref[pl.ds(pl.multiple_of((1 - odd) * window, window), window), :]
    far_ref[:window] = fine_ref[pl.ds(pl.multiple_of(odd * window, window), window), :]
    tall = jnp.maximum(cells[0].astype(F32), cells[1].astype(F32))
    pooled = []
    for part in range(features // LANES):
        pool_ref[part] = tall[:, part * LANES : (part + 1) * LANES]
        even = pool_ref[part, pl.ds(0, window // 2, stride=2), :]
        odd = pool_ref[part, pl.ds(1, window // 2, stride=2), :]
        pooled.append(jnp.maximum(even, odd).astype(BF16))
    pooled = jnp.concatenate(pooled, axis=1)
    coarse = layer_norm(dot(pooled, lateral_ref[1]), gain_ref[1, 0][None, :]).astype(BF16)
    near_ref[window:] = coarse
    far_ref[window:] = coarse


def conv_level(stacked_ref, weight_ref, level, rows, window, sum_ref):
    block = rows * window
    place = lax.broadcasted_iota(jnp.int32, (block, weight_ref.shape[-1]), 0) % window
    taps = []
    for tap_col in range(3):
        total = None
        for tap_row in range(3):
            term = dot(
                stacked_ref[tap_row * window : tap_row * window + block],
                weight_ref[level, tap_row, tap_col],
            )
            total = term if total is None else total + term
        taps.append(total)
    left = jnp.where(place == 0, 0.0, pltpu.roll(taps[0], 1, axis=0))
    right = jnp.where(place == window - 1, 0.0, pltpu.roll(taps[2], block - 1, axis=0))
    sum_ref[...] = left + taps[1] + right


def conv_kernel(
    near_ref,
    far_ref,
    got_near_ref,
    got_far_ref,
    weight_ref,
    gain_ref,
    fine_ref,
    coarse_ref,
    fine_in,
    coarse_in,
    fine_sum,
    coarse_sum,
):
    core = lax.axis_index("head")
    odd = lax.axis_index("blk") % 2
    window = fine_sum.shape[0] // 2
    half = window // 2
    for ref, place in (
        (near_ref, 2 - odd),
        (far_ref, 1 + odd),
        (got_near_ref, 3 - 3 * odd),
        (got_far_ref, 3 * odd),
    ):
        fine_in[pl.ds(pl.multiple_of(place * window, window), window), :] = ref[:window]
    coarse_in[half : 2 * half] = near_ref[window:]
    for ref, place in ((got_near_ref, 2 - 2 * odd), (got_far_ref, 2 * odd)):
        coarse_in[pl.ds(pl.multiple_of(place * half, half), half), :] = ref[window:]
    conv_level(fine_in, weight_ref, 0, 2, window, fine_sum)
    conv_level(coarse_in, weight_ref, 1, 1, half, coarse_sum)
    cols = fine_ref.shape[1]
    shift = GRID_COLS - window
    inset = cols - shift
    for row in range(2):
        here = pl.ds(pl.multiple_of(row * window + core * inset, 8), cols)
        fine_ref[row] = layer_norm(fine_sum[here, :], gain_ref[0, 1][None, :]).astype(BF16)
    here = pl.ds(pl.multiple_of(core * (inset // 2), 8), cols // 2)
    coarse_ref[0] = layer_norm(coarse_sum[here, :], gain_ref[1, 1][None, :]).astype(BF16)


def attend_shared(queries, keys, values):
    factor = HEAD_DIM ** (-0.5)
    step = math.gcd(keys.shape[0], 1536)
    rows = queries.shape[0]

    def block(state, pair):
        running, totals, weighted = state
        key, value = pair
        scores = (
            lax.dot_general(queries, key, (((1,), (1,)), ((), ())), preferred_element_type=F32)
            * factor
        )
        newmax = jnp.maximum(running, jnp.max(scores, axis=-1, keepdims=True))
        weights = jnp.exp(scores - newmax)
        shrink = jnp.exp(running - newmax)
        totals = totals * shrink + jnp.sum(weights, axis=-1, keepdims=True)
        weighted = weighted * shrink + dot(weights.astype(BF16), value)
        return (newmax, totals, weighted), None

    state = (
        jnp.full((rows, 1), -jnp.inf, F32),
        jnp.zeros((rows, 1), F32),
        jnp.zeros((rows, HEAD_DIM), F32),
    )
    state, _ = lax.scan(
        block, state, (keys.reshape(-1, step, HEAD_DIM), values.reshape(-1, step, HEAD_DIM))
    )
    return (state[2] / state[1]).astype(BF16)


def exchange(value):
    return lax.all_to_all(value, "blk", split_axis=0, concat_axis=0, tiled=True)


def attention_shared(mine, other, norm_gain, qkv_weight, slices):
    rows = mine.shape[0]
    width = qkv_weight.shape[2]
    heads = width // HEAD_DIM
    blocks = heads * slices
    share = rows // slices
    queries, keys, values = call(
        plain_qkv_kernel, [((rows, width), BF16)] * 3, (mine, other, norm_gain, qkv_weight)
    )
    query_send = jnp.transpose(
        queries.reshape(slices, share, heads, HEAD_DIM), (2, 0, 1, 3)
    ).reshape(blocks, share * HEAD_DIM)
    pair = jnp.concatenate(
        (keys.reshape(rows, heads, HEAD_DIM), values.reshape(rows, heads, HEAD_DIM)), axis=2
    )
    pair = jnp.transpose(pair, (1, 0, 2))
    pair_send = jnp.broadcast_to(pair[:, None], (heads, slices, rows, 2 * HEAD_DIM)).reshape(
        blocks, rows, 2 * HEAD_DIM
    )
    query_got = exchange(query_send).reshape(blocks * share, HEAD_DIM)
    pair_got = exchange(pair_send).reshape(blocks * rows, 2 * HEAD_DIM)
    one_head = attend_shared(query_got, pair_got[:, :HEAD_DIM], pair_got[:, HEAD_DIM:])
    back = exchange(one_head.reshape(blocks, share * HEAD_DIM))
    return jnp.transpose(back.reshape(heads, slices, share, HEAD_DIM), (1, 2, 0, 3)).reshape(
        rows, width
    )


def body(tokens, norm_gain, qkv_weight, out_weight, lateral_weight, conv_weight, level_gains):
    rows, half = tokens.shape
    features = out_weight.shape[1]
    width = qkv_weight.shape[2]
    heads = width // HEAD_DIM
    blocks = lax.axis_size("blk")
    cores = lax.axis_size("head")
    grid_rows = rows // GRID_COLS
    cols = GRID_COLS // cores
    channels = lateral_weight.shape[2]
    window = 2 * GRID_COLS // 3
    swap = [(i, cores - 1 - i) for i in range(cores)]

    other = lax.ppermute(tokens, "head", swap)
    (near_weight,) = call(
        fetch_kernel,
        [(qkv_weight.shape, BF16)],
        (qkv_weight,),
        [pltpu.SemaphoreType.DMA((qkv_weight.shape[0],))],
        space=pltpu.HBM,
    )
    tail = (out_weight, tokens, other)
    tail_outs = [
        ((grid_rows, window, features), BF16),
        ((grid_rows, window, features), F32),
    ]
    full = pltpu.VMEM((rows, features), F32)
    out_flops = 2 * rows * width * features
    if heads == blocks:
        (send,) = call(
            qkv_kernel,
            [((blocks, rows + rows // 2, LANES), BF16)],
            (tokens, other, norm_gain, near_weight),
            flops=6 * rows * features * width,
        )
        got = exchange(send)
        total = blocks * rows
        (one_head,) = call(
            attend_kernel,
            [((blocks, rows // 2, LANES), BF16)],
            (got,),
            [
                pltpu.VMEM((total, LANES), BF16),
                pltpu.VMEM((total, LANES), BF16),
                pltpu.VMEM((HEAD_DIM, total), BF16),
                pltpu.VMEM((2 * HEAD_DIM, total // 2), F32),
            ],
            flops=4 * total * total * LANES,
            exps=total * total,
        )
        back = exchange(one_head)
        peer_term, keep = call(
            out_kernel,
            tail_outs,
            (back,) + tail,
            [full, pltpu.VMEM((rows, width), BF16)],
            flops=out_flops,
        )
    else:
        attended = attention_shared(
            tokens, other, norm_gain, near_weight, blocks // heads
        )
        peer_term, keep = call(plain_out_kernel, tail_outs, (attended,) + tail, [full], out_flops)
    peer_term = lax.ppermute(peer_term, "head", swap)

    message = (window + window // 2, channels)
    near, far = call(
        lateral_kernel,
        [(message, BF16), (message, BF16)],
        (keep, peer_term, lateral_weight, level_gains),
        [
            pltpu.VMEM((features // LANES, window, LANES), F32),
            pltpu.VMEM((2 * window, channels), BF16),
        ],
        flops=5 * window * features * channels,
    )
    far_pairs = [(i, i + 1) for i in range(1, blocks - 1, 2)]
    far_pairs += [(j, i) for i, j in far_pairs]
    got_far = lax.ppermute(far, "blk", far_pairs)
    got_near = lax.ppermute(near, "blk", [(i, i ^ 1) for i in range(blocks)])
    return call(
        conv_kernel,
        [((grid_rows, cols, channels), BF16), ((grid_rows // 2, cols // 2, channels), BF16)],
        (near, far, got_near, got_far, conv_weight, level_gains),
        [
            pltpu.VMEM((4 * window, channels), BF16),
            pltpu.VMEM((3 * window // 2, channels), BF16),
            pltpu.VMEM((2 * window, channels), F32),
            pltpu.VMEM((window // 2, channels), F32),
        ],
        flops=45 * window * channels * channels,
    )


def solution(mesh):
    in_specs = (
        P(("groups", "blk"), "head"),
        P(),
        P(None, None, "head"),
        P("head", None),
        P(),
        P(),
        P(),
    )
    out_specs = (P(("groups", "blk"), "head", None), P(("groups", "blk"), "head", None))
    return jax.shard_map(body, mesh=mesh, in_specs=in_specs, out_specs=out_specs, check_vma=False)
```

```python
import functools
import math

import jax
import jax.numpy as jnp
from jax import lax
from jax.experimental import pallas as pl
from jax.experimental.pallas import tpu as pltpu
from jax.sharding import PartitionSpec as P

HEAD_DIM = 64
LANES = 128
GRID_COLS = 96
EPS = 1e-06
BF16 = jnp.bfloat16
F32 = jnp.float32
MIB = 1024 * 1024


def specs(count):
    return [pl.BlockSpec(memory_space=pltpu.VMEM)] * count


def nbytes(*arrays):
    return sum(math.prod(a.shape) * jnp.dtype(a.dtype).itemsize for a in arrays)


def call(kernel, outs, args, scratch=(), flops=0, exps=0, limit=24):
    outs = tuple(jax.ShapeDtypeStruct(shape, dtype) for shape, dtype in outs)
    return pl.pallas_call(
        kernel,
        out_shape=outs,
        in_specs=specs(len(args)),
        out_specs=tuple(specs(len(outs))),
        scratch_shapes=list(scratch),
        compiler_params=pltpu.CompilerParams(vmem_limit_bytes=limit * MIB),
        cost_estimate=pl.CostEstimate(
            flops=flops, transcendentals=exps, bytes_accessed=nbytes(*args, *outs)
        ),
    )(*args)


def layer_norm(values_in, gain_row):
    mean_row = jnp.mean(values_in, axis=-1, keepdims=True)
    centred = values_in - mean_row
    spread = jnp.mean(centred * centred, axis=-1, keepdims=True)
    return centred * lax.rsqrt(spread + EPS) * gain_row


def dot(a, b):
    return jnp.dot(a, b, preferred_element_type=F32)


def low_lanes(shape):
    return lax.broadcasted_iota(jnp.int32, shape, len(shape) - 1) % LANES < HEAD_DIM


def half_turn(tile):
    return pltpu.roll(tile, HEAD_DIM, axis=1)


def normalize(mine_ref, other_ref, gain_ref):
    half = mine_ref.shape[1]
    width = 2 * half
    mine, other = mine_ref[...], other_ref[...]
    mean = (
        jnp.sum(mine, axis=-1, keepdims=True) + jnp.sum(other, axis=-1, keepdims=True)
    ) / width
    mine, other = mine - mean, other - mean
    spread = (
        jnp.sum(mine * mine, axis=-1, keepdims=True)
        + jnp.sum(other * other, axis=-1, keepdims=True)
    ) / width
    scale = lax.rsqrt(spread + EPS)
    low_gain, high_gain = gain_ref[:half][None, :], gain_ref[half:][None, :]
    first = lax.axis_index("head") == 0
    mine = (mine * scale * jnp.where(first, low_gain, high_gain)).astype(BF16)
    other = (other * scale * jnp.where(first, high_gain, low_gain)).astype(BF16)
    return mine, other


def norm_kernel(mine_ref, other_ref, gain_ref, mine_out, other_out):
    mine_out[...], other_out[...] = normalize(mine_ref, other_ref, gain_ref)


def project(mine, other, weight_ref, part):
    core = lax.axis_index("head")
    half = mine.shape[1]
    mine_at = pl.ds(pl.multiple_of(core * half, half), half)
    other_at = pl.ds(pl.multiple_of((1 - core) * half, half), half)
    return (
        dot(mine, weight_ref[part, mine_at, :]) + dot(other, weight_ref[part, other_at, :])
    ).astype(BF16)


def plain_qkv_kernel(mine_ref, other_ref, gain_ref, weight_ref, *out_refs):
    mine, other = normalize(mine_ref, other_ref, gain_ref)
    for part, ref in enumerate(out_refs):
        ref[...] = project(mine, other, weight_ref, part)


def spread_lanes(column, width=LANES):
    return jnp.broadcast_to(column, (column.shape[0], width))


def across(lanes, width):
    whole, rest = divmod(width, LANES)
    return jnp.concatenate([lanes] * whole + ([lanes[:, :rest]] if rest else []), axis=1)


def absorb(pair, queries, keys, values, old):
    factor = HEAD_DIM ** (-0.5) * math.log2(math.e)
    cols = slice(pair * LANES, (pair + 1) * LANES)
    scores = lax.dot_general(
        queries, keys[:, cols], (((1,), (1,)), ((), ())), preferred_element_type=F32
    )
    top = spread_lanes(jnp.max(scores, axis=-1, keepdims=True))
    if old is not None:
        old_top, old_total, old_mixed = old
        top = jnp.maximum(top, old_top)
    weights = jnp.exp2((scores - across(top, scores.shape[1])) * factor)
    total = spread_lanes(jnp.sum(weights, axis=-1, keepdims=True))
    mixed = dot(weights.astype(BF16), values[:, cols])
    rows = mixed.shape[0] // 2
    low = low_lanes((rows, LANES))
    mixed = jnp.where(low, mixed[:rows], mixed[rows:])
    if old is not None:
        shrink = jnp.exp2((old_top - top) * factor)
        total = total + old_total * shrink
        mixed = mixed + old_mixed * jnp.where(low, shrink[:rows], shrink[rows:])
    return top, total, mixed


def own_kernel(
    mine_ref, other_ref, weight_ref, query_ref, top_ref, total_ref, mixed_ref
):
    mine, other = mine_ref[...], other_ref[...]
    rows = mine.shape[0]
    queries = project(mine, other, weight_ref, 0)
    keys = project(mine, other, weight_ref, 1)
    values = project(mine, other, weight_ref, 2)
    low = low_lanes((rows, LANES))
    for pair in range(query_ref.shape[0]):
        tile = queries[:, pair * LANES : (pair + 1) * LANES]
        query_ref[pair, :rows] = jnp.where(low, tile, jnp.zeros_like(tile))
        query_ref[pair, rows:] = jnp.where(low, jnp.zeros_like(tile), tile)
        top_ref[pair], total_ref[pair], mixed_ref[pair] = absorb(
            pair, query_ref[pair], keys, values, None
        )


def absorb_blocks(mine_refs, other_refs, weight_ref, query_ref, top_ref, total_ref, mixed_ref):
    mine = jnp.concatenate([ref[...] for ref in mine_refs], axis=0)
    other = jnp.concatenate([ref[...] for ref in other_refs], axis=0)
    keys = project(mine, other, weight_ref, 1)
    values = project(mine, other, weight_ref, 2)
    for pair in range(query_ref.shape[0]):
        old = top_ref[pair], total_ref[pair], mixed_ref[pair]
        yield pair, absorb(pair, query_ref[pair], keys, values, old)


def step_kernel(
    mine_a,
    mine_b,
    other_a,
    other_b,
    weight_ref,
    query_ref,
    top_ref,
    total_ref,
    mixed_ref,
    top_out,
    total_out,
    mixed_out,
):
    for pair, state in absorb_blocks(
        (mine_a, mine_b), (other_a, other_b), weight_ref, query_ref, top_ref, total_ref, mixed_ref
    ):
        top_out[pair], total_out[pair], mixed_out[pair] = state


def out_terms(attended, weight_ref, mine_ref, other_ref, send_ref, keep_ref, full_ref):
    core = lax.axis_index("head")
    window = send_ref.shape[1]
    half = mine_ref.shape[1]
    shift = GRID_COLS - window
    full_ref[...] = dot(attended, weight_ref[...])
    for row in range(send_ref.shape[0]):
        there = pl.ds(pl.multiple_of(row * GRID_COLS + (1 - core) * shift, 8), window)
        send_ref[row] = full_ref[there, :].astype(BF16)
        here = pl.ds(pl.multiple_of(row * GRID_COLS + core * shift, 8), window)
        for part, ref in ((core, mine_ref), (1 - core, other_ref)):
            cols = pl.ds(pl.multiple_of(part * half, half), half)
            keep_ref[row, :, cols] = full_ref[here, cols] + ref[here, :]


def last_kernel(
    mine_a,
    mine_b,
    other_a,
    other_b,
    weight_ref,
    query_ref,
    top_ref,
    total_ref,
    mixed_ref,
    out_weight_ref,
    tokens_ref,
    other_tokens_ref,
    send_ref,
    keep_ref,
    full_ref,
    att_ref,
):
    rows = mixed_ref.shape[1]
    low = low_lanes((rows, LANES))
    for pair, (_, total, mixed) in absorb_blocks(
        (mine_a, mine_b), (other_a, other_b), weight_ref, query_ref, top_ref, total_ref, mixed_ref
    ):
        cols = slice(pair * LANES, (pair + 1) * LANES)
        att_ref[:, cols] = (mixed / jnp.where(low, total[:rows], total[rows:])).astype(BF16)
    out_terms(
        att_ref[...], out_weight_ref, tokens_ref, other_tokens_ref, send_ref, keep_ref, full_ref
    )


def plain_out_kernel(att_ref, weight_ref, mine_ref, other_ref, send_ref, keep_ref, full_ref):
    out_terms(att_ref[...], weight_ref, mine_ref, other_ref, send_ref, keep_ref, full_ref)


def lateral_kernel(
    keep_ref, got_ref, lateral_ref, gain_ref, near_ref, far_ref, pool_ref, fine_ref
):
    odd = lax.axis_index("blk") % 2
    window, features = keep_ref.shape[1], keep_ref.shape[2]
    cells = (keep_ref[...] + got_ref[...].astype(F32)).astype(BF16)
    fine_ref[...] = layer_norm(
        dot(cells.reshape(2 * window, features), lateral_ref[0]), gain_ref[0, 0][None, :]
    ).astype(BF16)
    near_ref[:window] = fine_ref[pl.ds(pl.multiple_of((1 - odd) * window, window), window), :]
    far_ref[:window] = fine_ref[pl.ds(pl.multiple_of(odd * window, window), window), :]
    tall = jnp.maximum(cells[0].astype(F32), cells[1].astype(F32))
    pooled = []
    for part in range(features // LANES):
        pool_ref[part] = tall[:, part * LANES : (part + 1) * LANES]
        even = pool_ref[part, pl.ds(0, window // 2, stride=2), :]
        odd = pool_ref[part, pl.ds(1, window // 2, stride=2), :]
        pooled.append(jnp.maximum(even, odd).astype(BF16))
    pooled = jnp.concatenate(pooled, axis=1)
    coarse = layer_norm(dot(pooled, lateral_ref[1]), gain_ref[1, 0][None, :]).astype(BF16)
    near_ref[window:] = coarse
    far_ref[window:] = coarse


def conv_level(stacked_ref, weight_ref, level, rows, window, sum_ref):
    block = rows * window
    place = lax.broadcasted_iota(jnp.int32, (block, weight_ref.shape[-1]), 0) % window
    taps = []
    for tap_col in range(3):
        total = None
        for tap_row in range(3):
            term = dot(
                stacked_ref[tap_row * window : tap_row * window + block],
                weight_ref[level, tap_row, tap_col],
            )
            total = term if total is None else total + term
        taps.append(total)
    left = jnp.where(place == 0, 0.0, pltpu.roll(taps[0], 1, axis=0))
    right = jnp.where(place == window - 1, 0.0, pltpu.roll(taps[2], block - 1, axis=0))
    sum_ref[...] = left + taps[1] + right


def conv_kernel(
    near_ref,
    far_ref,
    got_near_ref,
    got_far_ref,
    weight_ref,
    gain_ref,
    fine_ref,
    coarse_ref,
    fine_in,
    coarse_in,
    fine_sum,
    coarse_sum,
):
    core = lax.axis_index("head")
    odd = lax.axis_index("blk") % 2
    window = fine_sum.shape[0] // 2
    half = window // 2
    for ref, place in (
        (near_ref, 2 - odd),
        (far_ref, 1 + odd),
        (got_near_ref, 3 - 3 * odd),
        (got_far_ref, 3 * odd),
    ):
        fine_in[pl.ds(pl.multiple_of(place * window, window), window), :] = ref[:window]
    coarse_in[half : 2 * half] = near_ref[window:]
    for ref, place in ((got_near_ref, 2 - 2 * odd), (got_far_ref, 2 * odd)):
        coarse_in[pl.ds(pl.multiple_of(place * half, half), half), :] = ref[window:]
    conv_level(fine_in, weight_ref, 0, 2, window, fine_sum)
    conv_level(coarse_in, weight_ref, 1, 1, half, coarse_sum)
    cols = fine_ref.shape[1]
    shift = GRID_COLS - window
    inset = cols - shift
    for row in range(2):
        here = pl.ds(pl.multiple_of(row * window + core * inset, 8), cols)
        fine_ref[row] = layer_norm(fine_sum[here, :], gain_ref[0, 1][None, :]).astype(BF16)
    here = pl.ds(pl.multiple_of(core * (inset // 2), 8), cols // 2)
    coarse_ref[0] = layer_norm(coarse_sum[here, :], gain_ref[1, 1][None, :]).astype(BF16)


def attend_shared(queries, keys, values):
    factor = HEAD_DIM ** (-0.5)
    step = math.gcd(keys.shape[0], 1536)
    rows = queries.shape[0]

    def block(state, pair):
        running, totals, weighted = state
        key, value = pair
        scores = (
            lax.dot_general(queries, key, (((1,), (1,)), ((), ())), preferred_element_type=F32)
            * factor
        )
        newmax = jnp.maximum(running, jnp.max(scores, axis=-1, keepdims=True))
        weights = jnp.exp(scores - newmax)
        shrink = jnp.exp(running - newmax)
        totals = totals * shrink + jnp.sum(weights, axis=-1, keepdims=True)
        weighted = weighted * shrink + dot(weights.astype(BF16), value)
        return (newmax, totals, weighted), None

    state = (
        jnp.full((rows, 1), -jnp.inf, F32),
        jnp.zeros((rows, 1), F32),
        jnp.zeros((rows, HEAD_DIM), F32),
    )
    state, _ = lax.scan(
        block, state, (keys.reshape(-1, step, HEAD_DIM), values.reshape(-1, step, HEAD_DIM))
    )
    return (state[2] / state[1]).astype(BF16)


def exchange(value):
    return lax.all_to_all(value, "blk", split_axis=0, concat_axis=0, tiled=True)


def attention_shared(mine, other, norm_gain, qkv_weight, slices):
    rows = mine.shape[0]
    width = qkv_weight.shape[2]
    heads = width // HEAD_DIM
    blocks = heads * slices
    share = rows // slices
    queries, keys, values = call(
        plain_qkv_kernel, [((rows, width), BF16)] * 3, (mine, other, norm_gain, qkv_weight)
    )
    query_send = jnp.transpose(
        queries.reshape(slices, share, heads, HEAD_DIM), (2, 0, 1, 3)
    ).reshape(blocks, share * HEAD_DIM)
    pair = jnp.concatenate(
        (keys.reshape(rows, heads, HEAD_DIM), values.reshape(rows, heads, HEAD_DIM)), axis=2
    )
    pair = jnp.transpose(pair, (1, 0, 2))
    pair_send = jnp.broadcast_to(pair[:, None], (heads, slices, rows, 2 * HEAD_DIM)).reshape(
        blocks, rows, 2 * HEAD_DIM
    )
    query_got = exchange(query_send).reshape(blocks * share, HEAD_DIM)
    pair_got = exchange(pair_send).reshape(blocks * rows, 2 * HEAD_DIM)
    one_head = attend_shared(query_got, pair_got[:, :HEAD_DIM], pair_got[:, HEAD_DIM:])
    back = exchange(one_head.reshape(blocks, share * HEAD_DIM))
    return jnp.transpose(back.reshape(heads, slices, share, HEAD_DIM), (1, 2, 0, 3)).reshape(
        rows, width
    )


def body(tokens, norm_gain, qkv_weight, out_weight, lateral_weight, conv_weight, level_gains):
    rows, half = tokens.shape
    features = out_weight.shape[1]
    width = qkv_weight.shape[2]
    heads = width // HEAD_DIM
    blocks = lax.axis_size("blk")
    cores = lax.axis_size("head")
    grid_rows = rows // GRID_COLS
    cols = GRID_COLS // cores
    channels = lateral_weight.shape[2]
    window = 2 * GRID_COLS // 3
    swap = [(i, cores - 1 - i) for i in range(cores)]

    other = lax.ppermute(tokens, "head", swap)
    tail = (out_weight, tokens, other)
    tail_outs = [
        ((grid_rows, window, features), BF16),
        ((grid_rows, window, features), F32),
    ]
    full = pltpu.VMEM((rows, features), F32)
    out_flops = 2 * rows * width * features
    if blocks <= heads:
        order = list(range(0, blocks, 2)) + list(range(blocks - 1, 0, -2))
        forth = [(order[i - 1], order[i]) for i in range(blocks)]
        back = [(target, source) for source, target in forth]
        mine, across_core = call(
            norm_kernel, [((rows, half), BF16)] * 2, (tokens, other, norm_gain)
        )
        pairs = width // LANES
        state_outs = [
            ((pairs, 2 * rows, LANES), F32),
            ((pairs, 2 * rows, LANES), F32),
            ((pairs, rows, LANES), F32),
        ]
        ahead = lax.ppermute(mine, "blk", forth)
        behind = lax.ppermute(mine, "blk", back)
        unit = 4 * rows * width * (features + rows)
        queries, *state = call(
            own_kernel,
            [((pairs, 2 * rows, LANES), BF16)] + state_outs,
            (mine, across_core, qkv_weight),
            flops=unit + 2 * rows * width * features,
            exps=heads * rows * rows,
        )
        ahead, behind, queries, state = lax.optimization_barrier((ahead, behind, queries, state))
        for step in range(1, blocks // 2):
            parts = (ahead, behind)
            others = tuple(lax.ppermute(part, "head", swap) for part in parts)
            if step == blocks // 2 - 1:
                ahead = lax.ppermute(ahead[: rows // 2], "blk", forth)
                behind = lax.ppermute(behind[rows // 2 :], "blk", back)
            else:
                ahead = lax.ppermute(ahead, "blk", forth)
                behind = lax.ppermute(behind, "blk", back)
            state = call(
                step_kernel,
                state_outs,
                parts + others + (qkv_weight, queries) + tuple(state),
                flops=2 * unit,
                exps=2 * heads * rows * rows,
            )
            ahead, behind, state = lax.optimization_barrier((ahead, behind, state))
        parts = (ahead, behind)
        others = tuple(lax.ppermute(part, "head", swap) for part in parts)
        peer_term, keep = call(
            last_kernel,
            tail_outs,
            parts + others + (qkv_weight, queries) + tuple(state) + tail,
            [full, pltpu.VMEM((rows, width), BF16)],
            flops=unit + out_flops,
            exps=heads * rows * rows,
        )
    else:
        attended = attention_shared(
            tokens, other, norm_gain, qkv_weight, blocks // heads
        )
        peer_term, keep = call(plain_out_kernel, tail_outs, (attended,) + tail, [full], out_flops)
    peer_term = lax.ppermute(peer_term, "head", swap)

    message = (window + window // 2, channels)
    near, far = call(
        lateral_kernel,
        [(message, BF16), (message, BF16)],
        (keep, peer_term, lateral_weight, level_gains),
        [
            pltpu.VMEM((features // LANES, window, LANES), F32),
            pltpu.VMEM((2 * window, channels), BF16),
        ],
        flops=5 * window * features * channels,
    )
    far_pairs = [(i, i + 1) for i in range(1, blocks - 1, 2)]
    far_pairs += [(j, i) for i, j in far_pairs]
    got_far = lax.ppermute(far, "blk", far_pairs)
    got_near = lax.ppermute(near, "blk", [(i, i ^ 1) for i in range(blocks)])
    return call(
        conv_kernel,
        [((grid_rows, cols, channels), BF16), ((grid_rows // 2, cols // 2, channels), BF16)],
        (near, far, got_near, got_far, conv_weight, level_gains),
        [
            pltpu.VMEM((4 * window, channels), BF16),
            pltpu.VMEM((3 * window // 2, channels), BF16),
            pltpu.VMEM((2 * window, channels), F32),
            pltpu.VMEM((window // 2, channels), F32),
        ],
        flops=45 * window * channels * channels,
    )


def solution(mesh):
    in_specs = (
        P(("groups", "blk"), "head"),
        P(),
        P(None, None, "head"),
        P("head", None),
        P(),
        P(),
        P(),
    )
    out_specs = (P(("groups", "blk"), "head", None), P(("groups", "blk"), "head", None))
    return jax.shard_map(body, mesh=mesh, in_specs=in_specs, out_specs=out_specs, check_vma=False)
```

```python
import math

import jax
import jax.numpy as jnp
from jax import lax
from jax.experimental import pallas as pl
from jax.experimental.pallas import tpu as pltpu
from jax.sharding import PartitionSpec as P

HEAD_DIM = 64
LANES = 128
GRID_COLS = 96
EPS = 1e-06
BF16 = jnp.bfloat16
F32 = jnp.float32
MIB = 1024 * 1024


def specs(count):
    return [pl.BlockSpec(memory_space=pltpu.VMEM)] * count


def nbytes(*arrays):
    return sum(math.prod(a.shape) * jnp.dtype(a.dtype).itemsize for a in arrays)


def call(kernel, outs, args, scratch=(), flops=0, exps=0, limit=24):
    outs = tuple(jax.ShapeDtypeStruct(shape, dtype) for shape, dtype in outs)
    return pl.pallas_call(
        kernel,
        out_shape=outs,
        in_specs=specs(len(args)),
        out_specs=tuple(specs(len(outs))),
        scratch_shapes=list(scratch),
        compiler_params=pltpu.CompilerParams(vmem_limit_bytes=limit * MIB),
        cost_estimate=pl.CostEstimate(
            flops=flops, transcendentals=exps, bytes_accessed=nbytes(*args, *outs)
        ),
    )(*args)


def layer_norm(values_in, gain_row):
    mean_row = jnp.mean(values_in, axis=-1, keepdims=True)
    centred = values_in - mean_row
    spread = jnp.mean(centred * centred, axis=-1, keepdims=True)
    return centred * lax.rsqrt(spread + EPS) * gain_row


def dot(a, b):
    return jnp.dot(a, b, preferred_element_type=F32)


def low_lanes(shape):
    return lax.broadcasted_iota(jnp.int32, shape, len(shape) - 1) % LANES < HEAD_DIM


def normalize(mine_ref, other_ref, gain_ref):
    half = mine_ref.shape[1]
    width = 2 * half
    mine, other = mine_ref[...], other_ref[...]
    mean = (
        jnp.sum(mine, axis=-1, keepdims=True) + jnp.sum(other, axis=-1, keepdims=True)
    ) / width
    mine, other = mine - mean, other - mean
    spread = (
        jnp.sum(mine * mine, axis=-1, keepdims=True)
        + jnp.sum(other * other, axis=-1, keepdims=True)
    ) / width
    scale = lax.rsqrt(spread + EPS)
    low_gain, high_gain = gain_ref[:half][None, :], gain_ref[half:][None, :]
    first = lax.axis_index("head") == 0
    mine = (mine * scale * jnp.where(first, low_gain, high_gain)).astype(BF16)
    other = (other * scale * jnp.where(first, high_gain, low_gain)).astype(BF16)
    return mine, other


def intake_kernel(tokens_ref, gain_ref, tokens_out, gain_out):
    tokens_out[...] = tokens_ref[...]
    gain_out[...] = gain_ref[...]


def norm_kernel(mine_ref, other_ref, gain_ref, mine_out, other_out):
    mine_out[...], other_out[...] = normalize(mine_ref, other_ref, gain_ref)


def project(mine, other, weight_ref, part):
    core = lax.axis_index("head")
    half = mine.shape[1]
    mine_at = pl.ds(pl.multiple_of(core * half, half), half)
    other_at = pl.ds(pl.multiple_of((1 - core) * half, half), half)
    return (
        dot(mine, weight_ref[part, mine_at, :]) + dot(other, weight_ref[part, other_at, :])
    ).astype(BF16)


def plain_qkv_kernel(mine_ref, other_ref, gain_ref, weight_ref, *out_refs):
    mine, other = normalize(mine_ref, other_ref, gain_ref)
    for part, ref in enumerate(out_refs):
        ref[...] = project(mine, other, weight_ref, part)


def spread_lanes(column, width=LANES):
    return jnp.broadcast_to(column, (column.shape[0], width))


def across(lanes, width):
    whole, rest = divmod(width, LANES)
    return jnp.concatenate([lanes] * whole + ([lanes[:, :rest]] if rest else []), axis=1)


def absorb(pair, queries, keys, values, old):
    factor = HEAD_DIM ** (-0.5) * math.log2(math.e)
    cols = slice(pair * LANES, (pair + 1) * LANES)
    scores = lax.dot_general(
        queries, keys[:, cols], (((1,), (1,)), ((), ())), preferred_element_type=F32
    )
    top = spread_lanes(jnp.max(scores, axis=-1, keepdims=True))
    if old is not None:
        old_top, old_total, old_mixed = old
        top = jnp.maximum(top, old_top)
    weights = jnp.exp2((scores - across(top, scores.shape[1])) * factor)
    total = spread_lanes(jnp.sum(weights, axis=-1, keepdims=True))
    mixed = dot(weights.astype(BF16), values[:, cols])
    rows = mixed.shape[0] // 2
    low = low_lanes((rows, LANES))
    mixed = jnp.where(low, mixed[:rows], mixed[rows:])
    if old is not None:
        shrink = jnp.exp2((old_top - top) * factor)
        total = total + old_total * shrink
        mixed = mixed + old_mixed * jnp.where(low, shrink[:rows], shrink[rows:])
    return top, total, mixed


def own_kernel(
    mine_ref, other_ref, weight_ref, query_ref, top_ref, total_ref, mixed_ref
):
    mine, other = mine_ref[...], other_ref[...]
    rows = mine.shape[0]
    queries = project(mine, other, weight_ref, 0)
    keys = project(mine, other, weight_ref, 1)
    values = project(mine, other, weight_ref, 2)
    low = low_lanes((rows, LANES))
    for pair in range(query_ref.shape[0]):
        tile = queries[:, pair * LANES : (pair + 1) * LANES]
        query_ref[pair, :rows] = jnp.where(low, tile, jnp.zeros_like(tile))
        query_ref[pair, rows:] = jnp.where(low, jnp.zeros_like(tile), tile)
        top_ref[pair], total_ref[pair], mixed_ref[pair] = absorb(
            pair, query_ref[pair], keys, values, None
        )


def absorb_blocks(mine_refs, other_refs, weight_ref, query_ref, top_ref, total_ref, mixed_ref):
    mine = jnp.concatenate([ref[...] for ref in mine_refs], axis=0)
    other = jnp.concatenate([ref[...] for ref in other_refs], axis=0)
    keys = project(mine, other, weight_ref, 1)
    values = project(mine, other, weight_ref, 2)
    for pair in range(query_ref.shape[0]):
        old = top_ref[pair], total_ref[pair], mixed_ref[pair]
        yield pair, absorb(pair, query_ref[pair], keys, values, old)


def mark_kernel(block_ref, mark_ref):
    mark_ref[...] = block_ref[: mark_ref.shape[0], : mark_ref.shape[1]]


def step_kernel(
    mine_a,
    mine_b,
    other_a,
    other_b,
    weight_ref,
    query_ref,
    top_ref,
    total_ref,
    mixed_ref,
    mark_ref,
    top_out,
    total_out,
    mixed_out,
):
    for pair, state in absorb_blocks(
        (mine_a, mine_b), (other_a, other_b), weight_ref, query_ref, top_ref, total_ref, mixed_ref
    ):
        top_out[pair], total_out[pair], mixed_out[pair] = state


def out_terms(attended, weight_ref, mine_ref, other_ref, send_ref, keep_ref, full_ref):
    core = lax.axis_index("head")
    window = send_ref.shape[1]
    half = mine_ref.shape[1]
    shift = GRID_COLS - window
    full_ref[...] = dot(attended, weight_ref[...])
    for row in range(send_ref.shape[0]):
        there = pl.ds(pl.multiple_of(row * GRID_COLS + (1 - core) * shift, 8), window)
        send_ref[row] = full_ref[there, :].astype(BF16)
        here = pl.ds(pl.multiple_of(row * GRID_COLS + core * shift, 8), window)
        for part, ref in ((core, mine_ref), (1 - core, other_ref)):
            cols = pl.ds(pl.multiple_of(part * half, half), half)
            keep_ref[row, :, cols] = full_ref[here, cols] + ref[here, :]


def last_kernel(
    mine_a,
    mine_b,
    other_a,
    other_b,
    weight_ref,
    query_ref,
    top_ref,
    total_ref,
    mixed_ref,
    out_weight_ref,
    tokens_ref,
    other_tokens_ref,
    send_ref,
    keep_ref,
    full_ref,
    att_ref,
):
    rows = mixed_ref.shape[1]
    low = low_lanes((rows, LANES))
    for pair, (_, total, mixed) in absorb_blocks(
        (mine_a, mine_b), (other_a, other_b), weight_ref, query_ref, top_ref, total_ref, mixed_ref
    ):
        cols = slice(pair * LANES, (pair + 1) * LANES)
        att_ref[:, cols] = (mixed / jnp.where(low, total[:rows], total[rows:])).astype(BF16)
    out_terms(
        att_ref[...], out_weight_ref, tokens_ref, other_tokens_ref, send_ref, keep_ref, full_ref
    )


def plain_out_kernel(att_ref, weight_ref, mine_ref, other_ref, send_ref, keep_ref, full_ref):
    out_terms(att_ref[...], weight_ref, mine_ref, other_ref, send_ref, keep_ref, full_ref)


def lateral_kernel(
    keep_ref, got_ref, lateral_ref, gain_ref, near_ref, far_ref, pool_ref, fine_ref
):
    odd = lax.axis_index("blk") % 2
    window, features = keep_ref.shape[1], keep_ref.shape[2]
    cells = (keep_ref[...] + got_ref[...].astype(F32)).astype(BF16)
    fine_ref[...] = layer_norm(
        dot(cells.reshape(2 * window, features), lateral_ref[0]), gain_ref[0, 0][None, :]
    ).astype(BF16)
    near_ref[:window] = fine_ref[pl.ds(pl.multiple_of((1 - odd) * window, window), window), :]
    far_ref[:window] = fine_ref[pl.ds(pl.multiple_of(odd * window, window), window), :]
    tall = jnp.maximum(cells[0].astype(F32), cells[1].astype(F32))
    pooled = []
    for part in range(features // LANES):
        pool_ref[part] = tall[:, part * LANES : (part + 1) * LANES]
        even = pool_ref[part, pl.ds(0, window // 2, stride=2), :]
        odd = pool_ref[part, pl.ds(1, window // 2, stride=2), :]
        pooled.append(jnp.maximum(even, odd).astype(BF16))
    pooled = jnp.concatenate(pooled, axis=1)
    coarse = layer_norm(dot(pooled, lateral_ref[1]), gain_ref[1, 0][None, :]).astype(BF16)
    near_ref[window:] = coarse
    far_ref[window:] = coarse


def conv_level(stacked_ref, weight_ref, level, rows, window, sum_ref):
    block = rows * window
    place = lax.broadcasted_iota(jnp.int32, (block, weight_ref.shape[-1]), 0) % window
    taps = []
    for tap_col in range(3):
        total = None
        for tap_row in range(3):
            term = dot(
                stacked_ref[tap_row * window : tap_row * window + block],
                weight_ref[level, tap_row, tap_col],
            )
            total = term if total is None else total + term
        taps.append(total)
    left = jnp.where(place == 0, 0.0, pltpu.roll(taps[0], 1, axis=0))
    right = jnp.where(place == window - 1, 0.0, pltpu.roll(taps[2], block - 1, axis=0))
    sum_ref[...] = left + taps[1] + right


def conv_kernel(
    near_ref,
    far_ref,
    got_near_ref,
    got_far_ref,
    weight_ref,
    gain_ref,
    fine_ref,
    coarse_ref,
    fine_in,
    coarse_in,
    fine_sum,
    coarse_sum,
):
    core = lax.axis_index("head")
    odd = lax.axis_index("blk") % 2
    window = fine_sum.shape[0] // 2
    half = window // 2
    for ref, place in (
        (near_ref, 2 - odd),
        (far_ref, 1 + odd),
        (got_near_ref, 3 - 3 * odd),
        (got_far_ref, 3 * odd),
    ):
        fine_in[pl.ds(pl.multiple_of(place * window, window), window), :] = ref[:window]
    coarse_in[half : 2 * half] = near_ref[window:]
    for ref, place in ((got_near_ref, 2 - 2 * odd), (got_far_ref, 2 * odd)):
        coarse_in[pl.ds(pl.multiple_of(place * half, half), half), :] = ref[window:]
    conv_level(fine_in, weight_ref, 0, 2, window, fine_sum)
    conv_level(coarse_in, weight_ref, 1, 1, half, coarse_sum)
    cols = fine_ref.shape[1]
    shift = GRID_COLS - window
    inset = cols - shift
    for row in range(2):
        here = pl.ds(pl.multiple_of(row * window + core * inset, 8), cols)
        fine_ref[row] = layer_norm(fine_sum[here, :], gain_ref[0, 1][None, :]).astype(BF16)
    here = pl.ds(pl.multiple_of(core * (inset // 2), 8), cols // 2)
    coarse_ref[0] = layer_norm(coarse_sum[here, :], gain_ref[1, 1][None, :]).astype(BF16)


def attend_shared(queries, keys, values):
    factor = HEAD_DIM ** (-0.5)
    step = math.gcd(keys.shape[0], 1536)
    rows = queries.shape[0]

    def block(state, pair):
        running, totals, weighted = state
        key, value = pair
        scores = (
            lax.dot_general(queries, key, (((1,), (1,)), ((), ())), preferred_element_type=F32)
            * factor
        )
        newmax = jnp.maximum(running, jnp.max(scores, axis=-1, keepdims=True))
        weights = jnp.exp(scores - newmax)
        shrink = jnp.exp(running - newmax)
        totals = totals * shrink + jnp.sum(weights, axis=-1, keepdims=True)
        weighted = weighted * shrink + dot(weights.astype(BF16), value)
        return (newmax, totals, weighted), None

    state = (
        jnp.full((rows, 1), -jnp.inf, F32),
        jnp.zeros((rows, 1), F32),
        jnp.zeros((rows, HEAD_DIM), F32),
    )
    state, _ = lax.scan(
        block, state, (keys.reshape(-1, step, HEAD_DIM), values.reshape(-1, step, HEAD_DIM))
    )
    return (state[2] / state[1]).astype(BF16)


def exchange(value):
    return lax.all_to_all(value, "blk", split_axis=0, concat_axis=0, tiled=True)


def attention_shared(mine, other, norm_gain, qkv_weight, slices):
    rows = mine.shape[0]
    width = qkv_weight.shape[2]
    heads = width // HEAD_DIM
    blocks = heads * slices
    share = rows // slices
    queries, keys, values = call(
        plain_qkv_kernel, [((rows, width), BF16)] * 3, (mine, other, norm_gain, qkv_weight)
    )
    query_send = jnp.transpose(
        queries.reshape(slices, share, heads, HEAD_DIM), (2, 0, 1, 3)
    ).reshape(blocks, share * HEAD_DIM)
    pair = jnp.concatenate(
        (keys.reshape(rows, heads, HEAD_DIM), values.reshape(rows, heads, HEAD_DIM)), axis=2
    )
    pair = jnp.transpose(pair, (1, 0, 2))
    pair_send = jnp.broadcast_to(pair[:, None], (heads, slices, rows, 2 * HEAD_DIM)).reshape(
        blocks, rows, 2 * HEAD_DIM
    )
    query_got = exchange(query_send).reshape(blocks * share, HEAD_DIM)
    pair_got = exchange(pair_send).reshape(blocks * rows, 2 * HEAD_DIM)
    one_head = attend_shared(query_got, pair_got[:, :HEAD_DIM], pair_got[:, HEAD_DIM:])
    back = exchange(one_head.reshape(blocks, share * HEAD_DIM))
    return jnp.transpose(back.reshape(heads, slices, share, HEAD_DIM), (1, 2, 0, 3)).reshape(
        rows, width
    )


def body(tokens, norm_gain, qkv_weight, out_weight, lateral_weight, conv_weight, level_gains):
    rows, half = tokens.shape
    features = out_weight.shape[1]
    width = qkv_weight.shape[2]
    heads = width // HEAD_DIM
    blocks = lax.axis_size("blk")
    cores = lax.axis_size("head")
    grid_rows = rows // GRID_COLS
    cols = GRID_COLS // cores
    channels = lateral_weight.shape[2]
    window = 2 * GRID_COLS // 3
    swap = [(i, cores - 1 - i) for i in range(cores)]

    other = lax.ppermute(tokens, "head", swap)
    tokens, norm_gain = call(
        intake_kernel,
        [(tokens.shape, F32), (norm_gain.shape, F32)],
        (tokens, norm_gain),
        flops=MIB * 1024,
    )
    other, tokens, norm_gain = lax.optimization_barrier((other, tokens, norm_gain))
    tail = (out_weight, tokens, other)
    tail_outs = [
        ((grid_rows, window, features), BF16),
        ((grid_rows, window, features), F32),
    ]
    full = pltpu.VMEM((rows, features), F32)
    out_flops = 2 * rows * width * features
    if blocks <= heads:
        order = list(range(0, blocks, 2)) + list(range(blocks - 1, 0, -2))
        forth = [(order[i - 1], order[i]) for i in range(blocks)]
        back = [(target, source) for source, target in forth]
        mine, across_core = call(
            norm_kernel, [((rows, half), BF16)] * 2, (tokens, other, norm_gain)
        )
        pairs = width // LANES
        state_outs = [
            ((pairs, 2 * rows, LANES), F32),
            ((pairs, 2 * rows, LANES), F32),
            ((pairs, rows, LANES), F32),
        ]
        ahead = lax.ppermute(mine, "blk", forth)
        behind = lax.ppermute(mine, "blk", back)
        unit = 4 * rows * width * (features + rows)
        queries, *state = call(
            own_kernel,
            [((pairs, 2 * rows, LANES), BF16)] + state_outs,
            (mine, across_core, qkv_weight),
            flops=unit + 2 * rows * width * features,
            exps=heads * rows * rows,
        )
        for step in range(1, blocks // 2):
            ahead, state[0] = lax.optimization_barrier((ahead, state[0]))
            behind, state[0] = lax.optimization_barrier((behind, state[0]))
            parts = (ahead, behind)
            (mark,) = call(mark_kernel, [((16, LANES), BF16)], (ahead,))
            if step == blocks // 2 - 1:
                ahead, behind = ahead[: rows // 2], behind[rows // 2 :]
            ahead = lax.ppermute(ahead, "blk", forth)
            behind = lax.ppermute(behind, "blk", back)
            others = (lax.ppermute(parts[0], "head", swap), lax.ppermute(parts[1], "head", swap))
            state = call(
                step_kernel,
                state_outs,
                parts + others + (qkv_weight, queries) + tuple(state) + (mark,),
                flops=2 * unit,
                exps=2 * heads * rows * rows,
            )
            state = list(state)
        ahead, behind, state = lax.optimization_barrier((ahead, behind, state))
        parts = (ahead, behind)
        others = tuple(lax.ppermute(part, "head", swap) for part in parts)
        peer_term, keep = call(
            last_kernel,
            tail_outs,
            parts + others + (qkv_weight, queries) + tuple(state) + tail,
            [full, pltpu.VMEM((rows, width), BF16)],
            flops=unit + out_flops,
            exps=heads * rows * rows,
        )
    else:
        attended = attention_shared(
            tokens, other, norm_gain, qkv_weight, blocks // heads
        )
        peer_term, keep = call(plain_out_kernel, tail_outs, (attended,) + tail, [full], out_flops)
    peer_term = lax.ppermute(peer_term, "head", swap)

    message = (window + window // 2, channels)
    near, far = call(
        lateral_kernel,
        [(message, BF16), (message, BF16)],
        (keep, peer_term, lateral_weight, level_gains),
        [
            pltpu.VMEM((features // LANES, window, LANES), F32),
            pltpu.VMEM((2 * window, channels), BF16),
        ],
        flops=5 * window * features * channels,
    )
    far_pairs = [(i, i + 1) for i in range(1, blocks - 1, 2)]
    far_pairs += [(j, i) for i, j in far_pairs]
    got_far = lax.ppermute(far, "blk", far_pairs)
    got_near = lax.ppermute(near, "blk", [(i, i ^ 1) for i in range(blocks)])
    return call(
        conv_kernel,
        [((grid_rows, cols, channels), BF16), ((grid_rows // 2, cols // 2, channels), BF16)],
        (near, far, got_near, got_far, conv_weight, level_gains),
        [
            pltpu.VMEM((4 * window, channels), BF16),
            pltpu.VMEM((3 * window // 2, channels), BF16),
            pltpu.VMEM((2 * window, channels), F32),
            pltpu.VMEM((window // 2, channels), F32),
        ],
        flops=45 * window * channels * channels,
    )


def solution(mesh):
    in_specs = (
        P(("groups", "blk"), "head"),
        P(),
        P(None, None, "head"),
        P("head", None),
        P(),
        P(),
        P(),
    )
    out_specs = (P(("groups", "blk"), "head", None), P(("groups", "blk"), "head", None))
    return jax.shard_map(body, mesh=mesh, in_specs=in_specs, out_specs=out_specs, check_vma=False)
```

```python
import math

import jax
import jax.numpy as jnp
from jax import lax
from jax.experimental import pallas as pl
from jax.experimental.pallas import tpu as pltpu
from jax.sharding import PartitionSpec as P

HEAD_DIM = 64
LANES = 128
GRID_COLS = 96
EPS = 1e-06
BF16 = jnp.bfloat16
F32 = jnp.float32
MIB = 1024 * 1024


def specs(count):
    return [pl.BlockSpec(memory_space=pltpu.VMEM)] * count


def nbytes(*arrays):
    return sum(math.prod(a.shape) * jnp.dtype(a.dtype).itemsize for a in arrays)


def call(kernel, outs, args, scratch=(), flops=0, exps=0, limit=24):
    outs = tuple(jax.ShapeDtypeStruct(shape, dtype) for shape, dtype in outs)
    return pl.pallas_call(
        kernel,
        out_shape=outs,
        in_specs=specs(len(args)),
        out_specs=tuple(specs(len(outs))),
        scratch_shapes=list(scratch),
        compiler_params=pltpu.CompilerParams(vmem_limit_bytes=limit * MIB),
        cost_estimate=pl.CostEstimate(
            flops=flops, transcendentals=exps, bytes_accessed=nbytes(*args, *outs)
        ),
    )(*args)


def layer_norm(values_in, gain_row):
    mean_row = jnp.mean(values_in, axis=-1, keepdims=True)
    centred = values_in - mean_row
    spread = jnp.mean(centred * centred, axis=-1, keepdims=True)
    return centred * lax.rsqrt(spread + EPS) * gain_row


def dot(a, b):
    return jnp.dot(a, b, preferred_element_type=F32)


def low_lanes(shape):
    return lax.broadcasted_iota(jnp.int32, shape, len(shape) - 1) % LANES < HEAD_DIM


def normalize(mine_ref, other_ref, gain_ref):
    half = mine_ref.shape[1]
    width = 2 * half
    mine, other = mine_ref[...], other_ref[...]
    mean = (
        jnp.sum(mine, axis=-1, keepdims=True) + jnp.sum(other, axis=-1, keepdims=True)
    ) / width
    mine, other = mine - mean, other - mean
    spread = (
        jnp.sum(mine * mine, axis=-1, keepdims=True)
        + jnp.sum(other * other, axis=-1, keepdims=True)
    ) / width
    scale = lax.rsqrt(spread + EPS)
    low_gain, high_gain = gain_ref[:half][None, :], gain_ref[half:][None, :]
    first = lax.axis_index("head") == 0
    mine = (mine * scale * jnp.where(first, low_gain, high_gain)).astype(BF16)
    other = (other * scale * jnp.where(first, high_gain, low_gain)).astype(BF16)
    return mine, other


def intake_kernel(tokens_ref, tokens_out):
    tokens_out[...] = tokens_ref[...]


def norm_kernel(mine_ref, other_ref, gain_ref, mine_out, other_out):
    mine_out[...], other_out[...] = normalize(mine_ref, other_ref, gain_ref)


def project(mine, other, weight_ref, part):
    core = lax.axis_index("head")
    half = mine.shape[1]
    mine_at = pl.ds(pl.multiple_of(core * half, half), half)
    other_at = pl.ds(pl.multiple_of((1 - core) * half, half), half)
    return (
        dot(mine, weight_ref[part, mine_at, :]) + dot(other, weight_ref[part, other_at, :])
    ).astype(BF16)


def plain_qkv_kernel(mine_ref, other_ref, gain_ref, weight_ref, *out_refs):
    mine, other = normalize(mine_ref, other_ref, gain_ref)
    for part, ref in enumerate(out_refs):
        ref[...] = project(mine, other, weight_ref, part)


def spread_lanes(column, width=LANES):
    return jnp.broadcast_to(column, (column.shape[0], width))


def across(lanes, width):
    whole, rest = divmod(width, LANES)
    return jnp.concatenate([lanes] * whole + ([lanes[:, :rest]] if rest else []), axis=1)


def absorb(pair, queries, keys, values, old):
    factor = HEAD_DIM ** (-0.5) * math.log2(math.e)
    cols = slice(pair * LANES, (pair + 1) * LANES)
    scores = lax.dot_general(
        queries, keys[:, cols], (((1,), (1,)), ((), ())), preferred_element_type=F32
    )
    top = spread_lanes(jnp.max(scores, axis=-1, keepdims=True))
    if old is not None:
        old_top, old_total, old_mixed = old
        top = jnp.maximum(top, old_top)
    weights = jnp.exp2((scores - across(top, scores.shape[1])) * factor)
    total = spread_lanes(jnp.sum(weights, axis=-1, keepdims=True))
    mixed = dot(weights.astype(BF16), values[:, cols])
    rows = mixed.shape[0] // 2
    low = low_lanes((rows, LANES))
    mixed = jnp.where(low, mixed[:rows], mixed[rows:])
    if old is not None:
        shrink = jnp.exp2((old_top - top) * factor)
        total = total + old_total * shrink
        mixed = mixed + old_mixed * jnp.where(low, shrink[:rows], shrink[rows:])
    return top, total, mixed


def own_kernel(
    mine_ref, other_ref, weight_ref, query_ref, top_ref, total_ref, mixed_ref
):
    mine, other = mine_ref[...], other_ref[...]
    rows = mine.shape[0]
    queries = project(mine, other, weight_ref, 0)
    keys = project(mine, other, weight_ref, 1)
    values = project(mine, other, weight_ref, 2)
    low = low_lanes((rows, LANES))
    for pair in range(query_ref.shape[0]):
        tile = queries[:, pair * LANES : (pair + 1) * LANES]
        query_ref[pair, :rows] = jnp.where(low, tile, jnp.zeros_like(tile))
        query_ref[pair, rows:] = jnp.where(low, jnp.zeros_like(tile), tile)
        top_ref[pair], total_ref[pair], mixed_ref[pair] = absorb(
            pair, query_ref[pair], keys, values, None
        )


def absorb_blocks(mine_refs, other_refs, weight_ref, query_ref, top_ref, total_ref, mixed_ref):
    mine = jnp.concatenate([ref[...] for ref in mine_refs], axis=0)
    other = jnp.concatenate([ref[...] for ref in other_refs], axis=0)
    keys = project(mine, other, weight_ref, 1)
    values = project(mine, other, weight_ref, 2)
    for pair in range(query_ref.shape[0]):
        old = top_ref[pair], total_ref[pair], mixed_ref[pair]
        yield pair, absorb(pair, query_ref[pair], keys, values, old)


def mark_kernel(block_ref, mark_ref):
    mark_ref[...] = block_ref[: mark_ref.shape[0], : mark_ref.shape[1]]


def step_kernel(
    mine_ref,
    other_ref,
    weight_ref,
    query_ref,
    top_ref,
    total_ref,
    mixed_ref,
    mark_ref,
    top_out,
    total_out,
    mixed_out,
):
    for pair, state in absorb_blocks(
        (mine_ref,), (other_ref,), weight_ref, query_ref, top_ref, total_ref, mixed_ref
    ):
        top_out[pair], total_out[pair], mixed_out[pair] = state


def out_terms(attended, weight_ref, mine_ref, other_ref, send_ref, keep_ref, full_ref):
    core = lax.axis_index("head")
    window = send_ref.shape[1]
    half = mine_ref.shape[1]
    shift = GRID_COLS - window
    full_ref[...] = dot(attended, weight_ref[...])
    for row in range(send_ref.shape[0]):
        there = pl.ds(pl.multiple_of(row * GRID_COLS + (1 - core) * shift, 8), window)
        send_ref[row] = full_ref[there, :].astype(BF16)
        here = pl.ds(pl.multiple_of(row * GRID_COLS + core * shift, 8), window)
        for part, ref in ((core, mine_ref), (1 - core, other_ref)):
            cols = pl.ds(pl.multiple_of(part * half, half), half)
            keep_ref[row, :, cols] = full_ref[here, cols] + ref[here, :]


def last_kernel(
    mine_a,
    mine_b,
    other_a,
    other_b,
    weight_ref,
    query_ref,
    top_ref,
    total_ref,
    mixed_ref,
    out_weight_ref,
    tokens_ref,
    other_tokens_ref,
    send_ref,
    keep_ref,
    full_ref,
    att_ref,
):
    rows = mixed_ref.shape[1]
    low = low_lanes((rows, LANES))
    for pair, (_, total, mixed) in absorb_blocks(
        (mine_a, mine_b), (other_a, other_b), weight_ref, query_ref, top_ref, total_ref, mixed_ref
    ):
        cols = slice(pair * LANES, (pair + 1) * LANES)
        att_ref[:, cols] = (mixed / jnp.where(low, total[:rows], total[rows:])).astype(BF16)
    out_terms(
        att_ref[...], out_weight_ref, tokens_ref, other_tokens_ref, send_ref, keep_ref, full_ref
    )


def plain_out_kernel(att_ref, weight_ref, mine_ref, other_ref, send_ref, keep_ref, full_ref):
    out_terms(att_ref[...], weight_ref, mine_ref, other_ref, send_ref, keep_ref, full_ref)


def lateral_kernel(
    keep_ref, got_ref, lateral_ref, gain_ref, near_ref, far_ref, pool_ref, fine_ref
):
    odd = lax.axis_index("blk") % 2
    window, features = keep_ref.shape[1], keep_ref.shape[2]
    cells = (keep_ref[...] + got_ref[...].astype(F32)).astype(BF16)
    fine_ref[...] = layer_norm(
        dot(cells.reshape(2 * window, features), lateral_ref[0]), gain_ref[0, 0][None, :]
    ).astype(BF16)
    near_ref[:window] = fine_ref[pl.ds(pl.multiple_of((1 - odd) * window, window), window), :]
    far_ref[:window] = fine_ref[pl.ds(pl.multiple_of(odd * window, window), window), :]
    tall = jnp.maximum(cells[0].astype(F32), cells[1].astype(F32))
    pooled = []
    for part in range(features // LANES):
        pool_ref[part] = tall[:, part * LANES : (part + 1) * LANES]
        even = pool_ref[part, pl.ds(0, window // 2, stride=2), :]
        odd = pool_ref[part, pl.ds(1, window // 2, stride=2), :]
        pooled.append(jnp.maximum(even, odd).astype(BF16))
    pooled = jnp.concatenate(pooled, axis=1)
    coarse = layer_norm(dot(pooled, lateral_ref[1]), gain_ref[1, 0][None, :]).astype(BF16)
    near_ref[window:] = coarse
    far_ref[window:] = coarse


def conv_level(stacked_ref, weight_ref, level, rows, window, sum_ref):
    block = rows * window
    place = lax.broadcasted_iota(jnp.int32, (block, weight_ref.shape[-1]), 0) % window
    taps = []
    for tap_col in range(3):
        total = None
        for tap_row in range(3):
            term = dot(
                stacked_ref[tap_row * window : tap_row * window + block],
                weight_ref[level, tap_row, tap_col],
            )
            total = term if total is None else total + term
        taps.append(total)
    left = jnp.where(place == 0, 0.0, pltpu.roll(taps[0], 1, axis=0))
    right = jnp.where(place == window - 1, 0.0, pltpu.roll(taps[2], block - 1, axis=0))
    sum_ref[...] = left + taps[1] + right


def conv_kernel(
    near_ref,
    far_ref,
    got_near_ref,
    got_far_ref,
    weight_ref,
    gain_ref,
    fine_ref,
    coarse_ref,
    fine_in,
    coarse_in,
    fine_sum,
    coarse_sum,
):
    core = lax.axis_index("head")
    odd = lax.axis_index("blk") % 2
    window = fine_sum.shape[0] // 2
    half = window // 2
    for ref, place in (
        (near_ref, 2 - odd),
        (far_ref, 1 + odd),
        (got_near_ref, 3 - 3 * odd),
        (got_far_ref, 3 * odd),
    ):
        fine_in[pl.ds(pl.multiple_of(place * window, window), window), :] = ref[:window]
    coarse_in[half : 2 * half] = near_ref[window:]
    for ref, place in ((got_near_ref, 2 - 2 * odd), (got_far_ref, 2 * odd)):
        coarse_in[pl.ds(pl.multiple_of(place * half, half), half), :] = ref[window:]
    conv_level(fine_in, weight_ref, 0, 2, window, fine_sum)
    conv_level(coarse_in, weight_ref, 1, 1, half, coarse_sum)
    cols = fine_ref.shape[1]
    shift = GRID_COLS - window
    inset = cols - shift
    for row in range(2):
        here = pl.ds(pl.multiple_of(row * window + core * inset, 8), cols)
        fine_ref[row] = layer_norm(fine_sum[here, :], gain_ref[0, 1][None, :]).astype(BF16)
    here = pl.ds(pl.multiple_of(core * (inset // 2), 8), cols // 2)
    coarse_ref[0] = layer_norm(coarse_sum[here, :], gain_ref[1, 1][None, :]).astype(BF16)


def attend_shared(queries, keys, values):
    factor = HEAD_DIM ** (-0.5)
    step = math.gcd(keys.shape[0], 1536)
    rows = queries.shape[0]

    def block(state, pair):
        running, totals, weighted = state
        key, value = pair
        scores = (
            lax.dot_general(queries, key, (((1,), (1,)), ((), ())), preferred_element_type=F32)
            * factor
        )
        newmax = jnp.maximum(running, jnp.max(scores, axis=-1, keepdims=True))
        weights = jnp.exp(scores - newmax)
        shrink = jnp.exp(running - newmax)
        totals = totals * shrink + jnp.sum(weights, axis=-1, keepdims=True)
        weighted = weighted * shrink + dot(weights.astype(BF16), value)
        return (newmax, totals, weighted), None

    state = (
        jnp.full((rows, 1), -jnp.inf, F32),
        jnp.zeros((rows, 1), F32),
        jnp.zeros((rows, HEAD_DIM), F32),
    )
    state, _ = lax.scan(
        block, state, (keys.reshape(-1, step, HEAD_DIM), values.reshape(-1, step, HEAD_DIM))
    )
    return (state[2] / state[1]).astype(BF16)


def exchange(value):
    return lax.all_to_all(value, "blk", split_axis=0, concat_axis=0, tiled=True)


def attention_shared(mine, other, norm_gain, qkv_weight, slices):
    rows = mine.shape[0]
    width = qkv_weight.shape[2]
    heads = width // HEAD_DIM
    blocks = heads * slices
    share = rows // slices
    queries, keys, values = call(
        plain_qkv_kernel, [((rows, width), BF16)] * 3, (mine, other, norm_gain, qkv_weight)
    )
    query_send = jnp.transpose(
        queries.reshape(slices, share, heads, HEAD_DIM), (2, 0, 1, 3)
    ).reshape(blocks, share * HEAD_DIM)
    pair = jnp.concatenate(
        (keys.reshape(rows, heads, HEAD_DIM), values.reshape(rows, heads, HEAD_DIM)), axis=2
    )
    pair = jnp.transpose(pair, (1, 0, 2))
    pair_send = jnp.broadcast_to(pair[:, None], (heads, slices, rows, 2 * HEAD_DIM)).reshape(
        blocks, rows, 2 * HEAD_DIM
    )
    query_got = exchange(query_send).reshape(blocks * share, HEAD_DIM)
    pair_got = exchange(pair_send).reshape(blocks * rows, 2 * HEAD_DIM)
    one_head = attend_shared(query_got, pair_got[:, :HEAD_DIM], pair_got[:, HEAD_DIM:])
    back = exchange(one_head.reshape(blocks, share * HEAD_DIM))
    return jnp.transpose(back.reshape(heads, slices, share, HEAD_DIM), (1, 2, 0, 3)).reshape(
        rows, width
    )


def body(tokens, norm_gain, qkv_weight, out_weight, lateral_weight, conv_weight, level_gains):
    rows, half = tokens.shape
    features = out_weight.shape[1]
    width = qkv_weight.shape[2]
    heads = width // HEAD_DIM
    blocks = lax.axis_size("blk")
    cores = lax.axis_size("head")
    grid_rows = rows // GRID_COLS
    cols = GRID_COLS // cores
    channels = lateral_weight.shape[2]
    window = 2 * GRID_COLS // 3
    swap = [(i, cores - 1 - i) for i in range(cores)]

    other = lax.ppermute(tokens, "head", swap)
    (tokens,) = call(intake_kernel, [(tokens.shape, F32)], (tokens,), flops=MIB * 1024)
    other, tokens = lax.optimization_barrier((other, tokens))
    tail = (out_weight, tokens, other)
    tail_outs = [
        ((grid_rows, window, features), BF16),
        ((grid_rows, window, features), F32),
    ]
    full = pltpu.VMEM((rows, features), F32)
    out_flops = 2 * rows * width * features
    if blocks <= heads:
        order = list(range(0, blocks, 2)) + list(range(blocks - 1, 0, -2))
        forth = [(order[i - 1], order[i]) for i in range(blocks)]
        back = [(target, source) for source, target in forth]
        mine, across_core = call(
            norm_kernel, [((rows, half), BF16)] * 2, (tokens, other, norm_gain)
        )
        pairs = width // LANES
        state_outs = [
            ((pairs, 2 * rows, LANES), F32),
            ((pairs, 2 * rows, LANES), F32),
            ((pairs, rows, LANES), F32),
        ]
        ahead = lax.ppermute(mine, "blk", forth)
        behind = lax.ppermute(mine, "blk", back)
        unit = 4 * rows * width * (features + rows)
        queries, *state = call(
            own_kernel,
            [((pairs, 2 * rows, LANES), BF16)] + state_outs,
            (mine, across_core, qkv_weight),
            flops=unit + 2 * rows * width * features,
            exps=heads * rows * rows,
        )
        for step in range(1, blocks // 2):
            ahead, state[0] = lax.optimization_barrier((ahead, state[0]))
            behind, state[0] = lax.optimization_barrier((behind, state[0]))
            parts = (ahead, behind)
            (mark,) = call(mark_kernel, [((16, LANES), BF16)], (ahead,))
            if step == blocks // 2 - 1:
                ahead, behind = ahead[: rows // 2], behind[rows // 2 :]
            ahead = lax.ppermute(ahead, "blk", forth)
            behind = lax.ppermute(behind, "blk", back)
            others = (lax.ppermute(parts[0], "head", swap), lax.ppermute(parts[1], "head", swap))
            for block in zip(parts, others):
                state = call(
                    step_kernel,
                    state_outs,
                    block + (qkv_weight, queries) + tuple(state) + (mark,),
                    flops=unit,
                    exps=heads * rows * rows,
                )
            state = list(state)
        ahead, behind, state = lax.optimization_barrier((ahead, behind, state))
        parts = (ahead, behind)
        others = tuple(lax.ppermute(part, "head", swap) for part in parts)
        peer_term, keep = call(
            last_kernel,
            tail_outs,
            parts + others + (qkv_weight, queries) + tuple(state) + tail,
            [full, pltpu.VMEM((rows, width), BF16)],
            flops=unit + out_flops,
            exps=heads * rows * rows,
        )
    else:
        attended = attention_shared(
            tokens, other, norm_gain, qkv_weight, blocks // heads
        )
        peer_term, keep = call(plain_out_kernel, tail_outs, (attended,) + tail, [full], out_flops)
    peer_term = lax.ppermute(peer_term, "head", swap)

    message = (window + window // 2, channels)
    near, far = call(
        lateral_kernel,
        [(message, BF16), (message, BF16)],
        (keep, peer_term, lateral_weight, level_gains),
        [
            pltpu.VMEM((features // LANES, window, LANES), F32),
            pltpu.VMEM((2 * window, channels), BF16),
        ],
        flops=5 * window * features * channels,
    )
    far_pairs = [(i, i + 1) for i in range(1, blocks - 1, 2)]
    far_pairs += [(j, i) for i, j in far_pairs]
    got_far = lax.ppermute(far, "blk", far_pairs)
    got_near = lax.ppermute(near, "blk", [(i, i ^ 1) for i in range(blocks)])
    return call(
        conv_kernel,
        [((grid_rows, cols, channels), BF16), ((grid_rows // 2, cols // 2, channels), BF16)],
        (near, far, got_near, got_far, conv_weight, level_gains),
        [
            pltpu.VMEM((4 * window, channels), BF16),
            pltpu.VMEM((3 * window // 2, channels), BF16),
            pltpu.VMEM((2 * window, channels), F32),
            pltpu.VMEM((window // 2, channels), F32),
        ],
        flops=45 * window * channels * channels,
    )


def solution(mesh):
    in_specs = (
        P(("groups", "blk"), "head"),
        P(),
        P(None, None, "head"),
        P("head", None),
        P(),
        P(),
        P(),
    )
    out_specs = (P(("groups", "blk"), "head", None), P(("groups", "blk"), "head", None))
    return jax.shard_map(body, mesh=mesh, in_specs=in_specs, out_specs=out_specs, check_vma=False)
```

```python
import math

import jax
import jax.numpy as jnp
from jax import lax
from jax.experimental import pallas as pl
from jax.experimental.pallas import tpu as pltpu
from jax.sharding import PartitionSpec as P

HEAD_DIM = 64
LANES = 128
GRID_COLS = 96
EPS = 1e-06
BF16 = jnp.bfloat16
F32 = jnp.float32
MIB = 1024 * 1024


def specs(count):
    return [pl.BlockSpec(memory_space=pltpu.VMEM)] * count


def nbytes(*arrays):
    return sum(math.prod(a.shape) * jnp.dtype(a.dtype).itemsize for a in arrays)


def call(kernel, outs, args, scratch=(), flops=0, exps=0, limit=24):
    outs = tuple(jax.ShapeDtypeStruct(shape, dtype) for shape, dtype in outs)
    return pl.pallas_call(
        kernel,
        out_shape=outs,
        in_specs=specs(len(args)),
        out_specs=tuple(specs(len(outs))),
        scratch_shapes=list(scratch),
        compiler_params=pltpu.CompilerParams(vmem_limit_bytes=limit * MIB),
        cost_estimate=pl.CostEstimate(
            flops=flops, transcendentals=exps, bytes_accessed=nbytes(*args, *outs)
        ),
    )(*args)


def layer_norm(values_in, gain_row):
    mean_row = jnp.mean(values_in, axis=-1, keepdims=True)
    centred = values_in - mean_row
    spread = jnp.mean(centred * centred, axis=-1, keepdims=True)
    return centred * lax.rsqrt(spread + EPS) * gain_row


def dot(a, b):
    return jnp.dot(a, b, preferred_element_type=F32)


def low_lanes(shape):
    return lax.broadcasted_iota(jnp.int32, shape, len(shape) - 1) % LANES < HEAD_DIM


def normalize(mine_ref, other_ref, gain_ref):
    half = mine_ref.shape[1]
    width = 2 * half
    mine, other = mine_ref[...], other_ref[...]
    mean = (
        jnp.sum(mine, axis=-1, keepdims=True) + jnp.sum(other, axis=-1, keepdims=True)
    ) / width
    mine, other = mine - mean, other - mean
    spread = (
        jnp.sum(mine * mine, axis=-1, keepdims=True)
        + jnp.sum(other * other, axis=-1, keepdims=True)
    ) / width
    scale = lax.rsqrt(spread + EPS)
    low_gain, high_gain = gain_ref[:half][None, :], gain_ref[half:][None, :]
    first = lax.axis_index("head") == 0
    mine = (mine * scale * jnp.where(first, low_gain, high_gain)).astype(BF16)
    other = (other * scale * jnp.where(first, high_gain, low_gain)).astype(BF16)
    return mine, other


def intake_kernel(tokens_ref, tokens_out):
    tokens_out[...] = tokens_ref[...]


def norm_kernel(mine_ref, other_ref, gain_ref, mine_out, other_out):
    mine_out[...], other_out[...] = normalize(mine_ref, other_ref, gain_ref)


def project(mine, other, weight_ref, part):
    core = lax.axis_index("head")
    half = mine.shape[1]
    mine_at = pl.ds(pl.multiple_of(core * half, half), half)
    other_at = pl.ds(pl.multiple_of((1 - core) * half, half), half)
    return (
        dot(mine, weight_ref[part, mine_at, :]) + dot(other, weight_ref[part, other_at, :])
    ).astype(BF16)


def plain_qkv_kernel(mine_ref, other_ref, gain_ref, weight_ref, *out_refs):
    mine, other = normalize(mine_ref, other_ref, gain_ref)
    for part, ref in enumerate(out_refs):
        ref[...] = project(mine, other, weight_ref, part)


def spread_lanes(column, width=LANES):
    return jnp.broadcast_to(column, (column.shape[0], width))


def across(lanes, width):
    whole, rest = divmod(width, LANES)
    return jnp.concatenate([lanes] * whole + ([lanes[:, :rest]] if rest else []), axis=1)


def absorb(pair, queries, keys, values, old):
    factor = HEAD_DIM ** (-0.5) * math.log2(math.e)
    cols = slice(pair * LANES, (pair + 1) * LANES)
    scores = lax.dot_general(
        queries, keys[:, cols], (((1,), (1,)), ((), ())), preferred_element_type=F32
    )
    top = spread_lanes(jnp.max(scores, axis=-1, keepdims=True))
    if old is not None:
        old_top, old_total, old_mixed = old
        top = jnp.maximum(top, old_top)
    weights = jnp.exp2((scores - across(top, scores.shape[1])) * factor)
    total = spread_lanes(jnp.sum(weights, axis=-1, keepdims=True))
    mixed = dot(weights.astype(BF16), values[:, cols])
    rows = mixed.shape[0] // 2
    low = low_lanes((rows, LANES))
    mixed = jnp.where(low, mixed[:rows], mixed[rows:])
    if old is not None:
        shrink = jnp.exp2((old_top - top) * factor)
        total = total + old_total * shrink
        mixed = mixed + old_mixed * jnp.where(low, shrink[:rows], shrink[rows:])
    return top, total, mixed


def own_kernel(
    mine_ref, other_ref, weight_ref, query_ref, top_ref, total_ref, mixed_ref
):
    mine, other = mine_ref[...], other_ref[...]
    rows = mine.shape[0]
    queries = project(mine, other, weight_ref, 0)
    keys = project(mine, other, weight_ref, 1)
    values = project(mine, other, weight_ref, 2)
    low = low_lanes((rows, LANES))
    for pair in range(query_ref.shape[0]):
        tile = queries[:, pair * LANES : (pair + 1) * LANES]
        query_ref[pair, :rows] = jnp.where(low, tile, jnp.zeros_like(tile))
        query_ref[pair, rows:] = jnp.where(low, jnp.zeros_like(tile), tile)
        top_ref[pair], total_ref[pair], mixed_ref[pair] = absorb(
            pair, query_ref[pair], keys, values, None
        )


def absorb_blocks(mine_refs, other_refs, weight_ref, query_ref, top_ref, total_ref, mixed_ref):
    mine = jnp.concatenate([ref[...] for ref in mine_refs], axis=0)
    other = jnp.concatenate([ref[...] for ref in other_refs], axis=0)
    keys = project(mine, other, weight_ref, 1)
    values = project(mine, other, weight_ref, 2)
    for pair in range(query_ref.shape[0]):
        old = top_ref[pair], total_ref[pair], mixed_ref[pair]
        yield pair, absorb(pair, query_ref[pair], keys, values, old)


def mark_kernel(block_ref, mark_ref):
    mark_ref[...] = block_ref[: mark_ref.shape[0], : mark_ref.shape[1]]


def step_kernel(
    mine_ref,
    other_ref,
    weight_ref,
    query_ref,
    top_ref,
    total_ref,
    mixed_ref,
    mark_ref,
    top_out,
    total_out,
    mixed_out,
):
    for pair, state in absorb_blocks(
        (mine_ref,), (other_ref,), weight_ref, query_ref, top_ref, total_ref, mixed_ref
    ):
        top_out[pair], total_out[pair], mixed_out[pair] = state


def send_terms(att_ref, weight_ref, send_ref):
    grid_rows, window = send_ref.shape[:2]
    shift = (1 - lax.axis_index("head")) * (GRID_COLS - window)
    cells = jnp.concatenate(
        [
            att_ref[pl.ds(pl.multiple_of(row * GRID_COLS + shift, 32), window), :]
            for row in range(grid_rows)
        ],
        axis=0,
    )
    send_ref[...] = dot(cells, weight_ref[...]).astype(BF16).reshape(send_ref.shape)


def keep_kernel(att_ref, weight_ref, mine_ref, other_ref, keep_ref, full_ref):
    core = lax.axis_index("head")
    grid_rows, window = keep_ref.shape[:2]
    half = mine_ref.shape[1]
    shift = core * (GRID_COLS - window)
    places = [
        pl.ds(pl.multiple_of(row * GRID_COLS + shift, 32), window) for row in range(grid_rows)
    ]
    cells = jnp.concatenate([att_ref[here, :] for here in places], axis=0)
    full_ref[...] = dot(cells, weight_ref[...])
    for row, here in enumerate(places):
        there = slice(row * window, (row + 1) * window)
        for part, ref in ((core, mine_ref), (1 - core, other_ref)):
            cols = pl.ds(pl.multiple_of(part * half, half), half)
            keep_ref[row, :, cols] = full_ref[there, cols] + ref[here, :]


def last_kernel(
    mine_ref,
    other_ref,
    weight_ref,
    query_ref,
    top_ref,
    total_ref,
    mixed_ref,
    out_weight_ref,
    send_ref,
    att_ref,
):
    rows = mixed_ref.shape[1]
    low = low_lanes((rows, LANES))
    for pair, (_, total, mixed) in absorb_blocks(
        (mine_ref,), (other_ref,), weight_ref, query_ref, top_ref, total_ref, mixed_ref
    ):
        cols = slice(pair * LANES, (pair + 1) * LANES)
        att_ref[:, cols] = (mixed / jnp.where(low, total[:rows], total[rows:])).astype(BF16)
    send_terms(att_ref, out_weight_ref, send_ref)


def plain_out_kernel(att_ref, weight_ref, send_ref):
    send_terms(att_ref, weight_ref, send_ref)


def lateral_kernel(
    keep_ref, got_ref, lateral_ref, gain_ref, near_ref, far_ref, pool_ref, fine_ref
):
    odd = lax.axis_index("blk") % 2
    window, features = keep_ref.shape[1], keep_ref.shape[2]
    cells = (keep_ref[...] + got_ref[...].astype(F32)).astype(BF16)
    fine_ref[...] = layer_norm(
        dot(cells.reshape(2 * window, features), lateral_ref[0]), gain_ref[0, 0][None, :]
    ).astype(BF16)
    near_ref[:window] = fine_ref[pl.ds(pl.multiple_of((1 - odd) * window, window), window), :]
    far_ref[:window] = fine_ref[pl.ds(pl.multiple_of(odd * window, window), window), :]
    tall = jnp.maximum(cells[0].astype(F32), cells[1].astype(F32))
    pooled = []
    for part in range(features // LANES):
        pool_ref[part] = tall[:, part * LANES : (part + 1) * LANES]
        even = pool_ref[part, pl.ds(0, window // 2, stride=2), :]
        odd = pool_ref[part, pl.ds(1, window // 2, stride=2), :]
        pooled.append(jnp.maximum(even, odd).astype(BF16))
    pooled = jnp.concatenate(pooled, axis=1)
    coarse = layer_norm(dot(pooled, lateral_ref[1]), gain_ref[1, 0][None, :]).astype(BF16)
    near_ref[window:] = coarse
    far_ref[window:] = coarse


def joined(terms, window):
    left, middle, right = (terms(tap_col) for tap_col in range(3))
    block = middle.shape[0]
    place = lax.broadcasted_iota(jnp.int32, middle.shape, 0) % window
    left = jnp.where(place == 0, 0.0, pltpu.roll(left, 1, axis=0))
    right = jnp.where(place == window - 1, 0.0, pltpu.roll(right, block - 1, axis=0))
    return left + middle + right


def own_conv_kernel(near_ref, far_ref, weight_ref, fine_ref, coarse_ref, fine_in):
    odd = lax.axis_index("blk") % 2
    window = fine_ref.shape[0] // 2
    for ref, place in ((near_ref, 1 - odd), (far_ref, odd)):
        fine_in[pl.ds(pl.multiple_of(place * window, window), window), :] = ref[:window]
    coarse = near_ref[window:]

    def fine_terms(tap_col):
        to_lower = dot(fine_in[:window], weight_ref[0, 0, tap_col])
        to_upper = dot(fine_in[window:], weight_ref[0, 2, tap_col])
        return dot(fine_in[...], weight_ref[0, 1, tap_col]) + jnp.concatenate(
            [to_upper, to_lower], axis=0
        )

    fine_ref[...] = joined(fine_terms, window)
    coarse_ref[...] = joined(lambda tap_col: dot(coarse, weight_ref[1, 1, tap_col]), window // 2)


def conv_kernel(
    got_near_ref,
    got_far_ref,
    own_fine_ref,
    own_coarse_ref,
    weight_ref,
    gain_ref,
    fine_ref,
    coarse_ref,
    edge_in,
    fine_sum,
    coarse_sum,
):
    core = lax.axis_index("head")
    odd = lax.axis_index("blk") % 2
    window = fine_sum.shape[0] // 2
    rows = got_near_ref.shape[0]
    for ref, place in ((got_near_ref, 1 - odd), (got_far_ref, odd)):
        edge_in[pl.ds(pl.multiple_of(place * rows, 32), rows), :] = ref[...]

    def fine_terms(tap_col):
        return jnp.concatenate(
            [
                dot(edge_in[:window], weight_ref[0, 0, tap_col]),
                dot(edge_in[rows : rows + window], weight_ref[0, 2, tap_col]),
            ],
            axis=0,
        )

    def coarse_terms(tap_col):
        return dot(edge_in[window:rows], weight_ref[1, 0, tap_col]) + dot(
            edge_in[rows + window :], weight_ref[1, 2, tap_col]
        )

    fine_sum[...] = own_fine_ref[...] + joined(fine_terms, window)
    coarse_sum[...] = own_coarse_ref[...] + joined(coarse_terms, window // 2)
    cols = fine_ref.shape[1]
    shift = GRID_COLS - window
    inset = cols - shift
    for row in range(2):
        here = pl.ds(pl.multiple_of(row * window + core * inset, 8), cols)
        fine_ref[row] = layer_norm(fine_sum[here, :], gain_ref[0, 1][None, :]).astype(BF16)
    here = pl.ds(pl.multiple_of(core * (inset // 2), 8), cols // 2)
    coarse_ref[0] = layer_norm(coarse_sum[here, :], gain_ref[1, 1][None, :]).astype(BF16)


def attend_shared(queries, keys, values):
    factor = HEAD_DIM ** (-0.5)
    step = math.gcd(keys.shape[0], 1536)
    rows = queries.shape[0]

    def block(state, pair):
        running, totals, weighted = state
        key, value = pair
        scores = (
            lax.dot_general(queries, key, (((1,), (1,)), ((), ())), preferred_element_type=F32)
            * factor
        )
        newmax = jnp.maximum(running, jnp.max(scores, axis=-1, keepdims=True))
        weights = jnp.exp(scores - newmax)
        shrink = jnp.exp(running - newmax)
        totals = totals * shrink + jnp.sum(weights, axis=-1, keepdims=True)
        weighted = weighted * shrink + dot(weights.astype(BF16), value)
        return (newmax, totals, weighted), None

    state = (
        jnp.full((rows, 1), -jnp.inf, F32),
        jnp.zeros((rows, 1), F32),
        jnp.zeros((rows, HEAD_DIM), F32),
    )
    state, _ = lax.scan(
        block, state, (keys.reshape(-1, step, HEAD_DIM), values.reshape(-1, step, HEAD_DIM))
    )
    return (state[2] / state[1]).astype(BF16)


def exchange(value):
    return lax.all_to_all(value, "blk", split_axis=0, concat_axis=0, tiled=True)


def attention_shared(mine, other, norm_gain, qkv_weight, slices):
    rows = mine.shape[0]
    width = qkv_weight.shape[2]
    heads = width // HEAD_DIM
    blocks = heads * slices
    share = rows // slices
    queries, keys, values = call(
        plain_qkv_kernel, [((rows, width), BF16)] * 3, (mine, other, norm_gain, qkv_weight)
    )
    query_send = jnp.transpose(
        queries.reshape(slices, share, heads, HEAD_DIM), (2, 0, 1, 3)
    ).reshape(blocks, share * HEAD_DIM)
    pair = jnp.concatenate(
        (keys.reshape(rows, heads, HEAD_DIM), values.reshape(rows, heads, HEAD_DIM)), axis=2
    )
    pair = jnp.transpose(pair, (1, 0, 2))
    pair_send = jnp.broadcast_to(pair[:, None], (heads, slices, rows, 2 * HEAD_DIM)).reshape(
        blocks, rows, 2 * HEAD_DIM
    )
    query_got = exchange(query_send).reshape(blocks * share, HEAD_DIM)
    pair_got = exchange(pair_send).reshape(blocks * rows, 2 * HEAD_DIM)
    one_head = attend_shared(query_got, pair_got[:, :HEAD_DIM], pair_got[:, HEAD_DIM:])
    back = exchange(one_head.reshape(blocks, share * HEAD_DIM))
    return jnp.transpose(back.reshape(heads, slices, share, HEAD_DIM), (1, 2, 0, 3)).reshape(
        rows, width
    )


def body(tokens, norm_gain, qkv_weight, out_weight, lateral_weight, conv_weight, level_gains):
    rows, half = tokens.shape
    features = out_weight.shape[1]
    width = qkv_weight.shape[2]
    heads = width // HEAD_DIM
    blocks = lax.axis_size("blk")
    cores = lax.axis_size("head")
    grid_rows = rows // GRID_COLS
    cols = GRID_COLS // cores
    channels = lateral_weight.shape[2]
    window = 2 * GRID_COLS // 3
    swap = [(i, cores - 1 - i) for i in range(cores)]

    other = lax.ppermute(tokens, "head", swap)
    (tokens,) = call(intake_kernel, [(tokens.shape, F32)], (tokens,), flops=MIB * 1024)
    other, tokens = lax.optimization_barrier((other, tokens))
    term_out = ((grid_rows, window, features), BF16)
    out_flops = 2 * grid_rows * window * width * features
    if blocks <= heads:
        order = list(range(0, blocks, 2)) + list(range(blocks - 1, 0, -2))
        forth = [(order[i - 1], order[i]) for i in range(blocks)]
        back = [(target, source) for source, target in forth]
        mine, across_core = call(
            norm_kernel, [((rows, half), BF16)] * 2, (tokens, other, norm_gain)
        )
        pairs = width // LANES
        state_outs = [
            ((pairs, 2 * rows, LANES), F32),
            ((pairs, 2 * rows, LANES), F32),
            ((pairs, rows, LANES), F32),
        ]
        ahead = lax.ppermute(mine, "blk", forth)
        behind = lax.ppermute(mine, "blk", back)
        unit = 4 * rows * width * (features + rows)
        queries, *state = call(
            own_kernel,
            [((pairs, 2 * rows, LANES), BF16)] + state_outs,
            (mine, across_core, qkv_weight),
            flops=unit + 2 * rows * width * features,
            exps=heads * rows * rows,
        )
        for step in range(1, blocks // 2):
            ahead, state[0] = lax.optimization_barrier((ahead, state[0]))
            behind, state[0] = lax.optimization_barrier((behind, state[0]))
            parts = (ahead, behind)
            (mark,) = call(mark_kernel, [((16, LANES), BF16)], (ahead,))
            if step == blocks // 2 - 1:
                ahead, behind = ahead[: rows // 2], behind[rows // 2 :]
            ahead = lax.ppermute(ahead, "blk", forth)
            behind = lax.ppermute(behind, "blk", back)
            others = (lax.ppermute(parts[0], "head", swap), lax.ppermute(parts[1], "head", swap))
            for block in zip(parts, others):
                state = call(
                    step_kernel,
                    state_outs,
                    block + (qkv_weight, queries) + tuple(state) + (mark,),
                    flops=unit,
                    exps=heads * rows * rows,
                )
            state = list(state)
        ahead, state[0] = lax.optimization_barrier((ahead, state[0]))
        behind, state[0] = lax.optimization_barrier((behind, state[0]))
        (mark,) = call(mark_kernel, [((16, LANES), BF16)], (ahead,))
        others = (lax.ppermute(ahead, "head", swap), lax.ppermute(behind, "head", swap))
        state = call(
            step_kernel,
            state_outs,
            (ahead, others[0], qkv_weight, queries) + tuple(state) + (mark,),
            flops=unit // 2,
            exps=heads * rows * rows // 2,
        )
        peer_term, attended = call(
            last_kernel,
            [term_out, ((rows, width), BF16)],
            (behind, others[1], qkv_weight, queries) + tuple(state) + (out_weight,),
            flops=unit // 2 + out_flops,
            exps=heads * rows * rows // 2,
        )
    else:
        attended = attention_shared(tokens, other, norm_gain, qkv_weight, blocks // heads)
        (peer_term,) = call(plain_out_kernel, [term_out], (attended, out_weight), flops=out_flops)
    peer_term = lax.ppermute(peer_term, "head", swap)
    (keep,) = call(
        keep_kernel,
        [((grid_rows, window, features), F32)],
        (attended, out_weight, tokens, other),
        [pltpu.VMEM((grid_rows * window, features), F32)],
        flops=out_flops,
    )

    message = (window + window // 2, channels)
    near, far = call(
        lateral_kernel,
        [(message, BF16), (message, BF16)],
        (keep, peer_term, lateral_weight, level_gains),
        [
            pltpu.VMEM((features // LANES, window, LANES), F32),
            pltpu.VMEM((2 * window, channels), BF16),
        ],
        flops=5 * window * features * channels,
    )
    far_pairs = [(i, i + 1) for i in range(1, blocks - 1, 2)]
    far_pairs += [(j, i) for i, j in far_pairs]
    got_far = lax.ppermute(far, "blk", far_pairs)
    got_near = lax.ppermute(near, "blk", [(i, i ^ 1) for i in range(blocks)])
    sums = [((2 * window, channels), F32), ((window // 2, channels), F32)]
    own_sums = call(
        own_conv_kernel,
        sums,
        (near, far, conv_weight),
        [pltpu.VMEM((2 * window, channels), BF16)],
        flops=27 * window * channels * channels,
    )
    return call(
        conv_kernel,
        [((grid_rows, cols, channels), BF16), ((grid_rows // 2, cols // 2, channels), BF16)],
        (got_near, got_far, *own_sums, conv_weight, level_gains),
        [pltpu.VMEM((2 * message[0], channels), BF16)]
        + [pltpu.VMEM(shape, dtype) for shape, dtype in sums],
        flops=18 * window * channels * channels,
    )


def solution(mesh):
    in_specs = (
        P(("groups", "blk"), "head"),
        P(),
        P(None, None, "head"),
        P("head", None),
        P(),
        P(),
        P(),
    )
    out_specs = (P(("groups", "blk"), "head", None), P(("groups", "blk"), "head", None))
    return jax.shard_map(body, mesh=mesh, in_specs=in_specs, out_specs=out_specs, check_vma=False)
```

```python
import functools
import math

import jax
import jax.numpy as jnp
from jax import lax
from jax.experimental import pallas as pl
from jax.experimental.pallas import tpu as pltpu
from jax.sharding import PartitionSpec as P

HEAD_DIM = 64
LANES = 128
GRID_COLS = 96
EPS = 1e-06
BF16 = jnp.bfloat16
F32 = jnp.float32
MIB = 1024 * 1024


def specs(count):
    return [pl.BlockSpec(memory_space=pltpu.VMEM)] * count


def nbytes(*arrays):
    return sum(math.prod(a.shape) * jnp.dtype(a.dtype).itemsize for a in arrays)


def call(kernel, outs, args, scratch=(), flops=0, exps=0, limit=24):
    outs = tuple(jax.ShapeDtypeStruct(shape, dtype) for shape, dtype in outs)
    return pl.pallas_call(
        kernel,
        out_shape=outs,
        in_specs=specs(len(args)),
        out_specs=tuple(specs(len(outs))),
        scratch_shapes=list(scratch),
        compiler_params=pltpu.CompilerParams(vmem_limit_bytes=limit * MIB),
        cost_estimate=pl.CostEstimate(
            flops=flops, transcendentals=exps, bytes_accessed=nbytes(*args, *outs)
        ),
    )(*args)


def layer_norm(values_in, gain_row):
    mean_row = jnp.mean(values_in, axis=-1, keepdims=True)
    centred = values_in - mean_row
    spread = jnp.mean(centred * centred, axis=-1, keepdims=True)
    return centred * lax.rsqrt(spread + EPS) * gain_row


def dot(a, b):
    return jnp.dot(a, b, preferred_element_type=F32)


def low_lanes(shape):
    return lax.broadcasted_iota(jnp.int32, shape, len(shape) - 1) % LANES < HEAD_DIM


def normalize(mine_ref, other_ref, gain_ref):
    half = mine_ref.shape[1]
    width = 2 * half
    mine, other = mine_ref[...], other_ref[...]
    mean = (
        jnp.sum(mine, axis=-1, keepdims=True) + jnp.sum(other, axis=-1, keepdims=True)
    ) / width
    mine, other = mine - mean, other - mean
    spread = (
        jnp.sum(mine * mine, axis=-1, keepdims=True)
        + jnp.sum(other * other, axis=-1, keepdims=True)
    ) / width
    scale = lax.rsqrt(spread + EPS)
    low_gain, high_gain = gain_ref[:half][None, :], gain_ref[half:][None, :]
    first = lax.axis_index("head") == 0
    mine = (mine * scale * jnp.where(first, low_gain, high_gain)).astype(BF16)
    other = (other * scale * jnp.where(first, high_gain, low_gain)).astype(BF16)
    return mine, other


def intake_kernel(tokens_ref, tokens_out):
    tokens_out[...] = tokens_ref[...]


def norm_kernel(mine_ref, other_ref, gain_ref, mine_out, other_out):
    mine_out[...], other_out[...] = normalize(mine_ref, other_ref, gain_ref)


def project(mine, other, weight_ref, part):
    core = lax.axis_index("head")
    half = mine.shape[1]
    mine_at = pl.ds(pl.multiple_of(core * half, half), half)
    other_at = pl.ds(pl.multiple_of((1 - core) * half, half), half)
    return (
        dot(mine, weight_ref[part, mine_at, :]) + dot(other, weight_ref[part, other_at, :])
    ).astype(BF16)


def plain_qkv_kernel(mine_ref, other_ref, gain_ref, weight_ref, *out_refs):
    mine, other = normalize(mine_ref, other_ref, gain_ref)
    for part, ref in enumerate(out_refs):
        ref[...] = project(mine, other, weight_ref, part)


def spread_lanes(column, width=LANES):
    return jnp.broadcast_to(column, (column.shape[0], width))


def across(lanes, width):
    whole, rest = divmod(width, LANES)
    return jnp.concatenate([lanes] * whole + ([lanes[:, :rest]] if rest else []), axis=1)


def absorb(pair, queries, keys, values, old):
    factor = HEAD_DIM ** (-0.5) * math.log2(math.e)
    cols = slice(pair * LANES, (pair + 1) * LANES)
    scores = lax.dot_general(
        queries, keys[:, cols], (((1,), (1,)), ((), ())), preferred_element_type=F32
    )
    top = spread_lanes(jnp.max(scores, axis=-1, keepdims=True))
    if old is not None:
        old_top, old_total, old_mixed = old
        top = jnp.maximum(top, old_top)
    weights = jnp.exp2((scores - across(top, scores.shape[1])) * factor)
    total = spread_lanes(jnp.sum(weights, axis=-1, keepdims=True))
    mixed = dot(weights.astype(BF16), values[:, cols])
    rows = mixed.shape[0] // 2
    low = low_lanes((rows, LANES))
    mixed = jnp.where(low, mixed[:rows], mixed[rows:])
    if old is not None:
        shrink = jnp.exp2((old_top - top) * factor)
        total = total + old_total * shrink
        mixed = mixed + old_mixed * jnp.where(low, shrink[:rows], shrink[rows:])
    return top, total, mixed


def own_kernel(
    mine_ref, other_ref, weight_ref, query_ref, top_ref, total_ref, mixed_ref
):
    mine, other = mine_ref[...], other_ref[...]
    rows = mine.shape[0]
    queries = project(mine, other, weight_ref, 0)
    keys = project(mine, other, weight_ref, 1)
    values = project(mine, other, weight_ref, 2)
    low = low_lanes((rows, LANES))
    for pair in range(query_ref.shape[0]):
        tile = queries[:, pair * LANES : (pair + 1) * LANES]
        query_ref[pair, :rows] = jnp.where(low, tile, jnp.zeros_like(tile))
        query_ref[pair, rows:] = jnp.where(low, jnp.zeros_like(tile), tile)
        top_ref[pair], total_ref[pair], mixed_ref[pair] = absorb(
            pair, query_ref[pair], keys, values, None
        )


def stacked(refs):
    return jnp.concatenate([ref[...] for ref in refs], axis=0) if len(refs) > 1 else refs[0][...]


def absorb_keys(keys, values, query_ref, top_ref, total_ref, mixed_ref):
    for pair in range(query_ref.shape[0]):
        old = top_ref[pair], total_ref[pair], mixed_ref[pair]
        yield pair, absorb(pair, query_ref[pair], keys, values, old)


def mark_kernel(block_ref, mark_ref):
    mark_ref[...] = block_ref[: mark_ref.shape[0], : mark_ref.shape[1]]


def step_kernel(pieces, *refs):
    mine_refs, other_refs = refs[:pieces], refs[pieces : 2 * pieces]
    weight_ref, *state_refs = refs[2 * pieces : 2 * pieces + 5]
    out_refs = refs[-3:]
    mine, other = stacked(mine_refs), stacked(other_refs)
    keys = project(mine, other, weight_ref, 1)
    values = project(mine, other, weight_ref, 2)
    for pair, state in absorb_keys(keys, values, *state_refs):
        for ref, value in zip(out_refs, state):
            ref[pair] = value


def half_kernel(mine_a, mine_b, weight_ref, mark_ref, keys_ref, values_ref):
    mine = stacked((mine_a, mine_b))
    half = mine.shape[1]
    here = pl.ds(pl.multiple_of(lax.axis_index("head") * half, half), half)
    keys_ref[...] = dot(mine, weight_ref[1, here, :])
    values_ref[...] = dot(mine, weight_ref[2, here, :])


def send_terms(att_ref, weight_ref, send_ref):
    grid_rows, window = send_ref.shape[:2]
    shift = (1 - lax.axis_index("head")) * (GRID_COLS - window)
    cells = jnp.concatenate(
        [
            att_ref[pl.ds(pl.multiple_of(row * GRID_COLS + shift, 32), window), :]
            for row in range(grid_rows)
        ],
        axis=0,
    )
    send_ref[...] = dot(cells, weight_ref[...]).astype(BF16).reshape(send_ref.shape)


def keep_kernel(att_ref, weight_ref, mine_ref, other_ref, keep_ref, full_ref):
    core = lax.axis_index("head")
    grid_rows, window = keep_ref.shape[:2]
    half = mine_ref.shape[1]
    shift = core * (GRID_COLS - window)
    places = [
        pl.ds(pl.multiple_of(row * GRID_COLS + shift, 32), window) for row in range(grid_rows)
    ]
    cells = jnp.concatenate([att_ref[here, :] for here in places], axis=0)
    full_ref[...] = dot(cells, weight_ref[...])
    for row, here in enumerate(places):
        there = slice(row * window, (row + 1) * window)
        for part, ref in ((core, mine_ref), (1 - core, other_ref)):
            cols = pl.ds(pl.multiple_of(part * half, half), half)
            keep_ref[row, :, cols] = full_ref[there, cols] + ref[here, :]


def last_kernel(
    other_a,
    other_b,
    keys_ref,
    values_ref,
    weight_ref,
    query_ref,
    top_ref,
    total_ref,
    mixed_ref,
    out_weight_ref,
    send_ref,
    att_ref,
):
    rows = mixed_ref.shape[1]
    low = low_lanes((rows, LANES))
    other = stacked((other_a, other_b))
    half = other.shape[1]
    there = pl.ds(pl.multiple_of((1 - lax.axis_index("head")) * half, half), half)
    keys = (keys_ref[...] + dot(other, weight_ref[1, there, :])).astype(BF16)
    values = (values_ref[...] + dot(other, weight_ref[2, there, :])).astype(BF16)
    for pair, (_, total, mixed) in absorb_keys(
        keys, values, query_ref, top_ref, total_ref, mixed_ref
    ):
        cols = slice(pair * LANES, (pair + 1) * LANES)
        att_ref[:, cols] = (mixed / jnp.where(low, total[:rows], total[rows:])).astype(BF16)
    send_terms(att_ref, out_weight_ref, send_ref)


def plain_out_kernel(att_ref, weight_ref, send_ref):
    send_terms(att_ref, weight_ref, send_ref)


def lateral_kernel(
    keep_ref, got_ref, lateral_ref, gain_ref, near_ref, far_ref, pool_ref, fine_ref
):
    odd = lax.axis_index("blk") % 2
    window, features = keep_ref.shape[1], keep_ref.shape[2]
    cells = (keep_ref[...] + got_ref[...].astype(F32)).astype(BF16)
    fine_ref[...] = layer_norm(
        dot(cells.reshape(2 * window, features), lateral_ref[0]), gain_ref[0, 0][None, :]
    ).astype(BF16)
    near_ref[:window] = fine_ref[pl.ds(pl.multiple_of((1 - odd) * window, window), window), :]
    far_ref[:window] = fine_ref[pl.ds(pl.multiple_of(odd * window, window), window), :]
    tall = jnp.maximum(cells[0].astype(F32), cells[1].astype(F32))
    pooled = []
    for part in range(features // LANES):
        pool_ref[part] = tall[:, part * LANES : (part + 1) * LANES]
        even = pool_ref[part, pl.ds(0, window // 2, stride=2), :]
        odd = pool_ref[part, pl.ds(1, window // 2, stride=2), :]
        pooled.append(jnp.maximum(even, odd).astype(BF16))
    pooled = jnp.concatenate(pooled, axis=1)
    coarse = layer_norm(dot(pooled, lateral_ref[1]), gain_ref[1, 0][None, :]).astype(BF16)
    near_ref[window:] = coarse
    far_ref[window:] = coarse


def joined(terms, window):
    left, middle, right = (terms(tap_col) for tap_col in range(3))
    block = middle.shape[0]
    place = lax.broadcasted_iota(jnp.int32, middle.shape, 0) % window
    left = jnp.where(place == 0, 0.0, pltpu.roll(left, 1, axis=0))
    right = jnp.where(place == window - 1, 0.0, pltpu.roll(right, block - 1, axis=0))
    return left + middle + right


def own_conv_kernel(near_ref, far_ref, weight_ref, fine_ref, coarse_ref, fine_in):
    odd = lax.axis_index("blk") % 2
    window = fine_ref.shape[0] // 2
    for ref, place in ((near_ref, 1 - odd), (far_ref, odd)):
        fine_in[pl.ds(pl.multiple_of(place * window, window), window), :] = ref[:window]
    coarse = near_ref[window:]

    def fine_terms(tap_col):
        to_lower = dot(fine_in[:window], weight_ref[0, 0, tap_col])
        to_upper = dot(fine_in[window:], weight_ref[0, 2, tap_col])
        return dot(fine_in[...], weight_ref[0, 1, tap_col]) + jnp.concatenate(
            [to_upper, to_lower], axis=0
        )

    fine_ref[...] = joined(fine_terms, window)
    coarse_ref[...] = joined(lambda tap_col: dot(coarse, weight_ref[1, 1, tap_col]), window // 2)


def conv_kernel(
    got_near_ref,
    got_far_ref,
    own_fine_ref,
    own_coarse_ref,
    weight_ref,
    gain_ref,
    fine_ref,
    coarse_ref,
    edge_in,
    fine_sum,
    coarse_sum,
):
    core = lax.axis_index("head")
    odd = lax.axis_index("blk") % 2
    window = fine_sum.shape[0] // 2
    rows = got_near_ref.shape[0]
    for ref, place in ((got_near_ref, 1 - odd), (got_far_ref, odd)):
        edge_in[pl.ds(pl.multiple_of(place * rows, 32), rows), :] = ref[...]

    def fine_terms(tap_col):
        return jnp.concatenate(
            [
                dot(edge_in[:window], weight_ref[0, 0, tap_col]),
                dot(edge_in[rows : rows + window], weight_ref[0, 2, tap_col]),
            ],
            axis=0,
        )

    def coarse_terms(tap_col):
        return dot(edge_in[window:rows], weight_ref[1, 0, tap_col]) + dot(
            edge_in[rows + window :], weight_ref[1, 2, tap_col]
        )

    fine_sum[...] = own_fine_ref[...] + joined(fine_terms, window)
    coarse_sum[...] = own_coarse_ref[...] + joined(coarse_terms, window // 2)
    cols = fine_ref.shape[1]
    shift = GRID_COLS - window
    inset = cols - shift
    for row in range(2):
        here = pl.ds(pl.multiple_of(row * window + core * inset, 8), cols)
        fine_ref[row] = layer_norm(fine_sum[here, :], gain_ref[0, 1][None, :]).astype(BF16)
    here = pl.ds(pl.multiple_of(core * (inset // 2), 8), cols // 2)
    coarse_ref[0] = layer_norm(coarse_sum[here, :], gain_ref[1, 1][None, :]).astype(BF16)


def attend_shared(queries, keys, values):
    factor = HEAD_DIM ** (-0.5)
    step = math.gcd(keys.shape[0], 1536)
    rows = queries.shape[0]

    def block(state, pair):
        running, totals, weighted = state
        key, value = pair
        scores = (
            lax.dot_general(queries, key, (((1,), (1,)), ((), ())), preferred_element_type=F32)
            * factor
        )
        newmax = jnp.maximum(running, jnp.max(scores, axis=-1, keepdims=True))
        weights = jnp.exp(scores - newmax)
        shrink = jnp.exp(running - newmax)
        totals = totals * shrink + jnp.sum(weights, axis=-1, keepdims=True)
        weighted = weighted * shrink + dot(weights.astype(BF16), value)
        return (newmax, totals, weighted), None

    state = (
        jnp.full((rows, 1), -jnp.inf, F32),
        jnp.zeros((rows, 1), F32),
        jnp.zeros((rows, HEAD_DIM), F32),
    )
    state, _ = lax.scan(
        block, state, (keys.reshape(-1, step, HEAD_DIM), values.reshape(-1, step, HEAD_DIM))
    )
    return (state[2] / state[1]).astype(BF16)


def exchange(value):
    return lax.all_to_all(value, "blk", split_axis=0, concat_axis=0, tiled=True)


def attention_shared(mine, other, norm_gain, qkv_weight, slices):
    rows = mine.shape[0]
    width = qkv_weight.shape[2]
    heads = width // HEAD_DIM
    blocks = heads * slices
    share = rows // slices
    queries, keys, values = call(
        plain_qkv_kernel, [((rows, width), BF16)] * 3, (mine, other, norm_gain, qkv_weight)
    )
    query_send = jnp.transpose(
        queries.reshape(slices, share, heads, HEAD_DIM), (2, 0, 1, 3)
    ).reshape(blocks, share * HEAD_DIM)
    pair = jnp.concatenate(
        (keys.reshape(rows, heads, HEAD_DIM), values.reshape(rows, heads, HEAD_DIM)), axis=2
    )
    pair = jnp.transpose(pair, (1, 0, 2))
    pair_send = jnp.broadcast_to(pair[:, None], (heads, slices, rows, 2 * HEAD_DIM)).reshape(
        blocks, rows, 2 * HEAD_DIM
    )
    query_got = exchange(query_send).reshape(blocks * share, HEAD_DIM)
    pair_got = exchange(pair_send).reshape(blocks * rows, 2 * HEAD_DIM)
    one_head = attend_shared(query_got, pair_got[:, :HEAD_DIM], pair_got[:, HEAD_DIM:])
    back = exchange(one_head.reshape(blocks, share * HEAD_DIM))
    return jnp.transpose(back.reshape(heads, slices, share, HEAD_DIM), (1, 2, 0, 3)).reshape(
        rows, width
    )


def body(tokens, norm_gain, qkv_weight, out_weight, lateral_weight, conv_weight, level_gains):
    rows, half = tokens.shape
    features = out_weight.shape[1]
    width = qkv_weight.shape[2]
    heads = width // HEAD_DIM
    blocks = lax.axis_size("blk")
    cores = lax.axis_size("head")
    grid_rows = rows // GRID_COLS
    cols = GRID_COLS // cores
    channels = lateral_weight.shape[2]
    window = 2 * GRID_COLS // 3
    swap = [(i, cores - 1 - i) for i in range(cores)]

    other = lax.ppermute(tokens, "head", swap)
    (tokens,) = call(intake_kernel, [(tokens.shape, F32)], (tokens,), flops=MIB * 1024)
    other, tokens = lax.optimization_barrier((other, tokens))
    term_out = ((grid_rows, window, features), BF16)
    out_flops = 2 * grid_rows * window * width * features
    if 6 <= blocks <= heads:
        order = list(range(0, blocks, 2)) + list(range(blocks - 1, 0, -2))
        forth = [(order[i - 1], order[i]) for i in range(blocks)]
        back = [(target, source) for source, target in forth]
        mine, across_core = call(
            norm_kernel, [((rows, half), BF16)] * 2, (tokens, other, norm_gain)
        )
        pairs = width // LANES
        state_outs = [
            ((pairs, 2 * rows, LANES), F32),
            ((pairs, 2 * rows, LANES), F32),
            ((pairs, rows, LANES), F32),
        ]
        ahead = lax.ppermute(mine, "blk", forth)
        behind = lax.ppermute(mine, "blk", back)
        unit = 4 * rows * width * (features + rows)
        queries, *state = call(
            own_kernel,
            [((pairs, 2 * rows, LANES), BF16)] + state_outs,
            (mine, across_core, qkv_weight),
            flops=unit + 2 * rows * width * features,
            exps=heads * rows * rows,
        )
        last = blocks // 2
        ahead, behind = (ahead,), (behind,)
        for step in range(1, last + 1):
            first, state[0] = lax.optimization_barrier((ahead[0], state[0]))
            ahead = (first,) + ahead[1:]
            first, state[0] = lax.optimization_barrier((behind[0], state[0]))
            behind = (first,) + behind[1:]
            arrived = ahead, behind
            (mark,) = call(mark_kernel, [((16, LANES), BF16)], (ahead[0],))
            if step == last - 1:
                ahead, behind = ahead[:1], behind[:1]
            elif step == last - 2:
                (whole_a,), (whole_b,) = ahead, behind
                ahead = whole_a[: rows // 2], whole_a[rows // 2 :]
                behind = whole_b[rows // 2 :], whole_b[: rows // 2]
            if step < last:
                ahead, behind = (
                    tuple(lax.ppermute(piece, "blk", pairs_of) for piece in pieces)
                    for pieces, pairs_of in ((ahead, forth), (behind, back))
                )
            traded = tuple(
                tuple(lax.ppermute(piece, "head", swap) for piece in pieces)
                for pieces in arrived
            )
            if step == last:
                break
            for mine, across_core in zip(arrived, traded):
                state = call(
                    functools.partial(step_kernel, len(mine)),
                    state_outs,
                    mine + across_core + (qkv_weight, queries) + tuple(state) + (mark,),
                    flops=unit,
                    exps=heads * rows * rows,
                )
            state = list(state)
        keys, values = call(
            half_kernel,
            [((rows, width), F32)] * 2,
            (*arrived[0], *arrived[1], qkv_weight, mark),
            flops=2 * rows * width * features,
        )
        peer_term, attended = call(
            last_kernel,
            [term_out, ((rows, width), BF16)],
            (*traded[0], *traded[1], keys, values, qkv_weight, queries)
            + tuple(state)
            + (out_weight,),
            flops=unit + out_flops,
            exps=heads * rows * rows,
        )
    else:
        attended = attention_shared(tokens, other, norm_gain, qkv_weight, blocks // heads)
        (peer_term,) = call(plain_out_kernel, [term_out], (attended, out_weight), flops=out_flops)
    peer_term = lax.ppermute(peer_term, "head", swap)
    (keep,) = call(
        keep_kernel,
        [((grid_rows, window, features), F32)],
        (attended, out_weight, tokens, other),
        [pltpu.VMEM((grid_rows * window, features), F32)],
        flops=out_flops,
    )

    message = (window + window // 2, channels)
    near, far = call(
        lateral_kernel,
        [(message, BF16), (message, BF16)],
        (keep, peer_term, lateral_weight, level_gains),
        [
            pltpu.VMEM((features // LANES, window, LANES), F32),
            pltpu.VMEM((2 * window, channels), BF16),
        ],
        flops=5 * window * features * channels,
    )
    far_pairs = [(i, i + 1) for i in range(1, blocks - 1, 2)]
    far_pairs += [(j, i) for i, j in far_pairs]
    got_far = lax.ppermute(far, "blk", far_pairs)
    got_near = lax.ppermute(near, "blk", [(i, i ^ 1) for i in range(blocks)])
    sums = [((2 * window, channels), F32), ((window // 2, channels), F32)]
    own_sums = call(
        own_conv_kernel,
        sums,
        (near, far, conv_weight),
        [pltpu.VMEM((2 * window, channels), BF16)],
        flops=27 * window * channels * channels,
    )
    return call(
        conv_kernel,
        [((grid_rows, cols, channels), BF16), ((grid_rows // 2, cols // 2, channels), BF16)],
        (got_near, got_far, *own_sums, conv_weight, level_gains),
        [pltpu.VMEM((2 * message[0], channels), BF16)]
        + [pltpu.VMEM(shape, dtype) for shape, dtype in sums],
        flops=18 * window * channels * channels,
    )


def solution(mesh):
    in_specs = (
        P(("groups", "blk"), "head"),
        P(),
        P(None, None, "head"),
        P("head", None),
        P(),
        P(),
        P(),
    )
    out_specs = (P(("groups", "blk"), "head", None), P(("groups", "blk"), "head", None))
    return jax.shard_map(body, mesh=mesh, in_specs=in_specs, out_specs=out_specs, check_vma=False)
```

```python
import math

import jax
import jax.numpy as jnp
from jax import lax
from jax.experimental import pallas as pl
from jax.experimental.pallas import tpu as pltpu
from jax.sharding import PartitionSpec as P

HEAD_DIM = 64
LANES = 128
GRID_COLS = 96
EPS = 1e-06
BF16 = jnp.bfloat16
F32 = jnp.float32
MIB = 1024 * 1024


def specs(count):
    return [pl.BlockSpec(memory_space=pltpu.VMEM)] * count


def nbytes(*arrays):
    return sum(math.prod(a.shape) * jnp.dtype(a.dtype).itemsize for a in arrays)


def call(kernel, outs, args, scratch=(), flops=0, exps=0, limit=24):
    outs = tuple(jax.ShapeDtypeStruct(shape, dtype) for shape, dtype in outs)
    return pl.pallas_call(
        kernel,
        out_shape=outs,
        in_specs=specs(len(args)),
        out_specs=tuple(specs(len(outs))),
        scratch_shapes=list(scratch),
        compiler_params=pltpu.CompilerParams(vmem_limit_bytes=limit * MIB),
        cost_estimate=pl.CostEstimate(
            flops=flops, transcendentals=exps, bytes_accessed=nbytes(*args, *outs)
        ),
    )(*args)


def layer_norm(values_in, gain_row):
    mean_row = jnp.mean(values_in, axis=-1, keepdims=True)
    centred = values_in - mean_row
    spread = jnp.mean(centred * centred, axis=-1, keepdims=True)
    return centred * lax.rsqrt(spread + EPS) * gain_row


def dot(a, b):
    return jnp.dot(a, b, preferred_element_type=F32)


def low_lanes(shape):
    return lax.broadcasted_iota(jnp.int32, shape, len(shape) - 1) % LANES < HEAD_DIM


def normalize(mine_ref, other_ref, gain_ref):
    half = mine_ref.shape[1]
    width = 2 * half
    mine, other = mine_ref[...], other_ref[...]
    mean = (
        jnp.sum(mine, axis=-1, keepdims=True) + jnp.sum(other, axis=-1, keepdims=True)
    ) / width
    mine, other = mine - mean, other - mean
    spread = (
        jnp.sum(mine * mine, axis=-1, keepdims=True)
        + jnp.sum(other * other, axis=-1, keepdims=True)
    ) / width
    scale = lax.rsqrt(spread + EPS)
    low_gain, high_gain = gain_ref[:half][None, :], gain_ref[half:][None, :]
    first = lax.axis_index("head") == 0
    mine = (mine * scale * jnp.where(first, low_gain, high_gain)).astype(BF16)
    other = (other * scale * jnp.where(first, high_gain, low_gain)).astype(BF16)
    return mine, other


def intake_kernel(tokens_ref, tokens_out):
    tokens_out[...] = tokens_ref[...]


def norm_kernel(mine_ref, other_ref, gain_ref, mine_out, other_out):
    mine_out[...], other_out[...] = normalize(mine_ref, other_ref, gain_ref)


def project(mine, other, weight_ref, part):
    core = lax.axis_index("head")
    half = mine.shape[1]
    mine_at = pl.ds(pl.multiple_of(core * half, half), half)
    other_at = pl.ds(pl.multiple_of((1 - core) * half, half), half)
    return (
        dot(mine, weight_ref[part, mine_at, :]) + dot(other, weight_ref[part, other_at, :])
    ).astype(BF16)


def plain_qkv_kernel(mine_ref, other_ref, gain_ref, weight_ref, *out_refs):
    mine, other = normalize(mine_ref, other_ref, gain_ref)
    for part, ref in enumerate(out_refs):
        ref[...] = project(mine, other, weight_ref, part)


def spread_lanes(column, width=LANES):
    return jnp.broadcast_to(column, (column.shape[0], width))


def across(lanes, width):
    whole, rest = divmod(width, LANES)
    return jnp.concatenate([lanes] * whole + ([lanes[:, :rest]] if rest else []), axis=1)


def absorb(pair, queries, keys, values, old):
    factor = HEAD_DIM ** (-0.5) * math.log2(math.e)
    cols = slice(pair * LANES, (pair + 1) * LANES)
    scores = lax.dot_general(
        queries, keys[:, cols], (((1,), (1,)), ((), ())), preferred_element_type=F32
    )
    top = spread_lanes(jnp.max(scores, axis=-1, keepdims=True))
    if old is not None:
        old_top, old_total, old_mixed = old
        top = jnp.maximum(top, old_top)
    weights = jnp.exp2((scores - across(top, scores.shape[1])) * factor)
    total = spread_lanes(jnp.sum(weights, axis=-1, keepdims=True))
    mixed = dot(weights.astype(BF16), values[:, cols])
    rows = mixed.shape[0] // 2
    low = low_lanes((rows, LANES))
    mixed = jnp.where(low, mixed[:rows], mixed[rows:])
    if old is not None:
        shrink = jnp.exp2((old_top - top) * factor)
        total = total + old_total * shrink
        mixed = mixed + old_mixed * jnp.where(low, shrink[:rows], shrink[rows:])
    return top, total, mixed


def own_kernel(
    mine_ref, other_ref, weight_ref, query_ref, top_ref, total_ref, mixed_ref
):
    mine, other = mine_ref[...], other_ref[...]
    rows = mine.shape[0]
    queries = project(mine, other, weight_ref, 0)
    keys = project(mine, other, weight_ref, 1)
    values = project(mine, other, weight_ref, 2)
    low = low_lanes((rows, LANES))
    for pair in range(query_ref.shape[0]):
        tile = queries[:, pair * LANES : (pair + 1) * LANES]
        query_ref[pair, :rows] = jnp.where(low, tile, jnp.zeros_like(tile))
        query_ref[pair, rows:] = jnp.where(low, jnp.zeros_like(tile), tile)
        top_ref[pair], total_ref[pair], mixed_ref[pair] = absorb(
            pair, query_ref[pair], keys, values, None
        )


def absorb_keys(keys, values, query_ref, top_ref, total_ref, mixed_ref):
    for pair in range(query_ref.shape[0]):
        old = top_ref[pair], total_ref[pair], mixed_ref[pair]
        yield pair, absorb(pair, query_ref[pair], keys, values, old)


def mark_kernel(block_ref, mark_ref):
    mark_ref[...] = block_ref[: mark_ref.shape[0], : mark_ref.shape[1]]


def step_kernel(
    mine_ref,
    other_ref,
    weight_ref,
    query_ref,
    top_ref,
    total_ref,
    mixed_ref,
    mark_ref,
    top_out,
    total_out,
    mixed_out,
):
    mine, other = mine_ref[...], other_ref[...]
    keys = project(mine, other, weight_ref, 1)
    values = project(mine, other, weight_ref, 2)
    for pair, state in absorb_keys(keys, values, query_ref, top_ref, total_ref, mixed_ref):
        top_out[pair], total_out[pair], mixed_out[pair] = state


def half_kernel(mine_a, mine_b, weight_ref, mark_ref, keys_ref, values_ref):
    mine = jnp.concatenate([mine_a[...], mine_b[...]], axis=0)
    half = mine.shape[1]
    here = pl.ds(pl.multiple_of(lax.axis_index("head") * half, half), half)
    keys_ref[...] = dot(mine, weight_ref[1, here, :])
    values_ref[...] = dot(mine, weight_ref[2, here, :])


def send_terms(att_ref, weight_ref, send_ref):
    grid_rows, window = send_ref.shape[:2]
    shift = (1 - lax.axis_index("head")) * (GRID_COLS - window)
    cells = jnp.concatenate(
        [
            att_ref[pl.ds(pl.multiple_of(row * GRID_COLS + shift, 32), window), :]
            for row in range(grid_rows)
        ],
        axis=0,
    )
    send_ref[...] = dot(cells, weight_ref[...]).astype(BF16).reshape(send_ref.shape)


def keep_kernel(att_ref, weight_ref, mine_ref, other_ref, keep_ref, full_ref):
    core = lax.axis_index("head")
    grid_rows, window = keep_ref.shape[:2]
    half = mine_ref.shape[1]
    shift = core * (GRID_COLS - window)
    places = [
        pl.ds(pl.multiple_of(row * GRID_COLS + shift, 32), window) for row in range(grid_rows)
    ]
    cells = jnp.concatenate([att_ref[here, :] for here in places], axis=0)
    full_ref[...] = dot(cells, weight_ref[...])
    for row, here in enumerate(places):
        there = slice(row * window, (row + 1) * window)
        for part, ref in ((core, mine_ref), (1 - core, other_ref)):
            cols = pl.ds(pl.multiple_of(part * half, half), half)
            keep_ref[row, :, cols] = full_ref[there, cols] + ref[here, :]


def last_kernel(
    other_a,
    other_b,
    keys_ref,
    values_ref,
    weight_ref,
    query_ref,
    top_ref,
    total_ref,
    mixed_ref,
    out_weight_ref,
    send_ref,
    att_ref,
):
    rows = mixed_ref.shape[1]
    low = low_lanes((rows, LANES))
    other = jnp.concatenate([other_a[...], other_b[...]], axis=0)
    half = other.shape[1]
    there = pl.ds(pl.multiple_of((1 - lax.axis_index("head")) * half, half), half)
    keys = (keys_ref[...] + dot(other, weight_ref[1, there, :])).astype(BF16)
    values = (values_ref[...] + dot(other, weight_ref[2, there, :])).astype(BF16)
    for pair, (_, total, mixed) in absorb_keys(
        keys, values, query_ref, top_ref, total_ref, mixed_ref
    ):
        cols = slice(pair * LANES, (pair + 1) * LANES)
        att_ref[:, cols] = (mixed / jnp.where(low, total[:rows], total[rows:])).astype(BF16)
    send_terms(att_ref, out_weight_ref, send_ref)


def plain_out_kernel(att_ref, weight_ref, send_ref):
    send_terms(att_ref, weight_ref, send_ref)


def lateral_kernel(
    keep_ref, got_ref, lateral_ref, gain_ref, first_ref, second_ref, pool_ref, fine_ref
):
    core = lax.axis_index("head")
    window, features = keep_ref.shape[1], keep_ref.shape[2]
    cells = (keep_ref[...] + got_ref[...].astype(F32)).astype(BF16)
    fine_ref[...] = layer_norm(
        dot(cells.reshape(2 * window, features), lateral_ref[0]), gain_ref[0, 0][None, :]
    ).astype(BF16)
    first_ref[:window] = fine_ref[pl.ds(pl.multiple_of((1 - core) * window, window), window), :]
    second_ref[:window] = fine_ref[pl.ds(pl.multiple_of(core * window, window), window), :]
    tall = jnp.maximum(cells[0].astype(F32), cells[1].astype(F32))
    pooled = []
    for part in range(features // LANES):
        pool_ref[part] = tall[:, part * LANES : (part + 1) * LANES]
        even = pool_ref[part, pl.ds(0, window // 2, stride=2), :]
        odd = pool_ref[part, pl.ds(1, window // 2, stride=2), :]
        pooled.append(jnp.maximum(even, odd).astype(BF16))
    pooled = jnp.concatenate(pooled, axis=1)
    coarse = layer_norm(dot(pooled, lateral_ref[1]), gain_ref[1, 0][None, :]).astype(BF16)
    first_ref[window:] = coarse
    second_ref[window:] = coarse


def joined(terms, window):
    left, middle, right = (terms(tap_col) for tap_col in range(3))
    block = middle.shape[0]
    place = lax.broadcasted_iota(jnp.int32, middle.shape, 0) % window
    left = jnp.where(place == 0, 0.0, pltpu.roll(left, 1, axis=0))
    right = jnp.where(place == window - 1, 0.0, pltpu.roll(right, block - 1, axis=0))
    return left + middle + right


def own_conv_kernel(first_ref, second_ref, weight_ref, fine_ref, coarse_ref, fine_in):
    core = lax.axis_index("head")
    window = fine_ref.shape[0] // 2
    for ref, place in ((first_ref, 1 - core), (second_ref, core)):
        fine_in[pl.ds(pl.multiple_of(place * window, window), window), :] = ref[:window]
    coarse = first_ref[window:]

    def fine_terms(tap_col):
        to_lower = dot(fine_in[:window], weight_ref[0, 0, tap_col])
        to_upper = dot(fine_in[window:], weight_ref[0, 2, tap_col])
        return dot(fine_in[...], weight_ref[0, 1, tap_col]) + jnp.concatenate(
            [to_upper, to_lower], axis=0
        )

    fine_ref[...] = joined(fine_terms, window)
    coarse_ref[...] = joined(lambda tap_col: dot(coarse, weight_ref[1, 1, tap_col]), window // 2)


def conv_kernel(
    got_first_ref,
    got_second_ref,
    own_fine_ref,
    own_coarse_ref,
    weight_ref,
    gain_ref,
    fine_ref,
    coarse_ref,
    edge_in,
    fine_sum,
    coarse_sum,
):
    core = lax.axis_index("head")
    block = lax.axis_index("blk")
    edge = (0, lax.axis_size("blk") - 1)
    window = fine_sum.shape[0] // 2
    rows = got_first_ref.shape[0]
    for ref, place in ((got_first_ref, core), (got_second_ref, 1 - core)):
        inside = block != jnp.where(place == 0, *edge)
        edge_in[pl.ds(pl.multiple_of(place * rows, 32), rows), :] = jnp.where(
            inside, ref[...].astype(F32), 0.0
        ).astype(BF16)

    def fine_terms(tap_col):
        return jnp.concatenate(
            [
                dot(edge_in[:window], weight_ref[0, 0, tap_col]),
                dot(edge_in[rows : rows + window], weight_ref[0, 2, tap_col]),
            ],
            axis=0,
        )

    def coarse_terms(tap_col):
        return dot(edge_in[window:rows], weight_ref[1, 0, tap_col]) + dot(
            edge_in[rows + window :], weight_ref[1, 2, tap_col]
        )

    fine_sum[...] = own_fine_ref[...] + joined(fine_terms, window)
    coarse_sum[...] = own_coarse_ref[...] + joined(coarse_terms, window // 2)
    cols = fine_ref.shape[1]
    shift = GRID_COLS - window
    inset = cols - shift
    for row in range(2):
        here = pl.ds(pl.multiple_of(row * window + core * inset, 8), cols)
        fine_ref[row] = layer_norm(fine_sum[here, :], gain_ref[0, 1][None, :]).astype(BF16)
    here = pl.ds(pl.multiple_of(core * (inset // 2), 8), cols // 2)
    coarse_ref[0] = layer_norm(coarse_sum[here, :], gain_ref[1, 1][None, :]).astype(BF16)


def attend_shared(queries, keys, values):
    factor = HEAD_DIM ** (-0.5)
    step = math.gcd(keys.shape[0], 1536)
    rows = queries.shape[0]

    def block(state, pair):
        running, totals, weighted = state
        key, value = pair
        scores = (
            lax.dot_general(queries, key, (((1,), (1,)), ((), ())), preferred_element_type=F32)
            * factor
        )
        newmax = jnp.maximum(running, jnp.max(scores, axis=-1, keepdims=True))
        weights = jnp.exp(scores - newmax)
        shrink = jnp.exp(running - newmax)
        totals = totals * shrink + jnp.sum(weights, axis=-1, keepdims=True)
        weighted = weighted * shrink + dot(weights.astype(BF16), value)
        return (newmax, totals, weighted), None

    state = (
        jnp.full((rows, 1), -jnp.inf, F32),
        jnp.zeros((rows, 1), F32),
        jnp.zeros((rows, HEAD_DIM), F32),
    )
    state, _ = lax.scan(
        block, state, (keys.reshape(-1, step, HEAD_DIM), values.reshape(-1, step, HEAD_DIM))
    )
    return (state[2] / state[1]).astype(BF16)


def exchange(value):
    return lax.all_to_all(value, "blk", split_axis=0, concat_axis=0, tiled=True)


def attention_shared(mine, other, norm_gain, qkv_weight, slices):
    rows = mine.shape[0]
    width = qkv_weight.shape[2]
    heads = width // HEAD_DIM
    blocks = heads * slices
    share = rows // slices
    queries, keys, values = call(
        plain_qkv_kernel, [((rows, width), BF16)] * 3, (mine, other, norm_gain, qkv_weight)
    )
    query_send = jnp.transpose(
        queries.reshape(slices, share, heads, HEAD_DIM), (2, 0, 1, 3)
    ).reshape(blocks, share * HEAD_DIM)
    pair = jnp.concatenate(
        (keys.reshape(rows, heads, HEAD_DIM), values.reshape(rows, heads, HEAD_DIM)), axis=2
    )
    pair = jnp.transpose(pair, (1, 0, 2))
    pair_send = jnp.broadcast_to(pair[:, None], (heads, slices, rows, 2 * HEAD_DIM)).reshape(
        blocks, rows, 2 * HEAD_DIM
    )
    query_got = exchange(query_send).reshape(blocks * share, HEAD_DIM)
    pair_got = exchange(pair_send).reshape(blocks * rows, 2 * HEAD_DIM)
    one_head = attend_shared(query_got, pair_got[:, :HEAD_DIM], pair_got[:, HEAD_DIM:])
    back = exchange(one_head.reshape(blocks, share * HEAD_DIM))
    return jnp.transpose(back.reshape(heads, slices, share, HEAD_DIM), (1, 2, 0, 3)).reshape(
        rows, width
    )


def body(tokens, norm_gain, qkv_weight, out_weight, lateral_weight, conv_weight, level_gains):
    rows, half = tokens.shape
    features = out_weight.shape[1]
    width = qkv_weight.shape[2]
    heads = width // HEAD_DIM
    blocks = lax.axis_size("blk")
    cores = lax.axis_size("head")
    grid_rows = rows // GRID_COLS
    cols = GRID_COLS // cores
    channels = lateral_weight.shape[2]
    window = 2 * GRID_COLS // 3
    swap = [(i, cores - 1 - i) for i in range(cores)]

    other = lax.ppermute(tokens, "head", swap)
    (tokens,) = call(intake_kernel, [(tokens.shape, F32)], (tokens,), flops=MIB * 1024)
    other, tokens = lax.optimization_barrier((other, tokens))
    term_out = ((grid_rows, window, features), BF16)
    out_flops = 2 * grid_rows * window * width * features
    if 4 <= blocks <= heads:
        order = list(range(0, blocks, 2)) + list(range(blocks - 1, 0, -2))
        forth = [(order[i - 1], order[i]) for i in range(blocks)]
        back = [(target, source) for source, target in forth]
        mine, across_core = call(
            norm_kernel, [((rows, half), BF16)] * 2, (tokens, other, norm_gain)
        )
        pairs = width // LANES
        state_outs = [
            ((pairs, 2 * rows, LANES), F32),
            ((pairs, 2 * rows, LANES), F32),
            ((pairs, rows, LANES), F32),
        ]
        ahead = lax.ppermute(mine, "blk", forth)
        behind = lax.ppermute(mine, "blk", back)
        unit = 4 * rows * width * (features + rows)
        queries, *state = call(
            own_kernel,
            [((pairs, 2 * rows, LANES), BF16)] + state_outs,
            (mine, across_core, qkv_weight),
            flops=unit + 2 * rows * width * features,
            exps=heads * rows * rows,
        )
        last = blocks // 2
        for step in range(1, last + 1):
            ahead, state[0] = lax.optimization_barrier((ahead, state[0]))
            behind, state[0] = lax.optimization_barrier((behind, state[0]))
            arrived = ahead, behind
            (mark,) = call(mark_kernel, [((16, LANES), BF16)], (ahead,))
            if step == last - 1:
                ahead, behind = ahead[: rows // 2], behind[rows // 2 :]
            if step < last:
                ahead = lax.ppermute(ahead, "blk", forth)
                behind = lax.ppermute(behind, "blk", back)
            traded = (
                lax.ppermute(arrived[0], "head", swap), lax.ppermute(arrived[1], "head", swap)
            )
            if step == last:
                break
            for block in zip(arrived, traded):
                state = call(
                    step_kernel,
                    state_outs,
                    block + (qkv_weight, queries) + tuple(state) + (mark,),
                    flops=unit,
                    exps=heads * rows * rows,
                )
            state = list(state)
        keys, values = call(
            half_kernel,
            [((rows, width), F32)] * 2,
            arrived + (qkv_weight, mark),
            flops=2 * rows * width * features,
        )
        peer_term, attended = call(
            last_kernel,
            [term_out, ((rows, width), BF16)],
            traded + (keys, values, qkv_weight, queries)
            + tuple(state)
            + (out_weight,),
            flops=unit + out_flops,
            exps=heads * rows * rows,
        )
    else:
        attended = attention_shared(tokens, other, norm_gain, qkv_weight, blocks // heads)
        (peer_term,) = call(plain_out_kernel, [term_out], (attended, out_weight), flops=out_flops)
    peer_term = lax.ppermute(peer_term, "head", swap)
    (keep,) = call(
        keep_kernel,
        [((grid_rows, window, features), F32)],
        (attended, out_weight, tokens, other),
        [pltpu.VMEM((grid_rows * window, features), F32)],
        flops=out_flops,
    )

    message = (window + window // 2, channels)
    first, second = call(
        lateral_kernel,
        [(message, BF16), (message, BF16)],
        (keep, peer_term, lateral_weight, level_gains),
        [
            pltpu.VMEM((features // LANES, window, LANES), F32),
            pltpu.VMEM((2 * window, channels), BF16),
        ],
        flops=5 * window * features * channels,
    )
    down_then_up = [
        loop
        for low in range(2)
        for loop in [
            [(cores * i + low, cores * (i + 1) + low) for i in range(blocks - 1)]
            + [(cores * (i + 1) + 1 - low, cores * i + 1 - low) for i in range(blocks - 1)]
            + [(cores * (blocks - 1) + low, cores * blocks - 1 - low), (1 - low, low)]
        ]
    ]
    got_second = lax.ppermute(second, ("blk", "head"), down_then_up[1])
    got_first = lax.ppermute(first, ("blk", "head"), down_then_up[0])
    sums = [((2 * window, channels), F32), ((window // 2, channels), F32)]
    own_sums = call(
        own_conv_kernel,
        sums,
        (first, second, conv_weight),
        [pltpu.VMEM((2 * window, channels), BF16)],
        flops=27 * window * channels * channels,
    )
    return call(
        conv_kernel,
        [((grid_rows, cols, channels), BF16), ((grid_rows // 2, cols // 2, channels), BF16)],
        (got_first, got_second, *own_sums, conv_weight, level_gains),
        [pltpu.VMEM((2 * message[0], channels), BF16)]
        + [pltpu.VMEM(shape, dtype) for shape, dtype in sums],
        flops=18 * window * channels * channels,
    )


def solution(mesh):
    in_specs = (
        P(("groups", "blk"), "head"),
        P(),
        P(None, None, "head"),
        P("head", None),
        P(),
        P(),
        P(),
    )
    out_specs = (P(("groups", "blk"), "head", None), P(("groups", "blk"), "head", None))
    return jax.shard_map(body, mesh=mesh, in_specs=in_specs, out_specs=out_specs, check_vma=False)
```

```python
import math

import jax
import jax.numpy as jnp
from jax import lax
from jax.experimental import pallas as pl
from jax.experimental.pallas import tpu as pltpu
from jax.sharding import PartitionSpec as P

HEAD_DIM = 64
LANES = 128
GRID_COLS = 96
EPS = 1e-06
BF16 = jnp.bfloat16
F32 = jnp.float32
MIB = 1024 * 1024


def specs(count, space):
    return [pl.BlockSpec(memory_space=space)] * count


def nbytes(*arrays):
    return sum(math.prod(a.shape) * jnp.dtype(a.dtype).itemsize for a in arrays)


def call(kernel, outs, args, scratch=(), flops=0, exps=0, out_space=pltpu.VMEM):
    outs = tuple(jax.ShapeDtypeStruct(shape, dtype) for shape, dtype in outs)
    return pl.pallas_call(
        kernel,
        out_shape=outs,
        in_specs=specs(len(args), pltpu.VMEM),
        out_specs=tuple(specs(len(outs), out_space)),
        scratch_shapes=list(scratch),
        compiler_params=pltpu.CompilerParams(vmem_limit_bytes=24 * MIB),
        cost_estimate=pl.CostEstimate(
            flops=flops, transcendentals=exps, bytes_accessed=nbytes(*args, *outs)
        ),
    )(*args)


def layer_norm(values_in, gain_row):
    mean_row = jnp.mean(values_in, axis=-1, keepdims=True)
    centred = values_in - mean_row
    spread = jnp.mean(centred * centred, axis=-1, keepdims=True)
    return centred * lax.rsqrt(spread + EPS) * gain_row


def dot(a, b):
    return jnp.dot(a, b, preferred_element_type=F32)


def low_lanes(shape):
    return lax.broadcasted_iota(jnp.int32, shape, len(shape) - 1) % LANES < HEAD_DIM


def normalize(mine_ref, other_ref, gain_ref):
    half = mine_ref.shape[1]
    width = 2 * half
    mine, other = mine_ref[...], other_ref[...]
    mean = (
        jnp.sum(mine, axis=-1, keepdims=True) + jnp.sum(other, axis=-1, keepdims=True)
    ) / width
    mine, other = mine - mean, other - mean
    spread = (
        jnp.sum(mine * mine, axis=-1, keepdims=True)
        + jnp.sum(other * other, axis=-1, keepdims=True)
    ) / width
    scale = lax.rsqrt(spread + EPS)
    low_gain, high_gain = gain_ref[:half][None, :], gain_ref[half:][None, :]
    first = lax.axis_index("head") == 0
    mine = (mine * scale * jnp.where(first, low_gain, high_gain)).astype(BF16)
    other = (other * scale * jnp.where(first, high_gain, low_gain)).astype(BF16)
    return mine, other


def intake_kernel(tokens_ref, tokens_out):
    tokens_out[...] = tokens_ref[...]


def norm_kernel(mine_ref, other_ref, gain_ref, mine_out, other_out):
    mine_out[...], other_out[...] = normalize(mine_ref, other_ref, gain_ref)


def project(mine, other, weight_ref, part):
    core = lax.axis_index("head")
    half = mine.shape[1]
    mine_at = pl.ds(pl.multiple_of(core * half, half), half)
    other_at = pl.ds(pl.multiple_of((1 - core) * half, half), half)
    return (
        dot(mine, weight_ref[part, mine_at, :]) + dot(other, weight_ref[part, other_at, :])
    ).astype(BF16)


def plain_qkv_kernel(mine_ref, other_ref, gain_ref, weight_ref, *out_refs):
    mine, other = normalize(mine_ref, other_ref, gain_ref)
    for part, ref in enumerate(out_refs):
        ref[...] = project(mine, other, weight_ref, part)


def spread_lanes(column, width=LANES):
    return jnp.broadcast_to(column, (column.shape[0], width))


def across(lanes, width):
    whole, rest = divmod(width, LANES)
    return jnp.concatenate([lanes] * whole + ([lanes[:, :rest]] if rest else []), axis=1)


def absorb(pair, queries, keys, values, old):
    factor = HEAD_DIM ** (-0.5) * math.log2(math.e)
    cols = slice(pair * LANES, (pair + 1) * LANES)
    scores = lax.dot_general(
        queries, keys[:, cols], (((1,), (1,)), ((), ())), preferred_element_type=F32
    )
    top = spread_lanes(jnp.max(scores, axis=-1, keepdims=True))
    if old is not None:
        old_top, old_total, old_mixed = old
        top = jnp.maximum(top, old_top)
    weights = jnp.exp2((scores - across(top, scores.shape[1])) * factor)
    total = spread_lanes(jnp.sum(weights, axis=-1, keepdims=True))
    mixed = dot(weights.astype(BF16), values[:, cols])
    rows = mixed.shape[0] // 2
    low = low_lanes((rows, LANES))
    mixed = jnp.where(low, mixed[:rows], mixed[rows:])
    if old is not None:
        shrink = jnp.exp2((old_top - top) * factor)
        total = total + old_total * shrink
        mixed = mixed + old_mixed * jnp.where(low, shrink[:rows], shrink[rows:])
    return top, total, mixed


def own_kernel(
    mine_ref, other_ref, weight_ref, query_ref, top_ref, total_ref, mixed_ref
):
    mine, other = mine_ref[...], other_ref[...]
    rows = mine.shape[0]
    queries = project(mine, other, weight_ref, 0)
    keys = project(mine, other, weight_ref, 1)
    values = project(mine, other, weight_ref, 2)
    low = low_lanes((rows, LANES))
    for pair in range(query_ref.shape[0]):
        tile = queries[:, pair * LANES : (pair + 1) * LANES]
        query_ref[pair, :rows] = jnp.where(low, tile, jnp.zeros_like(tile))
        query_ref[pair, rows:] = jnp.where(low, jnp.zeros_like(tile), tile)
        top_ref[pair], total_ref[pair], mixed_ref[pair] = absorb(
            pair, query_ref[pair], keys, values, None
        )


def absorb_keys(keys, values, query_ref, top_ref, total_ref, mixed_ref):
    for pair in range(query_ref.shape[0]):
        old = top_ref[pair], total_ref[pair], mixed_ref[pair]
        yield pair, absorb(pair, query_ref[pair], keys, values, old)


def mark_kernel(block_ref, mark_ref):
    mark_ref[...] = block_ref[: mark_ref.shape[0], : mark_ref.shape[1]]


def step_kernel(
    mine_ref,
    other_ref,
    weight_ref,
    query_ref,
    top_ref,
    total_ref,
    mixed_ref,
    mark_ref,
    top_out,
    total_out,
    mixed_out,
):
    mine, other = mine_ref[...], other_ref[...]
    keys = project(mine, other, weight_ref, 1)
    values = project(mine, other, weight_ref, 2)
    for pair, state in absorb_keys(keys, values, query_ref, top_ref, total_ref, mixed_ref):
        top_out[pair], total_out[pair], mixed_out[pair] = state


def half_kernel(mine_a, mine_b, weight_ref, mark_ref, keys_ref, values_ref):
    mine = jnp.concatenate([mine_a[...], mine_b[...]], axis=0)
    half = mine.shape[1]
    here = pl.ds(pl.multiple_of(lax.axis_index("head") * half, half), half)
    keys_ref[...] = dot(mine, weight_ref[1, here, :])
    values_ref[...] = dot(mine, weight_ref[2, here, :])


def send_terms(att_ref, weight_ref, send_ref):
    grid_rows, window = send_ref.shape[:2]
    shift = (1 - lax.axis_index("head")) * (GRID_COLS - window)
    cells = jnp.concatenate(
        [
            att_ref[pl.ds(pl.multiple_of(row * GRID_COLS + shift, 32), window), :]
            for row in range(grid_rows)
        ],
        axis=0,
    )
    send_ref[...] = dot(cells, weight_ref[...]).astype(BF16).reshape(send_ref.shape)


def keep_kernel(att_ref, weight_ref, mine_ref, other_ref, keep_ref, full_ref):
    core = lax.axis_index("head")
    grid_rows, window = keep_ref.shape[:2]
    half = mine_ref.shape[1]
    shift = core * (GRID_COLS - window)
    places = [
        pl.ds(pl.multiple_of(row * GRID_COLS + shift, 32), window) for row in range(grid_rows)
    ]
    cells = jnp.concatenate([att_ref[here, :] for here in places], axis=0)
    full_ref[...] = dot(cells, weight_ref[...])
    for row, here in enumerate(places):
        there = slice(row * window, (row + 1) * window)
        for part, ref in ((core, mine_ref), (1 - core, other_ref)):
            cols = pl.ds(pl.multiple_of(part * half, half), half)
            keep_ref[row, :, cols] = full_ref[there, cols] + ref[here, :]


def last_kernel(
    other_a,
    other_b,
    keys_ref,
    values_ref,
    weight_ref,
    query_ref,
    top_ref,
    total_ref,
    mixed_ref,
    out_weight_ref,
    send_ref,
    att_ref,
):
    rows = mixed_ref.shape[1]
    low = low_lanes((rows, LANES))
    other = jnp.concatenate([other_a[...], other_b[...]], axis=0)
    half = other.shape[1]
    there = pl.ds(pl.multiple_of((1 - lax.axis_index("head")) * half, half), half)
    keys = (keys_ref[...] + dot(other, weight_ref[1, there, :])).astype(BF16)
    values = (values_ref[...] + dot(other, weight_ref[2, there, :])).astype(BF16)
    for pair, (_, total, mixed) in absorb_keys(
        keys, values, query_ref, top_ref, total_ref, mixed_ref
    ):
        cols = slice(pair * LANES, (pair + 1) * LANES)
        att_ref[:, cols] = (mixed / jnp.where(low, total[:rows], total[rows:])).astype(BF16)
    send_terms(att_ref, out_weight_ref, send_ref)


def plain_out_kernel(att_ref, weight_ref, send_ref):
    send_terms(att_ref, weight_ref, send_ref)


def lateral_kernel(
    keep_ref, got_ref, lateral_ref, gain_ref, first_ref, second_ref, pool_ref, fine_ref
):
    core = lax.axis_index("head")
    window, features = keep_ref.shape[1], keep_ref.shape[2]
    cells = (keep_ref[...] + got_ref[...].astype(F32)).astype(BF16)
    fine_ref[...] = layer_norm(
        dot(cells.reshape(2 * window, features), lateral_ref[0]), gain_ref[0, 0][None, :]
    ).astype(BF16)
    first_ref[:window] = fine_ref[pl.ds(pl.multiple_of((1 - core) * window, window), window), :]
    second_ref[:window] = fine_ref[pl.ds(pl.multiple_of(core * window, window), window), :]
    tall = jnp.maximum(cells[0].astype(F32), cells[1].astype(F32))
    pooled = []
    for part in range(features // LANES):
        pool_ref[part] = tall[:, part * LANES : (part + 1) * LANES]
        even = pool_ref[part, pl.ds(0, window // 2, stride=2), :]
        odd = pool_ref[part, pl.ds(1, window // 2, stride=2), :]
        pooled.append(jnp.maximum(even, odd).astype(BF16))
    pooled = jnp.concatenate(pooled, axis=1)
    coarse = layer_norm(dot(pooled, lateral_ref[1]), gain_ref[1, 0][None, :]).astype(BF16)
    first_ref[window:] = coarse
    second_ref[window:] = coarse


def joined(terms, window):
    left, middle, right = (terms(tap_col) for tap_col in range(3))
    block = middle.shape[0]
    place = lax.broadcasted_iota(jnp.int32, middle.shape, 0) % window
    left = jnp.where(place == 0, 0.0, pltpu.roll(left, 1, axis=0))
    right = jnp.where(place == window - 1, 0.0, pltpu.roll(right, block - 1, axis=0))
    return left + middle + right


def own_conv_kernel(first_ref, second_ref, weight_ref, fine_ref, coarse_ref, fine_in):
    core = lax.axis_index("head")
    window = fine_ref.shape[0] // 2
    for ref, place in ((first_ref, 1 - core), (second_ref, core)):
        fine_in[pl.ds(pl.multiple_of(place * window, window), window), :] = ref[:window]
    coarse = first_ref[window:]

    def fine_terms(tap_col):
        to_lower = dot(fine_in[:window], weight_ref[0, 0, tap_col])
        to_upper = dot(fine_in[window:], weight_ref[0, 2, tap_col])
        return dot(fine_in[...], weight_ref[0, 1, tap_col]) + jnp.concatenate(
            [to_upper, to_lower], axis=0
        )

    fine_ref[...] = joined(fine_terms, window)
    coarse_ref[...] = joined(lambda tap_col: dot(coarse, weight_ref[1, 1, tap_col]), window // 2)


def conv_kernel(
    got_first_ref,
    got_second_ref,
    own_fine_ref,
    own_coarse_ref,
    weight_ref,
    gain_ref,
    fine_ref,
    coarse_ref,
    edge_in,
    fine_sum,
    coarse_sum,
    fine_out,
    coarse_out,
    sems,
):
    core = lax.axis_index("head")
    block = lax.axis_index("blk")
    edge = (0, lax.axis_size("blk") - 1)
    window = fine_sum.shape[0] // 2
    rows = got_first_ref.shape[0]
    for ref, place in ((got_first_ref, core), (got_second_ref, 1 - core)):
        inside = block != jnp.where(place == 0, *edge)
        edge_in[pl.ds(pl.multiple_of(place * rows, 32), rows), :] = jnp.where(
            inside, ref[...].astype(F32), 0.0
        ).astype(BF16)

    def fine_terms(tap_col):
        return jnp.concatenate(
            [
                dot(edge_in[:window], weight_ref[0, 0, tap_col]),
                dot(edge_in[rows : rows + window], weight_ref[0, 2, tap_col]),
            ],
            axis=0,
        )

    def coarse_terms(tap_col):
        return dot(edge_in[window:rows], weight_ref[1, 0, tap_col]) + dot(
            edge_in[rows + window :], weight_ref[1, 2, tap_col]
        )

    cols = fine_ref.shape[1]
    shift = GRID_COLS - window
    inset = cols - shift
    copies = [
        pltpu.make_async_copy(source.at[row], target.at[row], sems.at[place])
        for place, (source, target, row) in enumerate(
            [(fine_out, fine_ref, 0), (fine_out, fine_ref, 1), (coarse_out, coarse_ref, 0)]
        )
    ]
    fine_sum[...] = own_fine_ref[...] + joined(fine_terms, window)
    for row in range(2):
        here = pl.ds(pl.multiple_of(row * window + core * inset, 8), cols)
        fine_out[row] = layer_norm(fine_sum[here, :], gain_ref[0, 1][None, :]).astype(BF16)
        copies[row].start()
    coarse_sum[...] = own_coarse_ref[...] + joined(coarse_terms, window // 2)
    here = pl.ds(pl.multiple_of(core * (inset // 2), 8), cols // 2)
    coarse_out[0] = layer_norm(coarse_sum[here, :], gain_ref[1, 1][None, :]).astype(BF16)
    copies[2].start()
    for copy in copies:
        copy.wait()


def attend_shared(queries, keys, values):
    factor = HEAD_DIM ** (-0.5)
    step = math.gcd(keys.shape[0], 1536)
    rows = queries.shape[0]

    def block(state, pair):
        running, totals, weighted = state
        key, value = pair
        scores = (
            lax.dot_general(queries, key, (((1,), (1,)), ((), ())), preferred_element_type=F32)
            * factor
        )
        newmax = jnp.maximum(running, jnp.max(scores, axis=-1, keepdims=True))
        weights = jnp.exp(scores - newmax)
        shrink = jnp.exp(running - newmax)
        totals = totals * shrink + jnp.sum(weights, axis=-1, keepdims=True)
        weighted = weighted * shrink + dot(weights.astype(BF16), value)
        return (newmax, totals, weighted), None

    state = (
        jnp.full((rows, 1), -jnp.inf, F32),
        jnp.zeros((rows, 1), F32),
        jnp.zeros((rows, HEAD_DIM), F32),
    )
    state, _ = lax.scan(
        block, state, (keys.reshape(-1, step, HEAD_DIM), values.reshape(-1, step, HEAD_DIM))
    )
    return (state[2] / state[1]).astype(BF16)


def exchange(value):
    return lax.all_to_all(value, "blk", split_axis=0, concat_axis=0, tiled=True)


def attention_shared(mine, other, norm_gain, qkv_weight, slices):
    rows = mine.shape[0]
    width = qkv_weight.shape[2]
    heads = width // HEAD_DIM
    blocks = heads * slices
    share = rows // slices
    queries, keys, values = call(
        plain_qkv_kernel, [((rows, width), BF16)] * 3, (mine, other, norm_gain, qkv_weight)
    )
    query_send = jnp.transpose(
        queries.reshape(slices, share, heads, HEAD_DIM), (2, 0, 1, 3)
    ).reshape(blocks, share * HEAD_DIM)
    pair = jnp.concatenate(
        (keys.reshape(rows, heads, HEAD_DIM), values.reshape(rows, heads, HEAD_DIM)), axis=2
    )
    pair = jnp.transpose(pair, (1, 0, 2))
    pair_send = jnp.broadcast_to(pair[:, None], (heads, slices, rows, 2 * HEAD_DIM)).reshape(
        blocks, rows, 2 * HEAD_DIM
    )
    query_got = exchange(query_send).reshape(blocks * share, HEAD_DIM)
    pair_got = exchange(pair_send).reshape(blocks * rows, 2 * HEAD_DIM)
    one_head = attend_shared(query_got, pair_got[:, :HEAD_DIM], pair_got[:, HEAD_DIM:])
    back = exchange(one_head.reshape(blocks, share * HEAD_DIM))
    return jnp.transpose(back.reshape(heads, slices, share, HEAD_DIM), (1, 2, 0, 3)).reshape(
        rows, width
    )


def body(tokens, norm_gain, qkv_weight, out_weight, lateral_weight, conv_weight, level_gains):
    rows, half = tokens.shape
    features = out_weight.shape[1]
    width = qkv_weight.shape[2]
    heads = width // HEAD_DIM
    blocks = lax.axis_size("blk")
    cores = lax.axis_size("head")
    grid_rows = rows // GRID_COLS
    cols = GRID_COLS // cores
    channels = lateral_weight.shape[2]
    window = 2 * GRID_COLS // 3
    swap = [(i, cores - 1 - i) for i in range(cores)]

    other = lax.ppermute(tokens, "head", swap)
    (tokens,) = call(intake_kernel, [(tokens.shape, F32)], (tokens,), flops=MIB * 1024)
    other, tokens = lax.optimization_barrier((other, tokens))
    term_out = ((grid_rows, window, features), BF16)
    out_flops = 2 * grid_rows * window * width * features
    if 4 <= blocks <= heads:
        order = list(range(0, blocks, 2)) + list(range(blocks - 1, 0, -2))
        forth = [(order[i - 1], order[i]) for i in range(blocks)]
        back = [(target, source) for source, target in forth]
        mine, across_core = call(
            norm_kernel, [((rows, half), BF16)] * 2, (tokens, other, norm_gain)
        )
        pairs = width // LANES
        state_outs = [
            ((pairs, 2 * rows, LANES), F32),
            ((pairs, 2 * rows, LANES), F32),
            ((pairs, rows, LANES), F32),
        ]
        ahead = lax.ppermute(mine, "blk", forth)
        behind = lax.ppermute(mine, "blk", back)
        unit = 4 * rows * width * (features + rows)
        queries, *state = call(
            own_kernel,
            [((pairs, 2 * rows, LANES), BF16)] + state_outs,
            (mine, across_core, qkv_weight),
            flops=unit + 2 * rows * width * features,
            exps=heads * rows * rows,
        )
        last = blocks // 2
        cut = 2 * rows // 3
        for step in range(1, last + 1):
            ahead, state[0] = lax.optimization_barrier((ahead, state[0]))
            behind, state[0] = lax.optimization_barrier((behind, state[0]))
            arrived = ahead, behind
            (mark,) = call(mark_kernel, [((16, LANES), BF16)], (ahead,))
            if step == last - 1:
                ahead, behind = ahead[:cut], behind[cut:]
            if step < last:
                ahead = lax.ppermute(ahead, "blk", forth)
                behind = lax.ppermute(behind, "blk", back)
            traded = (
                lax.ppermute(arrived[0], "head", swap), lax.ppermute(arrived[1], "head", swap)
            )
            if step == last:
                break
            for block in zip(arrived, traded):
                state = call(
                    step_kernel,
                    state_outs,
                    block + (qkv_weight, queries) + tuple(state) + (mark,),
                    flops=unit,
                    exps=heads * rows * rows,
                )
            state = list(state)
        keys, values = call(
            half_kernel,
            [((rows, width), F32)] * 2,
            arrived + (qkv_weight, mark),
            flops=2 * rows * width * features,
        )
        peer_term, attended = call(
            last_kernel,
            [term_out, ((rows, width), BF16)],
            traded + (keys, values, qkv_weight, queries)
            + tuple(state)
            + (out_weight,),
            flops=unit + out_flops,
            exps=heads * rows * rows,
        )
    else:
        attended = attention_shared(tokens, other, norm_gain, qkv_weight, blocks // heads)
        (peer_term,) = call(plain_out_kernel, [term_out], (attended, out_weight), flops=out_flops)
    peer_term = lax.ppermute(peer_term, "head", swap)
    (keep,) = call(
        keep_kernel,
        [((grid_rows, window, features), F32)],
        (attended, out_weight, tokens, other),
        [pltpu.VMEM((grid_rows * window, features), F32)],
        flops=out_flops,
    )

    message = (window + window // 2, channels)
    first, second = call(
        lateral_kernel,
        [(message, BF16), (message, BF16)],
        (keep, peer_term, lateral_weight, level_gains),
        [
            pltpu.VMEM((features // LANES, window, LANES), F32),
            pltpu.VMEM((2 * window, channels), BF16),
        ],
        flops=5 * window * features * channels,
    )
    down_then_up = [
        loop
        for low in range(2)
        for loop in [
            [(cores * i + low, cores * (i + 1) + low) for i in range(blocks - 1)]
            + [(cores * (i + 1) + 1 - low, cores * i + 1 - low) for i in range(blocks - 1)]
            + [(cores * (blocks - 1) + low, cores * blocks - 1 - low), (1 - low, low)]
        ]
    ]
    got_second = lax.ppermute(second, ("blk", "head"), down_then_up[1])
    got_first = lax.ppermute(first, ("blk", "head"), down_then_up[0])
    sums = [((2 * window, channels), F32), ((window // 2, channels), F32)]
    own_sums = call(
        own_conv_kernel,
        sums,
        (first, second, conv_weight),
        [pltpu.VMEM((2 * window, channels), BF16)],
        flops=27 * window * channels * channels,
    )
    outs = [
        ((grid_rows, cols, channels), BF16),
        ((grid_rows // 2, cols // 2, channels), BF16),
    ]
    scratch = [pltpu.VMEM(shape, dtype) for shape, dtype in sums + outs]
    return call(
        conv_kernel,
        outs,
        (got_first, got_second, *own_sums, conv_weight, level_gains),
        [pltpu.VMEM((2 * message[0], channels), BF16)]
        + scratch
        + [pltpu.SemaphoreType.DMA((3,))],
        flops=18 * window * channels * channels,
        out_space=pl.ANY,
    )


def solution(mesh):
    in_specs = (
        P(("groups", "blk"), "head"),
        P(),
        P(None, None, "head"),
        P("head", None),
        P(),
        P(),
        P(),
    )
    out_specs = (P(("groups", "blk"), "head", None), P(("groups", "blk"), "head", None))
    return jax.shard_map(body, mesh=mesh, in_specs=in_specs, out_specs=out_specs, check_vma=False)
```

```python
import math

import jax
import jax.numpy as jnp
from jax import lax
from jax.experimental import pallas as pl
from jax.experimental.pallas import tpu as pltpu
from jax.sharding import PartitionSpec as P

HEAD_DIM = 64
LANES = 128
GRID_COLS = 96
EPS = 1e-06
BF16 = jnp.bfloat16
F32 = jnp.float32
MIB = 1024 * 1024


def specs(count):
    return [pl.BlockSpec(memory_space=pltpu.VMEM)] * count


def nbytes(*arrays):
    return sum(math.prod(a.shape) * jnp.dtype(a.dtype).itemsize for a in arrays)


def call(kernel, outs, args, scratch=(), flops=0, exps=0):
    outs = tuple(jax.ShapeDtypeStruct(shape, dtype) for shape, dtype in outs)
    return pl.pallas_call(
        kernel,
        out_shape=outs,
        in_specs=specs(len(args)),
        out_specs=tuple(specs(len(outs))),
        scratch_shapes=list(scratch),
        compiler_params=pltpu.CompilerParams(vmem_limit_bytes=24 * MIB),
        cost_estimate=pl.CostEstimate(
            flops=flops, transcendentals=exps, bytes_accessed=nbytes(*args, *outs)
        ),
    )(*args)


def layer_norm(values_in, gain_row):
    mean_row = jnp.mean(values_in, axis=-1, keepdims=True)
    centred = values_in - mean_row
    spread = jnp.mean(centred * centred, axis=-1, keepdims=True)
    return centred * lax.rsqrt(spread + EPS) * gain_row


def dot(a, b):
    return jnp.dot(a, b, preferred_element_type=F32)


def low_lanes(shape):
    return lax.broadcasted_iota(jnp.int32, shape, len(shape) - 1) % LANES < HEAD_DIM


def normalize(mine_ref, other_ref, gain_ref):
    half = mine_ref.shape[1]
    width = 2 * half
    mine, other = mine_ref[...], other_ref[...]
    mean = (
        jnp.sum(mine, axis=-1, keepdims=True) + jnp.sum(other, axis=-1, keepdims=True)
    ) / width
    mine, other = mine - mean, other - mean
    spread = (
        jnp.sum(mine * mine, axis=-1, keepdims=True)
        + jnp.sum(other * other, axis=-1, keepdims=True)
    ) / width
    scale = lax.rsqrt(spread + EPS)
    low_gain, high_gain = gain_ref[:half][None, :], gain_ref[half:][None, :]
    first = lax.axis_index("head") == 0
    mine = (mine * scale * jnp.where(first, low_gain, high_gain)).astype(BF16)
    other = (other * scale * jnp.where(first, high_gain, low_gain)).astype(BF16)
    return mine, other


def intake_kernel(tokens_ref, tokens_out):
    tokens_out[...] = tokens_ref[...]


def norm_kernel(mine_ref, other_ref, gain_ref, mine_out, other_out):
    mine_out[...], other_out[...] = normalize(mine_ref, other_ref, gain_ref)


def project(mine, other, weight_ref, part):
    core = lax.axis_index("head")
    half = mine.shape[1]
    mine_at = pl.ds(pl.multiple_of(core * half, half), half)
    other_at = pl.ds(pl.multiple_of((1 - core) * half, half), half)
    return (
        dot(mine, weight_ref[part, mine_at, :]) + dot(other, weight_ref[part, other_at, :])
    ).astype(BF16)


def plain_qkv_kernel(mine_ref, other_ref, gain_ref, weight_ref, *out_refs):
    mine, other = normalize(mine_ref, other_ref, gain_ref)
    for part, ref in enumerate(out_refs):
        ref[...] = project(mine, other, weight_ref, part)


def spread_lanes(column, width=LANES):
    return jnp.broadcast_to(column, (column.shape[0], width))


def across(lanes, width):
    whole, rest = divmod(width, LANES)
    return jnp.concatenate([lanes] * whole + ([lanes[:, :rest]] if rest else []), axis=1)


def absorb(pair, queries, keys, values, old):
    factor = HEAD_DIM ** (-0.5) * math.log2(math.e)
    cols = slice(pair * LANES, (pair + 1) * LANES)
    scores = lax.dot_general(
        queries, keys[:, cols], (((1,), (1,)), ((), ())), preferred_element_type=F32
    )
    top = spread_lanes(jnp.max(scores, axis=-1, keepdims=True))
    if old is not None:
        old_top, old_total, old_mixed = old
        top = jnp.maximum(top, old_top)
    weights = jnp.exp2((scores - across(top, scores.shape[1])) * factor)
    total = spread_lanes(jnp.sum(weights, axis=-1, keepdims=True))
    mixed = dot(weights.astype(BF16), values[:, cols])
    rows = mixed.shape[0] // 2
    low = low_lanes((rows, LANES))
    mixed = jnp.where(low, mixed[:rows], mixed[rows:])
    if old is not None:
        shrink = jnp.exp2((old_top - top) * factor)
        total = total + old_total * shrink
        mixed = mixed + old_mixed * jnp.where(low, shrink[:rows], shrink[rows:])
    return top, total, mixed


def own_kernel(
    mine_ref, other_ref, weight_ref, query_ref, top_ref, total_ref, mixed_ref
):
    mine, other = mine_ref[...], other_ref[...]
    rows = mine.shape[0]
    queries = project(mine, other, weight_ref, 0)
    keys = project(mine, other, weight_ref, 1)
    values = project(mine, other, weight_ref, 2)
    low = low_lanes((rows, LANES))
    for pair in range(query_ref.shape[0]):
        tile = queries[:, pair * LANES : (pair + 1) * LANES]
        query_ref[pair, :rows] = jnp.where(low, tile, jnp.zeros_like(tile))
        query_ref[pair, rows:] = jnp.where(low, jnp.zeros_like(tile), tile)
        top_ref[pair], total_ref[pair], mixed_ref[pair] = absorb(
            pair, query_ref[pair], keys, values, None
        )


def absorb_keys(keys, values, query_ref, top_ref, total_ref, mixed_ref):
    for pair in range(query_ref.shape[0]):
        old = top_ref[pair], total_ref[pair], mixed_ref[pair]
        yield pair, absorb(pair, query_ref[pair], keys, values, old)


def mark_kernel(block_ref, mark_ref):
    mark_ref[...] = block_ref[: mark_ref.shape[0], : mark_ref.shape[1]]


def step_kernel(
    mine_ref,
    other_ref,
    weight_ref,
    query_ref,
    top_ref,
    total_ref,
    mixed_ref,
    mark_ref,
    top_out,
    total_out,
    mixed_out,
):
    mine, other = mine_ref[...], other_ref[...]
    keys = project(mine, other, weight_ref, 1)
    values = project(mine, other, weight_ref, 2)
    for pair, state in absorb_keys(keys, values, query_ref, top_ref, total_ref, mixed_ref):
        top_out[pair], total_out[pair], mixed_out[pair] = state


def half_kernel(mine_a, mine_b, weight_ref, mark_ref, keys_ref, values_ref):
    mine = jnp.concatenate([mine_a[...], mine_b[...]], axis=0)
    half = mine.shape[1]
    here = pl.ds(pl.multiple_of(lax.axis_index("head") * half, half), half)
    keys_ref[...] = dot(mine, weight_ref[1, here, :])
    values_ref[...] = dot(mine, weight_ref[2, here, :])


def send_terms(att_ref, weight_ref, send_ref):
    grid_rows, window = send_ref.shape[:2]
    shift = (1 - lax.axis_index("head")) * (GRID_COLS - window)
    cells = jnp.concatenate(
        [
            att_ref[pl.ds(pl.multiple_of(row * GRID_COLS + shift, 32), window), :]
            for row in range(grid_rows)
        ],
        axis=0,
    )
    send_ref[...] = dot(cells, weight_ref[...]).astype(BF16).reshape(send_ref.shape)


def keep_kernel(att_ref, weight_ref, mine_ref, other_ref, keep_ref, full_ref):
    core = lax.axis_index("head")
    grid_rows, window = keep_ref.shape[:2]
    half = mine_ref.shape[1]
    shift = core * (GRID_COLS - window)
    places = [
        pl.ds(pl.multiple_of(row * GRID_COLS + shift, 32), window) for row in range(grid_rows)
    ]
    cells = jnp.concatenate([att_ref[here, :] for here in places], axis=0)
    full_ref[...] = dot(cells, weight_ref[...])
    for row, here in enumerate(places):
        there = slice(row * window, (row + 1) * window)
        for part, ref in ((core, mine_ref), (1 - core, other_ref)):
            cols = pl.ds(pl.multiple_of(part * half, half), half)
            keep_ref[row, :, cols] = full_ref[there, cols] + ref[here, :]


def last_kernel(
    other_a,
    other_b,
    keys_ref,
    values_ref,
    weight_ref,
    query_ref,
    top_ref,
    total_ref,
    mixed_ref,
    out_weight_ref,
    send_ref,
    att_ref,
):
    rows = mixed_ref.shape[1]
    low = low_lanes((rows, LANES))
    other = jnp.concatenate([other_a[...], other_b[...]], axis=0)
    half = other.shape[1]
    there = pl.ds(pl.multiple_of((1 - lax.axis_index("head")) * half, half), half)
    keys = (keys_ref[...] + dot(other, weight_ref[1, there, :])).astype(BF16)
    values = (values_ref[...] + dot(other, weight_ref[2, there, :])).astype(BF16)
    for pair, (_, total, mixed) in absorb_keys(
        keys, values, query_ref, top_ref, total_ref, mixed_ref
    ):
        cols = slice(pair * LANES, (pair + 1) * LANES)
        att_ref[:, cols] = (mixed / jnp.where(low, total[:rows], total[rows:])).astype(BF16)
    send_terms(att_ref, out_weight_ref, send_ref)


def plain_out_kernel(att_ref, weight_ref, send_ref):
    send_terms(att_ref, weight_ref, send_ref)


def lateral_kernel(
    keep_ref, got_ref, lateral_ref, gain_ref, first_ref, second_ref, pool_ref, fine_ref
):
    core = lax.axis_index("head")
    window, features = keep_ref.shape[1], keep_ref.shape[2]
    cells = (keep_ref[...] + got_ref[...].astype(F32)).astype(BF16)
    fine_ref[...] = layer_norm(
        dot(cells.reshape(2 * window, features), lateral_ref[0]), gain_ref[0, 0][None, :]
    ).astype(BF16)
    first_ref[:window] = fine_ref[pl.ds(pl.multiple_of((1 - core) * window, window), window), :]
    second_ref[:window] = fine_ref[pl.ds(pl.multiple_of(core * window, window), window), :]
    tall = jnp.maximum(cells[0].astype(F32), cells[1].astype(F32))
    pooled = []
    for part in range(features // LANES):
        pool_ref[part] = tall[:, part * LANES : (part + 1) * LANES]
        even = pool_ref[part, pl.ds(0, window // 2, stride=2), :]
        odd = pool_ref[part, pl.ds(1, window // 2, stride=2), :]
        pooled.append(jnp.maximum(even, odd).astype(BF16))
    pooled = jnp.concatenate(pooled, axis=1)
    coarse = layer_norm(dot(pooled, lateral_ref[1]), gain_ref[1, 0][None, :]).astype(BF16)
    first_ref[window:] = coarse
    second_ref[window:] = coarse


def joined(terms, window):
    left, middle, right = (terms(tap_col) for tap_col in range(3))
    block = middle.shape[0]
    place = lax.broadcasted_iota(jnp.int32, middle.shape, 0) % window
    left = jnp.where(place == 0, 0.0, pltpu.roll(left, 1, axis=0))
    right = jnp.where(place == window - 1, 0.0, pltpu.roll(right, block - 1, axis=0))
    return left + middle + right


def own_conv_kernel(first_ref, second_ref, weight_ref, fine_ref, coarse_ref, fine_in):
    core = lax.axis_index("head")
    window = fine_ref.shape[0] // 2
    for ref, place in ((first_ref, 1 - core), (second_ref, core)):
        fine_in[pl.ds(pl.multiple_of(place * window, window), window), :] = ref[:window]
    coarse = first_ref[window:]

    def fine_terms(tap_col):
        to_lower = dot(fine_in[:window], weight_ref[0, 0, tap_col])
        to_upper = dot(fine_in[window:], weight_ref[0, 2, tap_col])
        return dot(fine_in[...], weight_ref[0, 1, tap_col]) + jnp.concatenate(
            [to_upper, to_lower], axis=0
        )

    fine_ref[...] = joined(fine_terms, window)
    coarse_ref[...] = joined(lambda tap_col: dot(coarse, weight_ref[1, 1, tap_col]), window // 2)


def conv_kernel(
    got_first_ref,
    got_second_ref,
    own_fine_ref,
    own_coarse_ref,
    weight_ref,
    gain_ref,
    fine_ref,
    coarse_ref,
    edge_in,
    fine_sum,
    coarse_sum,
):
    core = lax.axis_index("head")
    block = lax.axis_index("blk")
    edge = (0, lax.axis_size("blk") - 1)
    window = fine_sum.shape[0] // 2
    rows = got_first_ref.shape[0]
    for ref, place in ((got_first_ref, core), (got_second_ref, 1 - core)):
        inside = block != jnp.where(place == 0, *edge)
        edge_in[pl.ds(pl.multiple_of(place * rows, 32), rows), :] = jnp.where(
            inside, ref[...].astype(F32), 0.0
        ).astype(BF16)

    def fine_terms(tap_col):
        return jnp.concatenate(
            [
                dot(edge_in[:window], weight_ref[0, 0, tap_col]),
                dot(edge_in[rows : rows + window], weight_ref[0, 2, tap_col]),
            ],
            axis=0,
        )

    def coarse_terms(tap_col):
        return dot(edge_in[window:rows], weight_ref[1, 0, tap_col]) + dot(
            edge_in[rows + window :], weight_ref[1, 2, tap_col]
        )

    cols = fine_ref.shape[1]
    shift = GRID_COLS - window
    inset = cols - shift
    fine_sum[...] = own_fine_ref[...] + joined(fine_terms, window)
    coarse_sum[...] = own_coarse_ref[...] + joined(coarse_terms, window // 2)
    for row in range(2):
        here = pl.ds(pl.multiple_of(row * window + core * inset, 8), cols)
        fine_ref[row] = layer_norm(fine_sum[here, :], gain_ref[0, 1][None, :]).astype(BF16)
    here = pl.ds(pl.multiple_of(core * (inset // 2), 8), cols // 2)
    coarse_ref[0] = layer_norm(coarse_sum[here, :], gain_ref[1, 1][None, :]).astype(BF16)


def attend_shared(queries, keys, values):
    factor = HEAD_DIM ** (-0.5)
    step = math.gcd(keys.shape[0], 1536)
    rows = queries.shape[0]

    def block(state, pair):
        running, totals, weighted = state
        key, value = pair
        scores = (
            lax.dot_general(queries, key, (((1,), (1,)), ((), ())), preferred_element_type=F32)
            * factor
        )
        newmax = jnp.maximum(running, jnp.max(scores, axis=-1, keepdims=True))
        weights = jnp.exp(scores - newmax)
        shrink = jnp.exp(running - newmax)
        totals = totals * shrink + jnp.sum(weights, axis=-1, keepdims=True)
        weighted = weighted * shrink + dot(weights.astype(BF16), value)
        return (newmax, totals, weighted), None

    state = (
        jnp.full((rows, 1), -jnp.inf, F32),
        jnp.zeros((rows, 1), F32),
        jnp.zeros((rows, HEAD_DIM), F32),
    )
    state, _ = lax.scan(
        block, state, (keys.reshape(-1, step, HEAD_DIM), values.reshape(-1, step, HEAD_DIM))
    )
    return (state[2] / state[1]).astype(BF16)


def exchange(value):
    return lax.all_to_all(value, "blk", split_axis=0, concat_axis=0, tiled=True)


def attention_shared(mine, other, norm_gain, qkv_weight, slices):
    rows = mine.shape[0]
    width = qkv_weight.shape[2]
    heads = width // HEAD_DIM
    blocks = heads * slices
    share = rows // slices
    queries, keys, values = call(
        plain_qkv_kernel, [((rows, width), BF16)] * 3, (mine, other, norm_gain, qkv_weight)
    )
    query_send = jnp.transpose(
        queries.reshape(slices, share, heads, HEAD_DIM), (2, 0, 1, 3)
    ).reshape(blocks, share * HEAD_DIM)
    pair = jnp.concatenate(
        (keys.reshape(rows, heads, HEAD_DIM), values.reshape(rows, heads, HEAD_DIM)), axis=2
    )
    pair = jnp.transpose(pair, (1, 0, 2))
    pair_send = jnp.broadcast_to(pair[:, None], (heads, slices, rows, 2 * HEAD_DIM)).reshape(
        blocks, rows, 2 * HEAD_DIM
    )
    query_got = exchange(query_send).reshape(blocks * share, HEAD_DIM)
    pair_got = exchange(pair_send).reshape(blocks * rows, 2 * HEAD_DIM)
    one_head = attend_shared(query_got, pair_got[:, :HEAD_DIM], pair_got[:, HEAD_DIM:])
    back = exchange(one_head.reshape(blocks, share * HEAD_DIM))
    return jnp.transpose(back.reshape(heads, slices, share, HEAD_DIM), (1, 2, 0, 3)).reshape(
        rows, width
    )


def body(tokens, norm_gain, qkv_weight, out_weight, lateral_weight, conv_weight, level_gains):
    rows, half = tokens.shape
    features = out_weight.shape[1]
    width = qkv_weight.shape[2]
    heads = width // HEAD_DIM
    blocks = lax.axis_size("blk")
    cores = lax.axis_size("head")
    grid_rows = rows // GRID_COLS
    cols = GRID_COLS // cores
    channels = lateral_weight.shape[2]
    window = 2 * GRID_COLS // 3
    swap = [(i, cores - 1 - i) for i in range(cores)]

    other = lax.ppermute(tokens, "head", swap)
    (tokens,) = call(intake_kernel, [(tokens.shape, F32)], (tokens,), flops=MIB * 1024)
    other, tokens = lax.optimization_barrier((other, tokens))
    term_out = ((grid_rows, window, features), BF16)
    out_flops = 2 * grid_rows * window * width * features
    if 4 <= blocks <= heads:
        order = list(range(0, blocks, 2)) + list(range(blocks - 1, 0, -2))
        forth = [(order[i - 1], order[i]) for i in range(blocks)]
        back = [(target, source) for source, target in forth]
        mine, across_core = call(
            norm_kernel, [((rows, half), BF16)] * 2, (tokens, other, norm_gain)
        )
        pairs = width // LANES
        state_outs = [
            ((pairs, 2 * rows, LANES), F32),
            ((pairs, 2 * rows, LANES), F32),
            ((pairs, rows, LANES), F32),
        ]
        ahead = lax.ppermute(mine, "blk", forth)
        behind = lax.ppermute(mine, "blk", back)
        unit = 4 * rows * width * (features + rows)
        queries, *state = call(
            own_kernel,
            [((pairs, 2 * rows, LANES), BF16)] + state_outs,
            (mine, across_core, qkv_weight),
            flops=unit + 2 * rows * width * features,
            exps=heads * rows * rows,
        )
        last = blocks // 2
        cut = 5 * rows // 6
        for step in range(1, last + 1):
            ahead, state[0] = lax.optimization_barrier((ahead, state[0]))
            behind, state[0] = lax.optimization_barrier((behind, state[0]))
            arrived = ahead, behind
            (mark,) = call(mark_kernel, [((16, LANES), BF16)], (ahead,))
            if step == last - 1:
                ahead, behind = ahead[:cut], behind[cut:]
            if step < last:
                ahead = lax.ppermute(ahead, "blk", forth)
                behind = lax.ppermute(behind, "blk", back)
            traded = (
                lax.ppermute(arrived[0], "head", swap), lax.ppermute(arrived[1], "head", swap)
            )
            if step == last:
                break
            for block in zip(arrived, traded):
                state = call(
                    step_kernel,
                    state_outs,
                    block + (qkv_weight, queries) + tuple(state) + (mark,),
                    flops=unit,
                    exps=heads * rows * rows,
                )
            state = list(state)
        keys, values = call(
            half_kernel,
            [((rows, width), F32)] * 2,
            arrived + (qkv_weight, mark),
            flops=2 * rows * width * features,
        )
        peer_term, attended = call(
            last_kernel,
            [term_out, ((rows, width), BF16)],
            traded + (keys, values, qkv_weight, queries)
            + tuple(state)
            + (out_weight,),
            flops=unit + out_flops,
            exps=heads * rows * rows,
        )
    else:
        attended = attention_shared(tokens, other, norm_gain, qkv_weight, blocks // heads)
        (peer_term,) = call(plain_out_kernel, [term_out], (attended, out_weight), flops=out_flops)
    peer_term = lax.ppermute(peer_term, "head", swap)
    (keep,) = call(
        keep_kernel,
        [((grid_rows, window, features), F32)],
        (attended, out_weight, tokens, other),
        [pltpu.VMEM((grid_rows * window, features), F32)],
        flops=out_flops,
    )

    message = (window + window // 2, channels)
    first, second = call(
        lateral_kernel,
        [(message, BF16), (message, BF16)],
        (keep, peer_term, lateral_weight, level_gains),
        [
            pltpu.VMEM((features // LANES, window, LANES), F32),
            pltpu.VMEM((2 * window, channels), BF16),
        ],
        flops=5 * window * features * channels,
    )
    down_then_up = [
        loop
        for low in range(2)
        for loop in [
            [(cores * i + low, cores * (i + 1) + low) for i in range(blocks - 1)]
            + [(cores * (i + 1) + 1 - low, cores * i + 1 - low) for i in range(blocks - 1)]
            + [(cores * (blocks - 1) + low, cores * blocks - 1 - low), (1 - low, low)]
        ]
    ]
    got_second = lax.ppermute(second, ("blk", "head"), down_then_up[1])
    got_first = lax.ppermute(first, ("blk", "head"), down_then_up[0])
    sums = [((2 * window, channels), F32), ((window // 2, channels), F32)]
    own_sums = call(
        own_conv_kernel,
        sums,
        (first, second, conv_weight),
        [pltpu.VMEM((2 * window, channels), BF16)],
        flops=27 * window * channels * channels,
    )
    return call(
        conv_kernel,
        [((grid_rows, cols, channels), BF16), ((grid_rows // 2, cols // 2, channels), BF16)],
        (got_first, got_second, *own_sums, conv_weight, level_gains),
        [pltpu.VMEM((2 * message[0], channels), BF16)]
        + [pltpu.VMEM(shape, dtype) for shape, dtype in sums],
        flops=18 * window * channels * channels,
    )


def solution(mesh):
    in_specs = (
        P(("groups", "blk"), "head"),
        P(),
        P(None, None, "head"),
        P("head", None),
        P(),
        P(),
        P(),
    )
    out_specs = (P(("groups", "blk"), "head", None), P(("groups", "blk"), "head", None))
    return jax.shard_map(body, mesh=mesh, in_specs=in_specs, out_specs=out_specs, check_vma=False)
```

```python
import math

import jax
import jax.numpy as jnp
from jax import lax
from jax.experimental import pallas as pl
from jax.experimental.pallas import tpu as pltpu
from jax.sharding import PartitionSpec as P

HEAD_DIM = 64
LANES = 128
GRID_COLS = 96
EPS = 1e-06
BF16 = jnp.bfloat16
F32 = jnp.float32
MIB = 1024 * 1024


def specs(count):
    return [pl.BlockSpec(memory_space=pltpu.VMEM)] * count


def nbytes(*arrays):
    return sum(math.prod(a.shape) * jnp.dtype(a.dtype).itemsize for a in arrays)


def call(kernel, outs, args, scratch=(), flops=0, exps=0):
    outs = tuple(jax.ShapeDtypeStruct(shape, dtype) for shape, dtype in outs)
    return pl.pallas_call(
        kernel,
        out_shape=outs,
        in_specs=specs(len(args)),
        out_specs=tuple(specs(len(outs))),
        scratch_shapes=list(scratch),
        compiler_params=pltpu.CompilerParams(vmem_limit_bytes=24 * MIB),
        cost_estimate=pl.CostEstimate(
            flops=flops, transcendentals=exps, bytes_accessed=nbytes(*args, *outs)
        ),
    )(*args)


def layer_norm(values_in, gain_row):
    mean_row = jnp.mean(values_in, axis=-1, keepdims=True)
    centred = values_in - mean_row
    spread = jnp.mean(centred * centred, axis=-1, keepdims=True)
    return centred * lax.rsqrt(spread + EPS) * gain_row


def dot(a, b):
    return jnp.dot(a, b, preferred_element_type=F32)


def low_lanes(shape):
    return lax.broadcasted_iota(jnp.int32, shape, len(shape) - 1) % LANES < HEAD_DIM


def normalize(mine_ref, other_ref, gain_ref):
    half = mine_ref.shape[1]
    width = 2 * half
    mine, other = mine_ref[...], other_ref[...]
    mean = (
        jnp.sum(mine, axis=-1, keepdims=True) + jnp.sum(other, axis=-1, keepdims=True)
    ) / width
    mine, other = mine - mean, other - mean
    spread = (
        jnp.sum(mine * mine, axis=-1, keepdims=True)
        + jnp.sum(other * other, axis=-1, keepdims=True)
    ) / width
    scale = lax.rsqrt(spread + EPS)
    low_gain, high_gain = gain_ref[:half][None, :], gain_ref[half:][None, :]
    first = lax.axis_index("head") == 0
    mine = (mine * scale * jnp.where(first, low_gain, high_gain)).astype(BF16)
    other = (other * scale * jnp.where(first, high_gain, low_gain)).astype(BF16)
    return mine, other


def intake_kernel(tokens_ref, tokens_out):
    tokens_out[...] = tokens_ref[...]


def norm_kernel(mine_ref, other_ref, gain_ref, mine_out, other_out):
    mine_out[...], other_out[...] = normalize(mine_ref, other_ref, gain_ref)


def project(mine, other, weight_ref, part):
    core = lax.axis_index("head")
    half = mine.shape[1]
    mine_at = pl.ds(pl.multiple_of(core * half, half), half)
    other_at = pl.ds(pl.multiple_of((1 - core) * half, half), half)
    return (
        dot(mine, weight_ref[part, mine_at, :]) + dot(other, weight_ref[part, other_at, :])
    ).astype(BF16)


def plain_qkv_kernel(mine_ref, other_ref, gain_ref, weight_ref, *out_refs):
    mine, other = normalize(mine_ref, other_ref, gain_ref)
    for part, ref in enumerate(out_refs):
        ref[...] = project(mine, other, weight_ref, part)


def spread_lanes(column, width=LANES):
    return jnp.broadcast_to(column, (column.shape[0], width))


def across(lanes, width):
    whole, rest = divmod(width, LANES)
    return jnp.concatenate([lanes] * whole + ([lanes[:, :rest]] if rest else []), axis=1)


def absorb(pair, queries, keys, values, old):
    factor = HEAD_DIM ** (-0.5) * math.log2(math.e)
    cols = slice(pair * LANES, (pair + 1) * LANES)
    scores = lax.dot_general(
        queries, keys[:, cols], (((1,), (1,)), ((), ())), preferred_element_type=F32
    )
    top = spread_lanes(jnp.max(scores, axis=-1, keepdims=True))
    if old is not None:
        old_top, old_total, old_mixed = old
        top = jnp.maximum(top, old_top)
    weights = jnp.exp2((scores - across(top, scores.shape[1])) * factor)
    total = spread_lanes(jnp.sum(weights, axis=-1, keepdims=True))
    mixed = dot(weights.astype(BF16), values[:, cols])
    rows = mixed.shape[0] // 2
    low = low_lanes((rows, LANES))
    mixed = jnp.where(low, mixed[:rows], mixed[rows:])
    if old is not None:
        shrink = jnp.exp2((old_top - top) * factor)
        total = total + old_total * shrink
        mixed = mixed + old_mixed * jnp.where(low, shrink[:rows], shrink[rows:])
    return top, total, mixed


def own_kernel(
    mine_ref, other_ref, weight_ref, query_ref, top_ref, total_ref, mixed_ref
):
    mine, other = mine_ref[...], other_ref[...]
    rows = mine.shape[0]
    queries = project(mine, other, weight_ref, 0)
    keys = project(mine, other, weight_ref, 1)
    values = project(mine, other, weight_ref, 2)
    low = low_lanes((rows, LANES))
    for pair in range(query_ref.shape[0]):
        tile = queries[:, pair * LANES : (pair + 1) * LANES]
        query_ref[pair, :rows] = jnp.where(low, tile, jnp.zeros_like(tile))
        query_ref[pair, rows:] = jnp.where(low, jnp.zeros_like(tile), tile)
        top_ref[pair], total_ref[pair], mixed_ref[pair] = absorb(
            pair, query_ref[pair], keys, values, None
        )


def absorb_keys(keys, values, query_ref, top_ref, total_ref, mixed_ref):
    for pair in range(query_ref.shape[0]):
        old = top_ref[pair], total_ref[pair], mixed_ref[pair]
        yield pair, absorb(pair, query_ref[pair], keys, values, old)


def mark_kernel(block_ref, mark_ref):
    mark_ref[...] = block_ref[: mark_ref.shape[0], : mark_ref.shape[1]]


def step_kernel(
    mine_ref,
    other_ref,
    weight_ref,
    query_ref,
    top_ref,
    total_ref,
    mixed_ref,
    mark_ref,
    top_out,
    total_out,
    mixed_out,
):
    mine, other = mine_ref[...], other_ref[...]
    keys = project(mine, other, weight_ref, 1)
    values = project(mine, other, weight_ref, 2)
    for pair, state in absorb_keys(keys, values, query_ref, top_ref, total_ref, mixed_ref):
        top_out[pair], total_out[pair], mixed_out[pair] = state


def half_kernel(mine_a, mine_b, weight_ref, mark_ref, keys_ref, values_ref):
    mine = jnp.concatenate([mine_a[...], mine_b[...]], axis=0)
    half = mine.shape[1]
    here = pl.ds(pl.multiple_of(lax.axis_index("head") * half, half), half)
    keys_ref[...] = dot(mine, weight_ref[1, here, :])
    values_ref[...] = dot(mine, weight_ref[2, here, :])


def send_terms(att_ref, weight_ref, send_ref):
    grid_rows, window = send_ref.shape[:2]
    shift = (1 - lax.axis_index("head")) * (GRID_COLS - window)
    cells = jnp.concatenate(
        [
            att_ref[pl.ds(pl.multiple_of(row * GRID_COLS + shift, 32), window), :]
            for row in range(grid_rows)
        ],
        axis=0,
    )
    send_ref[...] = dot(cells, weight_ref[...]).astype(BF16).reshape(send_ref.shape)


def keep_kernel(att_ref, weight_ref, mine_ref, other_ref, keep_ref, full_ref):
    core = lax.axis_index("head")
    grid_rows, window = keep_ref.shape[:2]
    half = mine_ref.shape[1]
    shift = core * (GRID_COLS - window)
    places = [
        pl.ds(pl.multiple_of(row * GRID_COLS + shift, 32), window) for row in range(grid_rows)
    ]
    cells = jnp.concatenate([att_ref[here, :] for here in places], axis=0)
    full_ref[...] = dot(cells, weight_ref[...])
    for row, here in enumerate(places):
        there = slice(row * window, (row + 1) * window)
        for part, ref in ((core, mine_ref), (1 - core, other_ref)):
            cols = pl.ds(pl.multiple_of(part * half, half), half)
            keep_ref[row, :, cols] = full_ref[there, cols] + ref[here, :]


def last_kernel(
    other_a,
    other_b,
    keys_ref,
    values_ref,
    weight_ref,
    query_ref,
    top_ref,
    total_ref,
    mixed_ref,
    out_weight_ref,
    send_ref,
    att_ref,
):
    rows = mixed_ref.shape[1]
    low = low_lanes((rows, LANES))
    other = jnp.concatenate([other_a[...], other_b[...]], axis=0)
    half = other.shape[1]
    there = pl.ds(pl.multiple_of((1 - lax.axis_index("head")) * half, half), half)
    keys = (keys_ref[...] + dot(other, weight_ref[1, there, :])).astype(BF16)
    values = (values_ref[...] + dot(other, weight_ref[2, there, :])).astype(BF16)
    for pair, (_, total, mixed) in absorb_keys(
        keys, values, query_ref, top_ref, total_ref, mixed_ref
    ):
        cols = slice(pair * LANES, (pair + 1) * LANES)
        att_ref[:, cols] = (mixed / jnp.where(low, total[:rows], total[rows:])).astype(BF16)
    send_terms(att_ref, out_weight_ref, send_ref)


def plain_out_kernel(att_ref, weight_ref, send_ref):
    send_terms(att_ref, weight_ref, send_ref)


def lateral_kernel(
    keep_ref, got_ref, lateral_ref, gain_ref, first_ref, second_ref, pool_ref, fine_ref
):
    core = lax.axis_index("head")
    window, features = keep_ref.shape[1], keep_ref.shape[2]
    cells = (keep_ref[...] + got_ref[...].astype(F32)).astype(BF16)
    fine_ref[...] = layer_norm(
        dot(cells.reshape(2 * window, features), lateral_ref[0]), gain_ref[0, 0][None, :]
    ).astype(BF16)
    first_ref[:window] = fine_ref[pl.ds(pl.multiple_of((1 - core) * window, window), window), :]
    second_ref[:window] = fine_ref[pl.ds(pl.multiple_of(core * window, window), window), :]
    tall = jnp.maximum(cells[0].astype(F32), cells[1].astype(F32))
    pooled = []
    for part in range(features // LANES):
        pool_ref[part] = tall[:, part * LANES : (part + 1) * LANES]
        even = pool_ref[part, pl.ds(0, window // 2, stride=2), :]
        odd = pool_ref[part, pl.ds(1, window // 2, stride=2), :]
        pooled.append(jnp.maximum(even, odd).astype(BF16))
    pooled = jnp.concatenate(pooled, axis=1)
    coarse = layer_norm(dot(pooled, lateral_ref[1]), gain_ref[1, 0][None, :]).astype(BF16)
    first_ref[window:] = coarse
    second_ref[window:] = coarse


def joined(terms, window):
    left, middle, right = (terms(tap_col) for tap_col in range(3))
    block = middle.shape[0]
    place = lax.broadcasted_iota(jnp.int32, middle.shape, 0) % window
    left = jnp.where(place == 0, 0.0, pltpu.roll(left, 1, axis=0))
    right = jnp.where(place == window - 1, 0.0, pltpu.roll(right, block - 1, axis=0))
    return left + middle + right


def own_conv_kernel(first_ref, second_ref, weight_ref, fine_ref, coarse_ref, fine_in):
    core = lax.axis_index("head")
    window = fine_ref.shape[0] // 2
    for ref, place in ((first_ref, 1 - core), (second_ref, core)):
        fine_in[pl.ds(pl.multiple_of(place * window, window), window), :] = ref[:window]
    coarse = first_ref[window:]

    def fine_terms(tap_col):
        to_lower = dot(fine_in[:window], weight_ref[0, 0, tap_col])
        to_upper = dot(fine_in[window:], weight_ref[0, 2, tap_col])
        return dot(fine_in[...], weight_ref[0, 1, tap_col]) + jnp.concatenate(
            [to_upper, to_lower], axis=0
        )

    fine_ref[...] = joined(fine_terms, window)
    coarse_ref[...] = joined(lambda tap_col: dot(coarse, weight_ref[1, 1, tap_col]), window // 2)


def add_edge(got_ref, side, weight_ref, fine_ref, coarse_ref):
    window = fine_ref.shape[0] // 2
    inside = lax.axis_index("blk") != side * (lax.axis_size("blk") - 1)
    edge = jnp.where(inside, got_ref[...].astype(F32), 0.0).astype(BF16)
    here = pl.ds(pl.multiple_of(side * window, window), window)
    fine_ref[here, :] += joined(
        lambda tap_col: dot(edge[:window], weight_ref[0, 2 * side, tap_col]), window
    )
    coarse_ref[...] += joined(
        lambda tap_col: dot(edge[window:], weight_ref[1, 2 * side, tap_col]), window // 2
    )


def first_edge_kernel(
    got_ref, own_fine_ref, own_coarse_ref, weight_ref, fine_ref, coarse_ref
):
    fine_ref[...] = own_fine_ref[...]
    coarse_ref[...] = own_coarse_ref[...]
    add_edge(got_ref, lax.axis_index("head"), weight_ref, fine_ref, coarse_ref)


def conv_kernel(
    got_ref,
    own_fine_ref,
    own_coarse_ref,
    weight_ref,
    gain_ref,
    fine_ref,
    coarse_ref,
    fine_sum,
    coarse_sum,
):
    core = lax.axis_index("head")
    window = fine_sum.shape[0] // 2
    fine_sum[...] = own_fine_ref[...]
    coarse_sum[...] = own_coarse_ref[...]
    add_edge(got_ref, 1 - core, weight_ref, fine_sum, coarse_sum)
    cols = fine_ref.shape[1]
    inset = cols - (GRID_COLS - window)
    for row in range(2):
        here = pl.ds(pl.multiple_of(row * window + core * inset, 8), cols)
        fine_ref[row] = layer_norm(fine_sum[here, :], gain_ref[0, 1][None, :]).astype(BF16)
    here = pl.ds(pl.multiple_of(core * (inset // 2), 8), cols // 2)
    coarse_ref[0] = layer_norm(coarse_sum[here, :], gain_ref[1, 1][None, :]).astype(BF16)


def attend_shared(queries, keys, values):
    factor = HEAD_DIM ** (-0.5)
    step = math.gcd(keys.shape[0], 1536)
    rows = queries.shape[0]

    def block(state, pair):
        running, totals, weighted = state
        key, value = pair
        scores = (
            lax.dot_general(queries, key, (((1,), (1,)), ((), ())), preferred_element_type=F32)
            * factor
        )
        newmax = jnp.maximum(running, jnp.max(scores, axis=-1, keepdims=True))
        weights = jnp.exp(scores - newmax)
        shrink = jnp.exp(running - newmax)
        totals = totals * shrink + jnp.sum(weights, axis=-1, keepdims=True)
        weighted = weighted * shrink + dot(weights.astype(BF16), value)
        return (newmax, totals, weighted), None

    state = (
        jnp.full((rows, 1), -jnp.inf, F32),
        jnp.zeros((rows, 1), F32),
        jnp.zeros((rows, HEAD_DIM), F32),
    )
    state, _ = lax.scan(
        block, state, (keys.reshape(-1, step, HEAD_DIM), values.reshape(-1, step, HEAD_DIM))
    )
    return (state[2] / state[1]).astype(BF16)


def exchange(value):
    return lax.all_to_all(value, "blk", split_axis=0, concat_axis=0, tiled=True)


def attention_shared(mine, other, norm_gain, qkv_weight, slices):
    rows = mine.shape[0]
    width = qkv_weight.shape[2]
    heads = width // HEAD_DIM
    blocks = heads * slices
    share = rows // slices
    queries, keys, values = call(
        plain_qkv_kernel, [((rows, width), BF16)] * 3, (mine, other, norm_gain, qkv_weight)
    )
    query_send = jnp.transpose(
        queries.reshape(slices, share, heads, HEAD_DIM), (2, 0, 1, 3)
    ).reshape(blocks, share * HEAD_DIM)
    pair = jnp.concatenate(
        (keys.reshape(rows, heads, HEAD_DIM), values.reshape(rows, heads, HEAD_DIM)), axis=2
    )
    pair = jnp.transpose(pair, (1, 0, 2))
    pair_send = jnp.broadcast_to(pair[:, None], (heads, slices, rows, 2 * HEAD_DIM)).reshape(
        blocks, rows, 2 * HEAD_DIM
    )
    query_got = exchange(query_send).reshape(blocks * share, HEAD_DIM)
    pair_got = exchange(pair_send).reshape(blocks * rows, 2 * HEAD_DIM)
    one_head = attend_shared(query_got, pair_got[:, :HEAD_DIM], pair_got[:, HEAD_DIM:])
    back = exchange(one_head.reshape(blocks, share * HEAD_DIM))
    return jnp.transpose(back.reshape(heads, slices, share, HEAD_DIM), (1, 2, 0, 3)).reshape(
        rows, width
    )


def body(tokens, norm_gain, qkv_weight, out_weight, lateral_weight, conv_weight, level_gains):
    rows, half = tokens.shape
    features = out_weight.shape[1]
    width = qkv_weight.shape[2]
    heads = width // HEAD_DIM
    blocks = lax.axis_size("blk")
    cores = lax.axis_size("head")
    grid_rows = rows // GRID_COLS
    cols = GRID_COLS // cores
    channels = lateral_weight.shape[2]
    window = 2 * GRID_COLS // 3
    swap = [(i, cores - 1 - i) for i in range(cores)]

    other = lax.ppermute(tokens, "head", swap)
    (tokens,) = call(intake_kernel, [(tokens.shape, F32)], (tokens,), flops=MIB * 1024)
    other, tokens = lax.optimization_barrier((other, tokens))
    term_out = ((grid_rows, window, features), BF16)
    out_flops = 2 * grid_rows * window * width * features
    if 4 <= blocks <= heads:
        order = list(range(0, blocks, 2)) + list(range(blocks - 1, 0, -2))
        forth = [(order[i - 1], order[i]) for i in range(blocks)]
        back = [(target, source) for source, target in forth]
        mine, across_core = call(
            norm_kernel, [((rows, half), BF16)] * 2, (tokens, other, norm_gain)
        )
        pairs = width // LANES
        state_outs = [
            ((pairs, 2 * rows, LANES), F32),
            ((pairs, 2 * rows, LANES), F32),
            ((pairs, rows, LANES), F32),
        ]
        ahead = lax.ppermute(mine, "blk", forth)
        behind = lax.ppermute(mine, "blk", back)
        unit = 4 * rows * width * (features + rows)
        queries, *state = call(
            own_kernel,
            [((pairs, 2 * rows, LANES), BF16)] + state_outs,
            (mine, across_core, qkv_weight),
            flops=unit + 2 * rows * width * features,
            exps=heads * rows * rows,
        )
        last = blocks // 2
        cut = 5 * rows // 6
        for step in range(1, last + 1):
            ahead, state[0] = lax.optimization_barrier((ahead, state[0]))
            behind, state[0] = lax.optimization_barrier((behind, state[0]))
            arrived = ahead, behind
            (mark,) = call(mark_kernel, [((16, LANES), BF16)], (ahead,))
            if step == last - 1:
                ahead, behind = ahead[:cut], behind[cut:]
            if step < last:
                ahead = lax.ppermute(ahead, "blk", forth)
                behind = lax.ppermute(behind, "blk", back)
            traded = (
                lax.ppermute(arrived[0], "head", swap), lax.ppermute(arrived[1], "head", swap)
            )
            if step == last:
                break
            for block in zip(arrived, traded):
                state = call(
                    step_kernel,
                    state_outs,
                    block + (qkv_weight, queries) + tuple(state) + (mark,),
                    flops=unit,
                    exps=heads * rows * rows,
                )
            state = list(state)
        keys, values = call(
            half_kernel,
            [((rows, width), F32)] * 2,
            arrived + (qkv_weight, mark),
            flops=2 * rows * width * features,
        )
        peer_term, attended = call(
            last_kernel,
            [term_out, ((rows, width), BF16)],
            traded + (keys, values, qkv_weight, queries)
            + tuple(state)
            + (out_weight,),
            flops=unit + out_flops,
            exps=heads * rows * rows,
        )
    else:
        attended = attention_shared(tokens, other, norm_gain, qkv_weight, blocks // heads)
        (peer_term,) = call(plain_out_kernel, [term_out], (attended, out_weight), flops=out_flops)
    peer_term = lax.ppermute(peer_term, "head", swap)
    (keep,) = call(
        keep_kernel,
        [((grid_rows, window, features), F32)],
        (attended, out_weight, tokens, other),
        [pltpu.VMEM((grid_rows * window, features), F32)],
        flops=out_flops,
    )

    message = (window + window // 2, channels)
    first, second = call(
        lateral_kernel,
        [(message, BF16), (message, BF16)],
        (keep, peer_term, lateral_weight, level_gains),
        [
            pltpu.VMEM((features // LANES, window, LANES), F32),
            pltpu.VMEM((2 * window, channels), BF16),
        ],
        flops=5 * window * features * channels,
    )
    down_then_up = [
        loop
        for low in range(2)
        for loop in [
            [(cores * i + low, cores * (i + 1) + low) for i in range(blocks - 1)]
            + [(cores * (i + 1) + 1 - low, cores * i + 1 - low) for i in range(blocks - 1)]
            + [(cores * (blocks - 1) + low, cores * blocks - 1 - low), (1 - low, low)]
        ]
    ]
    got_second = lax.ppermute(second, ("blk", "head"), down_then_up[1])
    got_first = lax.ppermute(first, ("blk", "head"), down_then_up[0])
    sums = [((2 * window, channels), F32), ((window // 2, channels), F32)]
    own_sums = call(
        own_conv_kernel,
        sums,
        (first, second, conv_weight),
        [pltpu.VMEM((2 * window, channels), BF16)],
        flops=27 * window * channels * channels,
    )
    own_sums = call(
        first_edge_kernel,
        sums,
        (got_first, *own_sums, conv_weight),
        flops=9 * window * channels * channels,
    )
    return call(
        conv_kernel,
        [((grid_rows, cols, channels), BF16), ((grid_rows // 2, cols // 2, channels), BF16)],
        (got_second, *own_sums, conv_weight, level_gains),
        [pltpu.VMEM(shape, dtype) for shape, dtype in sums],
        flops=9 * window * channels * channels,
    )


def solution(mesh):
    in_specs = (
        P(("groups", "blk"), "head"),
        P(),
        P(None, None, "head"),
        P("head", None),
        P(),
        P(),
        P(),
    )
    out_specs = (P(("groups", "blk"), "head", None), P(("groups", "blk"), "head", None))
    return jax.shard_map(body, mesh=mesh, in_specs=in_specs, out_specs=out_specs, check_vma=False)
```
